128 devices in a mesh: dp: 2 (over core), row: 16 (over y, x), col: 4 (over z).
Axes of the slice: x: 4, y: 4, z: 4, core: 2. Of those that a mesh axis runs over, the one named last changes fastest.
Arguments:
- inputs: bfloat16 [768, 32768], P('col', ('dp', 'row')), may hold values from -6 to 6
- teacher: bfloat16 [768, 32768], P('col', ('dp', 'row')), may hold values from -6 to 6
- lengths: int32 [32], P(('dp', 'row')), may hold values from 256 to 1024
- query_weight: bfloat16 [768, 768], P('row', 'col'), may hold values from -0.21875 to 0.21875
- query_bias: float32 [768], P('col'), may hold values from -3 to 3
- key_weight: bfloat16 [768, 768], P('row', 'col'), may hold values from -0.21875 to 0.21875
- value_weight: bfloat16 [768, 768], P('row', 'col'), may hold values from -0.21875 to 0.21875
- value_bias: float32 [768], P('col'), may hold values from -3 to 3
- output_weight: bfloat16 [768, 768], P('col', 'row'), may hold values from -6 to 6
- output_bias: float32 [768], P('col'), may hold values from -3 to 3
- first_gain: float32 [768], P('col'), may hold values from 0.5 to 1.5
- first_shift: float32 [768], P('col'), may hold values from -3 to 3
- up_weight: bfloat16 [768, 3072], P('row', 'col'), may hold values from -0.21875 to 0.21875
- up_bias: float32 [3072], P('col'), may hold values from -3 to 3
- down_weight: bfloat16 [768, 3072], P('row', 'col'), may hold values from -0.109375 to 0.109375
- down_bias: float32 [768], P('col'), may hold values from -3 to 3
- second_gain: float32 [768], P('col'), may hold values from 0.5 to 1.5
- second_shift: float32 [768], P('col'), may hold values from -3 to 3
Outputs:
- output: bfloat16 [768, 32768], P('col', ('dp', 'row'))
- distill_loss: float32 [], replicated
- grad_inputs: float32 [768, 32768], P('col', ('dp', 'row'))
- grad_query_weight: float32 [768, 768], P('row', 'col')
- grad_query_bias: float32 [768], P('col')
- grad_key_weight: float32 [768, 768], P('row', 'col')
- grad_value_weight: float32 [768, 768], P('row', 'col')
- grad_value_bias: float32 [768], P('col')
- grad_output_weight: float32 [768, 768], P('col', 'row')
- grad_output_bias: float32 [768], P('col')
- grad_first_gain: float32 [768], P('col')
- grad_first_shift: float32 [768], P('col')
- grad_up_weight: float32 [768, 3072], P('row', 'col')
- grad_up_bias: float32 [3072], P('col')
- grad_down_weight: float32 [768, 3072], P('row', 'col')
- grad_down_bias: float32 [768], P('col')
- grad_second_gain: float32 [768], P('col')
- grad_second_shift: float32 [768], P('col')
The draws below stay inside these ranges and needn't reach their ends.
All inputs are finite; a program needn't handle non-finite values.
Results may differ from the reference program's by a relative error of at most 0.018.
Values may be sent and summed in bfloat16 or wider, within the bound.
A program may use at most 64 MiB of HBM per device.

```python
from functools import partial
import jax
import jax.numpy as jnp
from jax import lax

HEADS = 12
HEAD_DIM = 64
D = 768
FF = 3072
LEN = 1024
SEQS = 32
TOKENS = 32768


def plant(values, key, smallest, high):
    longest = values.shape.index(max(values.shape))
    spots = []
    for shift in (0, 1):
        where = [jax.random.randint(jax.random.fold_in(key, axis), (), 0, length) for axis, length in enumerate(values.shape)]
        where[longest] = (where[longest] + shift) % values.shape[longest]
        spots.append(tuple(where))
    return values.at[spots[0]].set(smallest).at[spots[1]].set(high)


def shard_levels(stream_key, extent, split, low, largest):
    level, own = 1.0, jax.random.fold_in(stream_key, 6)
    for dim, parts in split:
        heights = jnp.exp(jax.random.uniform(jax.random.fold_in(own, dim), (parts,), jnp.float32, low / len(split), largest / len(split)))
        level = level * jnp.repeat(heights, extent[dim] // parts).reshape([-1 if axis == dim else 1 for axis in range(len(extent))])
    return level


def normal_values(rng, extent, spread, bound, cuts=(), kind=jnp.bfloat16):
    drawn = jax.random.normal(rng, extent, jnp.float32) * spread
    if len(cuts) > 0:
        drawn = shard_levels(rng, extent, cuts, -0.22, 0.18) * drawn
    return jnp.clip(drawn, min=-bound, max=bound).astype(kind)


def setup_inputs(seed: int = 0) -> dict:
    seeds = jax.random.split(jax.random.key(seed), 19)
    inputs = normal_values(seeds[0], (D, TOKENS), 1.0, 6.0, ((0, 4), (1, 32)))
    teacher = normal_values(seeds[1], (D, TOKENS), 1.0, 6.0, ((0, 4), (1, 32)))
    lengths = plant(jax.random.randint(seeds[2], (SEQS,), LEN // 4, LEN + 1), jax.random.fold_in(seeds[2], 1), LEN // 4, LEN).astype(jnp.int32)
    query_weight = normal_values(seeds[3], (D, D), D ** -0.5, 0.21875, ((0, 16), (1, 4)))
    query_bias = normal_values(seeds[4], (D,), 0.5, 3.0, ((0, 4),), jnp.float32)
    key_weight = normal_values(seeds[5], (D, D), D ** -0.5, 0.21875, ((0, 16), (1, 4)))
    value_weight = normal_values(seeds[6], (D, D), D ** -0.5, 0.21875, ((0, 16), (1, 4)))
    value_bias = normal_values(seeds[7], (D,), 0.5, 3.0, ((0, 4),), jnp.float32)
    output_weight = normal_values(seeds[8], (D, D), (max(1, (D * 8) // (LEN * 5))) ** -0.5, 6.0, ((0, 4), (1, 16)))
    output_bias = normal_values(seeds[9], (D,), 0.5, 3.0, ((0, 4),), jnp.float32)
    first_gain = jnp.clip(1.0 + 0.1 * jax.random.normal(seeds[10], (D,), jnp.float32), 0.5, 1.5)
    first_shift = normal_values(seeds[11], (D,), 0.5, 3.0, ((0, 4),), jnp.float32)
    up_weight = normal_values(seeds[12], (D, FF), D ** -0.5, 0.21875, ((0, 16), (1, 4)))
    up_bias = normal_values(seeds[13], (FF,), 0.5, 3.0, ((0, 4),), jnp.float32)
    down_weight = normal_values(seeds[14], (D, FF), FF ** -0.5, 0.109375, ((0, 16), (1, 4)))
    down_bias = normal_values(seeds[15], (D,), 0.5, 3.0, ((0, 4),), jnp.float32)
    second_gain = jnp.clip(1.0 + 0.1 * jax.random.normal(seeds[16], (D,), jnp.float32), 0.5, 1.5)
    second_shift = normal_values(seeds[17], (D,), 0.5, 3.0, ((0, 4),), jnp.float32)
    return {"inputs": inputs, "teacher": teacher, "lengths": lengths, "query_weight": query_weight, "query_bias": query_bias, "key_weight": key_weight, "value_weight": value_weight, "value_bias": value_bias, "output_weight": output_weight, "output_bias": output_bias, "first_gain": first_gain, "first_shift": first_shift, "up_weight": up_weight, "up_bias": up_bias, "down_weight": down_weight, "down_bias": down_bias, "second_gain": second_gain, "second_shift": second_shift}


@jax.custom_vjp
def low(v):
    return lax.optimization_barrier(v.astype(jnp.bfloat16)).astype(jnp.float32)

@jax.custom_vjp
def low_back(v):
    return v

def low_keep(v):
    return (low(v), None)

def low_pass(kept, grad):
    return (grad,)

def back_keep(v):
    return (v, None)

def back_low(kept, grad):
    return (low(grad),)
low.defvjp(low_keep, low_pass)
low_back.defvjp(back_keep, back_low)
norm_eps = 1e-12
mask_value = -1e+30
root_half = 0.7071067811865476
per_group = 4

def matmul(left, right):
    return jnp.dot(left, right, precision=lax.Precision.HIGHEST, preferred_element_type=jnp.float32)

def normalize(resid, gain, shift):
    average = lax.optimization_barrier(jnp.mean(resid, axis=-1, keepdims=True))
    squares = lax.optimization_barrier(jnp.mean(resid * resid, axis=-1, keepdims=True))
    inv_scale = lax.rsqrt(squares - average * average + norm_eps)
    return (resid - average) * inv_scale * gain + shift

def attend(items):
    queries, keys_all, values_all, length = items
    head_q = queries.reshape(LEN, HEADS, HEAD_DIM)
    head_k = keys_all.reshape(LEN, HEADS, HEAD_DIM)
    head_v = values_all.reshape(LEN, HEADS, HEAD_DIM)
    score = jnp.einsum('qhd,khd->hqk', head_q, head_k, precision=lax.Precision.HIGHEST)
    score = low_back(score * HEAD_DIM ** (-0.5))
    keys_ok = jnp.arange(LEN) < length
    score = jnp.where(keys_ok[None, None, :], score, mask_value)
    highest = lax.optimization_barrier(jnp.max(score, axis=-1, keepdims=True))
    expo = jnp.exp(score - highest)
    probs = low(expo / lax.optimization_barrier(jnp.sum(expo, axis=-1, keepdims=True)))
    context = jnp.einsum('hqk,khd->qhd', probs, head_v, precision=lax.Precision.HIGHEST)
    return context.reshape(LEN, HEADS * HEAD_DIM)

def layer_group(params, items):
    block, target, group_lengths = items
    query_weight, query_bias, key_weight, value_weight, value_bias, output_weight, output_bias, first_gain, first_shift, up_weight, up_bias, down_weight, down_bias, second_gain, second_shift = params
    queries = low_back(low(matmul(block, query_weight) + query_bias))
    keys_all = low_back(low(matmul(block, key_weight)))
    values_all = low_back(low(matmul(block, value_weight) + value_bias))
    shaped = (per_group, LEN, D)
    context = lax.map(jax.checkpoint(attend), (queries.reshape(shaped), keys_all.reshape(shaped), values_all.reshape(shaped), group_lengths))
    context = low_back(low(context.reshape(per_group * LEN, D)))
    branch = low_back(matmul(context, output_weight) + output_bias)
    hidden = normalize(block + branch, first_gain, first_shift)
    pre_act = low_back(matmul(low(hidden), up_weight) + up_bias)
    activation = low(0.5 * pre_act * (1.0 + lax.erf(pre_act * root_half)))
    down = low_back(matmul(activation, down_weight.T) + down_bias)
    final = normalize(hidden + down, second_gain, second_shift)
    position = jnp.arange(per_group * LEN) % LEN
    valid = position < jnp.repeat(group_lengths, LEN)
    diff = final - target
    return (final, jnp.sum(jnp.where(valid[:, None], diff * diff, 0.0)))

def reference(inputs, teacher, lengths, query_weight, query_bias, key_weight, value_weight, value_bias, output_weight, output_bias, first_gain, first_shift, up_weight, up_bias, down_weight, down_bias, second_gain, second_shift):
    params = tuple((item.astype(jnp.float32) for item in (query_weight, query_bias, key_weight, value_weight, value_bias, output_weight, output_bias, first_gain, first_shift, up_weight, up_bias, down_weight, down_bias, second_gain, second_shift)))
    states = inputs.astype(jnp.float32).T
    target = teacher.astype(jnp.float32).T
    count = jnp.sum(lengths).astype(jnp.float32)
    groups = lengths.shape[0] // per_group

    def whole(flat, weights):
        items = (flat.reshape(groups, per_group * LEN, D), target.reshape(groups, per_group * LEN, D), lengths.reshape(groups, per_group))
        final, squares = lax.map(jax.checkpoint(partial(layer_group, weights)), items)
        loss_value = jnp.sum(squares) / (2.0 * D * count)
        return (loss_value, final.reshape(flat.shape))
    loss_value, pullback, final = jax.vjp(whole, states, params, has_aux=True)
    grad_states, grads = pullback(jnp.asarray(TOKENS * D, dtype=jnp.float32))
    return (final.T.astype(jnp.bfloat16), loss_value, grad_states.T, grads[0], grads[1], grads[2], grads[3], grads[4], grads[5], grads[6], grads[7], grads[8], grads[9], grads[10], grads[11], grads[12], grads[13], grads[14])
```

```python
import jax
import jax.numpy as jnp
from jax import lax
from jax.experimental import pallas as pl
from jax.experimental.pallas import tpu as pltpu
from jax.sharding import Mesh
from jax.sharding import PartitionSpec as P

D = 768
FF = 3072
LEN = 1024
HD = 64
HEADS = 3
C = 192
TOK = 256
RB = 48
SLOTS = 32768
EPS = 1e-12
MASK = -1e30
ROOT_HALF = 0.7071067811865476
INV_ROOT_TAU = 0.3989422804014327
AXES = ("dp", "row_0", "row_1", "col")
ROW = ("row_0", "row_1")
DP_ROW = ("dp", "row_0", "row_1")
N_SEM = 192
f32 = jnp.float32
bf16 = jnp.bfloat16


def mm(a, b):
    return lax.dot_general(a, b, (((1,), (0,)), ((), ())), preferred_element_type=f32)


def mt(a, b):
    return lax.dot_general(a, b, (((1,), (1,)), ((), ())), preferred_element_type=f32)


def transposed(a):
    return jnp.transpose(a, (1, 0))


class Sent:
    def __init__(self, copy):
        self.copy, self.open_send, self.open_recv = copy, True, True

    def wait_send(self):
        if self.open_send:
            self.copy.wait_send()
        self.open_send = False

    def wait_recv(self):
        if self.open_recv:
            self.copy.wait_recv()
        self.open_recv = False

    def wait(self):
        self.wait_send()
        self.wait_recv()


class Links:
    def __init__(self, ssem, rsem):
        self.ssem, self.rsem, self.n, self.all = ssem, rsem, 0, []

    def send(self, src, dst, dev):
        copy = pltpu.make_async_remote_copy(
            src_ref=src,
            dst_ref=dst,
            send_sem=self.ssem.at[self.n],
            recv_sem=self.rsem.at[self.n],
            device_id=dev,
            device_id_type=pl.DeviceIdType.MESH,
        )
        copy.start()
        self.n += 1
        self.all.append(Sent(copy))
        return self.all[-1]


def layer(
    x_in, t_in, len_in, wqkv_in, wo_in, up_in, down_in, vec_in, ub_in,
    out_o, gi_o, dw2_o, dwo_o, dqkv_o, sv_o, svq_o,
    xf, tf, wqkv, wo, w2, vec, ub, vcol, qkvt, ktm, qaug, vaug, vtm, pst, linv,
    ctxt, ctxa, hid, nrm, sg, bstore, astore, slope, brecv, arecv,
    g2, go, gq, dctx, dct, outt, delta,
    dqkvt, dxp, dxo, rx, r1, s1, r2, s2, r3, ro1, so1, ro2, so2, ro3, rq1, sq1, rq2,
    x1, xo1, xq1, gcol, sv, rsv, wown,
    lsem, ssem, rsem,
):
    d = lax.axis_index("dp")
    y = lax.axis_index("row_0")
    x = lax.axis_index("row_1")
    c = lax.axis_index("col")
    e = 1 - d
    r = 4 * y + x
    a_me = x * e + y * d
    b_me = y * e + x * d

    def ridx(a, b):
        return (4 * b + a) * e + (4 * a + b) * d

    def zdev(k):
        return {"col": lax.rem(c + k, 4)}

    def adev(k):
        return {"row_0": lax.rem(y + k * d, 4), "row_1": lax.rem(x + k * e, 4)}

    def bdev(k):
        return {"row_0": lax.rem(y + k * e, 4), "row_1": lax.rem(x + k * d, 4)}

    sib = {"dp": e}
    links = Links(ssem, rsem)

    def rows48(i):
        return pl.ds(pl.multiple_of(i * RB, 16), RB)

    n_local = [0]

    def local(src, dst):
        copy = pltpu.make_async_copy(src, dst, lsem.at[n_local[0]])
        copy.start()
        n_local[0] += 1
        return copy

    xrows = pl.ds(pl.multiple_of(c * C, 16), C)
    cx = local(x_in, xf.at[xrows])
    cq = local(wqkv_in, wqkv.at[rows48(r)])
    cup = local(up_in, wown.at[0])
    cdn = local(down_in, wown.at[1])
    cwo = local(wo_in, wo.at[r, c])
    cvec = local(vec_in, vec.at[c])
    cub = local(ub_in, ub.at[c])
    tcols = pl.ds(pl.multiple_of(c * TOK, 128), TOK)
    ct = local(t_in.at[:, tcols], tf.at[c])
    bar = pltpu.get_barrier_semaphore()
    for k in (1, 2, 3):
        for dev in (zdev(k), adev(k), bdev(k)):
            pl.semaphore_signal(bar, inc=1, device_id=dev, device_id_type=pl.DeviceIdType.MESH)
    pl.semaphore_signal(bar, inc=1, device_id=sib, device_id_type=pl.DeviceIdType.MESH)
    pl.semaphore_wait(bar, 10)

    def xhalf(i, top):
        return xf.at[pl.ds(pl.multiple_of(i * C + (0 if top else C // 2), 16), C // 2)]

    cx.wait()
    xs = {}
    for k, order in ((1, (True, False)), (3, (False, True))):
        for top in order:
            xs[k, top] = links.send(xhalf(c, top), xhalf(c, top), zdev(k))
    cq.wait()
    qa = [links.send(wqkv.at[rows48(r)], wqkv.at[rows48(r)], adev(k)) for k in (1, 2, 3)]
    cwo.wait()
    oz = [links.send(wo.at[r, c], wo.at[r, c], zdev(k)) for k in (1, 2, 3)]
    cvec.wait()
    vz = [links.send(vec.at[c], vec.at[c], zdev(k)) for k in (1, 2, 3)]
    cub.wait()
    uz = [links.send(ub.at[c], ub.at[c], zdev(k)) for k in (1, 2, 3)]
    cup.wait()
    cdn.wait()
    own_cols = pl.ds(pl.multiple_of(c * D, 128), D)
    wz = []
    for k in (1, 2, 3):
        wz.append(links.send(wown.at[d], w2.at[d, r, :, own_cols], zdev(k)))
    w2[d, r, :, own_cols] = wown[d]
    xs[1, True].wait_recv()
    left = lax.rem(c + 3, 4)
    xs["f", 1] = links.send(xhalf(left, True), xhalf(left, True), zdev(1))
    xs[3, False].wait_recv()
    right = lax.rem(c + 1, 4)
    xs["f", 3] = links.send(xhalf(right, False), xhalf(right, False), zdev(3))
    for copy in oz:
        copy.wait_recv()
    oa = [links.send(wo.at[r], wo.at[r], adev(k)) for k in (1, 2, 3)]
    for copy in qa:
        copy.wait_recv()
    qb = []
    for k in (1, 2, 3):
        for j in range(4):
            ref = wqkv.at[rows48(ridx(j, b_me))]
            qb.append(links.send(ref, ref, bdev(k)))
    for copy in wz:
        copy.wait_recv()
    wa = [links.send(w2.at[d, r], w2.at[d, r], adev(k)) for k in (1, 2, 3)]
    w_sib = [links.send(w2.at[d, r], w2.at[d, r], sib)]
    for copy in oa:
        copy.wait_recv()
    ob = []
    for k in (1, 2, 3):
        for j in range(4):
            ref = wo.at[ridx(j, b_me)]
            ob.append(links.send(ref, ref, bdev(k)))
    for copy in wa:
        copy.wait_recv()
    wb = []
    for k in (1, 2, 3):
        for j in range(4):
            ref = w2.at[d, ridx(j, b_me)]
            wb.append(links.send(ref, ref, bdev(k)))
    for k in (1, 2, 3):
        i = ridx(lax.rem(a_me + 4 - k, 4), b_me)
        w_sib.append(links.send(w2.at[d, i], w2.at[d, i], sib))

    for copy in vz + uz:
        copy.wait_recv()
    for i in range(4):
        vcol[i * C : (i + 1) * C, 0:16] = transposed(vec[i])
    vown = transposed(vec[c])
    length = len_in[0]

    for key in ((1, False), (3, True), ("f", 1), ("f", 3)):
        xs[key].wait_recv()
    for copy in qb:
        copy.wait_recv()
    wq_t = transposed(wqkv[:, 0:C])
    wk_t = transposed(wqkv[:, C : 2 * C])
    wv_t = transposed(wqkv[:, 2 * C :])
    dxp[0, :, 0:D] = wq_t
    dxp[1, :, 0:D] = wk_t
    dxp[2, :, 0:D] = wv_t
    q_bias = vown[:, 10:11]
    v_bias = vown[:, 11:12]
    lane_iota = lax.broadcasted_iota(jnp.int32, (1, TOK), 1)
    first_row = lax.broadcasted_iota(jnp.int32, (HD, TOK), 0) == 0

    def qkv_chunk(i, carry):
        cols = pl.ds(pl.multiple_of(i * TOK, 128), TOK)
        tok = xf[:, cols]
        q = (mm(dxp[0, :, 0:D], tok) + q_bias).astype(bf16)
        k = mm(dxp[1, :, 0:D], tok).astype(bf16)
        v = (mm(dxp[2, :, 0:D], tok) + v_bias).astype(bf16)
        q = (q.astype(f32) * (HD**-0.5)).astype(bf16)
        qkvt[0:C, cols] = q
        qkvt[C : 2 * C, cols] = k
        bias = jnp.where(lane_iota + i * TOK < length, 0.0, MASK)
        bias = jnp.where(first_row, jnp.broadcast_to(bias, (HD, TOK)), 0.0).astype(bf16)
        ones = jnp.where(first_row, 1.0, 0.0).astype(bf16)
        for h in range(HEADS):
            hs = slice(h * HD, (h + 1) * HD)
            qaug[h, 0:HD, cols] = q[hs]
            qaug[h, HD : 2 * HD, cols] = ones
            vaug[h, 0:HD, cols] = v[hs]
            vaug[h, HD : HD + 16, cols] = ones[0:16]
            ktm[h, cols, :] = transposed(jnp.concatenate([k[hs], bias], axis=0))
            vtm[h, cols, :] = transposed(jnp.concatenate([v[hs], ones], axis=0))
        return carry

    lax.fori_loop(0, 4, qkv_chunk, 0)

    def fwd_tile(n, carry):
        h = n // 4
        cols = pl.ds(pl.multiple_of(lax.rem(n, 4) * TOK, 128), TOK)
        score = mm(ktm[h], qaug[h, :, cols])
        top = jnp.max(score, axis=0, keepdims=True)
        probs = jnp.exp(score - top).astype(bf16)
        pst[h, :, cols] = probs
        both = mm(vaug[h], probs)
        inv = 1.0 / both[HD : HD + 1]
        linv[h, 0:1, cols] = inv
        ctxt[pl.ds(pl.multiple_of(h * HD, 16), HD), cols] = (both[0:HD] * inv).astype(bf16)
        return carry

    lax.fori_loop(0, 4 * HEADS, fwd_tile, 0)

    cc = []
    ctxa[c] = ctxt[:, tcols]
    for k in (1, 2, 3):
        there = pl.ds(pl.multiple_of(lax.rem(c + k, 4) * TOK, 128), TOK)
        cc.append(links.send(ctxt.at[:, there], ctxa.at[c], zdev(k)))
    tt = []
    ct.wait()
    for k in (1, 2, 3):
        there = pl.ds(pl.multiple_of(lax.rem(c + k, 4) * TOK, 128), TOK)
        tt.append(links.send(t_in.at[:, there], tf.at[c], zdev(k)))
    for copy in ob:
        copy.wait_recv()
    for k in (1, 2, 3):
        for j in range(4):
            wb[4 * (k - 1) + j].wait_recv()
            i = ridx(j, lax.rem(b_me + 4 - k, 4))
            w_sib.append(links.send(w2.at[d, i], w2.at[d, i], sib))
    for copy in cc:
        copy.wait_recv()

    def proj(i, carry):
        row = pl.ds(pl.multiple_of(i * C, 16), C)
        blocks = wo[pl.ds(i * 4, 4)]
        acc = xf[row, tcols].astype(f32) + vcol[row, 0:1]
        for j in range(4):
            acc = acc + mm(blocks[:, j].reshape(C, C), ctxa[j])
        hid[row] = acc
        return carry

    lax.fori_loop(0, 4, proj, 0)

    def norm_stats(ref):
        v = ref[...]
        mean = jnp.sum(v, axis=0, keepdims=True) * (1.0 / D)
        square = jnp.sum(v * v, axis=0, keepdims=True) * (1.0 / D)
        return mean, lax.rsqrt(square - mean * mean + EPS)

    mean1, inv1 = norm_stats(hid)

    def norm1(i, carry):
        row = pl.ds(pl.multiple_of(i * C, 16), C)
        n = (hid[row] - mean1) * inv1
        nrm[row] = n
        h = n * vcol[row, 1:2] + vcol[row, 2:3]
        hid[row] = h
        astore[0, row] = h.astype(bf16)
        return carry

    lax.fori_loop(0, 4, norm1, 0)
    outt[...] = transposed(astore[0])

    for copy in w_sib:
        copy.wait_recv()

    def up_chunk(i, carry):
        cols = pl.ds(pl.multiple_of(i * D, 128), D)
        pre = mm(outt[...], w2[0, :, :, cols].reshape(D, D)) + ub[i, 0:1]
        half = 0.5 * (1.0 + lax.erf(pre * ROOT_HALF))
        bstore[1, :, cols] = (pre * half).astype(bf16)
        slope[:, cols] = half + pre * jnp.exp(-0.5 * pre * pre) * INV_ROOT_TAU
        return carry

    lax.fori_loop(0, 4, up_chunk, 0)

    def down_chunk(i, carry):
        row = pl.ds(pl.multiple_of(i * C, 16), C)
        w = w2[1, pl.ds(i * 4, 4)].reshape(C, FF)
        hid[row] = hid[row] + mt(w, bstore[1]) + vcol[row, 3:4]
        return carry

    lax.fori_loop(0, 4, down_chunk, 0)

    mean2, inv2 = norm_stats(hid)
    for copy in tt:
        copy.wait_recv()
    valid = lane_iota + c * TOK < length
    gcol[...] = jnp.zeros(gcol.shape, f32)

    def norm2(i, carry):
        total, crossed, loss = carry
        row = pl.ds(pl.multiple_of(i * C, 16), C)
        n = (hid[row] - mean2) * inv2
        hid[row] = n
        final = n * vcol[row, 4:5] + vcol[row, 5:6]
        delta[row] = final.astype(bf16)
        g = jnp.where(valid, final - tf[i].astype(f32), 0.0)
        gcol[row, 4:5] = jnp.sum(g * n, axis=1, keepdims=True)
        gcol[row, 5:6] = jnp.sum(g, axis=1, keepdims=True)
        s = g * vcol[row, 4:5]
        sg[row] = s
        return (
            total + jnp.sum(s, axis=0, keepdims=True),
            crossed + jnp.sum(s * n, axis=0, keepdims=True),
            loss + jnp.sum(g * g, axis=0, keepdims=True),
        )

    zero = jnp.zeros((1, TOK), f32)
    total2, crossed2, loss_row = lax.fori_loop(0, 4, norm2, (zero, zero, zero))
    fo = []
    out_o_own = local(delta.at[xrows], out_o.at[:, tcols])
    for k in (1, 2, 3):
        there = pl.ds(pl.multiple_of(lax.rem(c + k, 4) * C, 16), C)
        fo.append(links.send(delta.at[there], out_o.at[:, tcols], zdev(k)))

    def norm2_back(i, carry):
        row = pl.ds(pl.multiple_of(i * C, 16), C)
        s = inv2 * (sg[row] - total2 * (1.0 / D) - hid[row] * (crossed2 * (1.0 / D)))
        sg[row] = s
        low = s.astype(bf16)
        astore[1, row] = low
        gcol[row, 3:4] = jnp.sum(low.astype(f32), axis=1, keepdims=True)
        return carry

    lax.fori_loop(0, 4, norm2_back, 0)
    outt[...] = transposed(astore[1])

    def act_chunk(i, carry):
        cols = pl.ds(pl.multiple_of(i * D, 128), D)
        g = mm(outt[...], w2[1, :, :, cols].reshape(D, D)) * slope[:, cols]
        low = g.astype(bf16)
        bstore[0, :, cols] = low
        sv[pl.ds(8 + i, 1)] = jnp.sum(low.astype(f32), axis=0, keepdims=True)
        return carry

    lax.fori_loop(0, 4, act_chunk, 0)
    ex = [
        links.send(astore.at[e], arecv, sib),
        links.send(bstore.at[e], brecv, sib),
    ]

    def hidden_back(i, carry):
        total, crossed = carry
        row = pl.ds(pl.multiple_of(i * C, 16), C)
        w = w2[0, pl.ds(i * 4, 4)].reshape(C, FF)
        g = sg[row] + mt(w, bstore[0])
        n = nrm[row]
        gcol[row, 1:2] = jnp.sum(g * n, axis=1, keepdims=True)
        gcol[row, 2:3] = jnp.sum(g, axis=1, keepdims=True)
        s = g * vcol[row, 1:2]
        sg[row] = s
        return (
            total + jnp.sum(s, axis=0, keepdims=True),
            crossed + jnp.sum(s * n, axis=0, keepdims=True),
        )

    total1, crossed1 = lax.fori_loop(0, 4, hidden_back, (zero, zero))

    def norm1_back(i, carry):
        row = pl.ds(pl.multiple_of(i * C, 16), C)
        s = inv1 * (sg[row] - total1 * (1.0 / D) - nrm[row] * (crossed1 * (1.0 / D)))
        sg[row] = s
        low = s.astype(bf16)
        delta[row] = low
        gcol[row, 0:1] = jnp.sum(low.astype(f32), axis=1, keepdims=True)
        return carry

    for copy in fo:
        copy.wait_send()
    out_o_own.wait()
    lax.fori_loop(0, 4, norm1_back, 0)
    outt[...] = transposed(delta[...])

    for j in range(4):
        dct[j] = transposed(mm(outt[...], wo[:, j].reshape(D, C)).astype(bf16))
    dctx[:, tcols] = dct[c]
    dc = []
    for k in (1, 2, 3):
        dc.append(links.send(dct.at[lax.rem(c + k, 4)], dctx.at[:, tcols], zdev(k)))

    for copy in ex:
        copy.wait_recv()
    s1_sends = {}

    def g2_block(i, carry):
        for j in range(4):
            cols = slice(j * D, (j + 1) * D)
            row = pl.ds(pl.multiple_of(i * C, 16), C)
            g = mm(astore[d, row], bstore[d, :, cols]) + mm(arecv[row], brecv[:, cols])
            g2[pl.ds(i * 4, 4), :, cols] = g.astype(bf16).reshape(4, RB, D)
        return carry

    lax.fori_loop(0, 4, g2_block, 0)
    for j in range(4):
        for k in (1, 2, 3):
            i = ridx(j, lax.rem(b_me + k, 4))
            s1_sends[j, k] = links.send(g2.at[i], r1.at[k - 1, j], bdev(k))
    for j in range(4):
        go[:, j] = mt(delta[...], ctxa[j]).astype(bf16).reshape(16, RB, C)
    o1_sends = {}
    for j in range(4):
        for k in (1, 2, 3):
            i = ridx(j, lax.rem(b_me + k, 4))
            o1_sends[j, k] = links.send(go.at[i], ro1.at[k - 1, j], bdev(k))

    for copy in dc:
        copy.wait_recv()

    dk = jnp.zeros((HD, LEN), f32)

    def bwd_head(h, carry):
        hrow = pl.ds(pl.multiple_of(h * HD, 16), HD)
        krow = pl.ds(pl.multiple_of(C + h * HD, 16), HD)
        vrow = pl.ds(pl.multiple_of(2 * C + h * HD, 16), HD)

        def bwd_tile(n, acc):
            dk, dv = acc
            cols = pl.ds(pl.multiple_of(n * TOK, 128), TOK)
            inv = linv[h, 0:1, cols]
            dc = dctx[hrow, cols].astype(f32)
            inner = jnp.sum(dc * ctxt[hrow, cols].astype(f32), axis=0, keepdims=True) * inv
            dcs = (dc * inv).astype(bf16)
            probs = pst[h, :, cols]
            dp = mm(vtm[h, :, 0:HD], dcs) - inner
            ds = (probs.astype(f32) * dp).astype(bf16)
            dqkvt[hrow, cols] = (mm(qkvt[krow, :], ds) * (HD**-0.5)).astype(bf16)
            dk = dk + mt(qkvt[hrow, cols], ds)
            dv = dv + mt(dcs, probs)
            return dk, dv

        dk, dv = lax.fori_loop(
            0, 4, bwd_tile, (jnp.zeros((HD, LEN), f32), jnp.zeros((HD, LEN), f32))
        )
        dqkvt[krow] = dk.astype(bf16)
        dqkvt[vrow] = dv.astype(bf16)
        return carry

    lax.fori_loop(0, HEADS, bwd_head, 0)

    xsend = []

    def dx_part(i):
        row = pl.ds(pl.multiple_of(i * C, 16), C)
        return row, mm(wqkv[row], dqkvt[...])

    for k in (2, 1, 3):
        i = lax.rem(c + k, 4)
        row, g = dx_part(i)
        dxo[...] = g
        dxo[:, tcols] = dxo[:, tcols] + sg[row]
        dxp[k - 1] = dxo[...].astype(bf16)
        xsend.append(links.send(dxp.at[k - 1], rx.at[k - 1], zdev(k)))
    row, g = dx_part(c)
    dxo[...] = g
    dxo[:, tcols] = dxo[:, tcols] + sg[row]

    for i in range(4):
        g = mt(xf[i * C : (i + 1) * C], dqkvt[...])
        gq[i * 4 : (i + 1) * 4] = g.astype(bf16).reshape(4, RB, 3 * C)
    q1_sends = {}
    for j in range(4):
        for k in (1, 2, 3):
            i = ridx(j, lax.rem(b_me + k, 4))
            q1_sends[j, k] = links.send(gq.at[i], rq1.at[k - 1, j], bdev(k))

    sv[0:8] = transposed(gcol[...])[0:8]
    sv[6:7] = jnp.broadcast_to(jnp.sum(loss_row, axis=1, keepdims=True), (1, D))
    sv[7:8] = jnp.broadcast_to(length.astype(f32), (1, D))
    bias_sum = mm_ones(dqkvt)
    sv[12:16] = jnp.zeros((4, D), f32)
    sv[12:13, 0 : 3 * C] = bias_sum
    v1 = [links.send(sv, rsv.at[0], sib)]
    for copy in v1:
        copy.wait()
    sv[...] = sv[...] + rsv[0]
    n_sv = 1
    for stage, dev in enumerate((adev, bdev, zdev)):
        if stage == 2:
            svq_o[...] = sv[8:16]
        vs = []
        for k in (1, 2, 3):
            vs.append(links.send(sv, rsv.at[n_sv], dev(k)))
            n_sv += 1
        for copy in vs:
            copy.wait()
        sv[...] = sv[...] + rsv[n_sv - 3] + rsv[n_sv - 2] + rsv[n_sv - 1]
    sv_o[...] = sv[...]

    def first_sums(sends, own, recv, summed, peer_recv):
        done = []
        for j in range(4):
            for k in (1, 2, 3):
                sends[j, k].wait_recv()
            i = ridx(j, b_me)
            total = own[i].astype(f32)
            for k in (1, 2, 3):
                total = total + recv[k - 1, j].astype(f32)
            summed[j] = total.astype(bf16)
        for k in (1, 2, 3):
            done.append(
                links.send(summed.at[lax.rem(a_me + k, 4)], peer_recv.at[k - 1], adev(k))
            )
        return done

    w2_sends = first_sums(s1_sends, g2, r1, s1, r2)
    o2_sends = first_sums(o1_sends, go, ro1, so1, ro2)
    q2_sends = first_sums(q1_sends, gq, rq1, sq1, rq2)

    for copy in xsend:
        copy.wait_recv()
    gi_o[...] = dxo[...] + rx[0].astype(f32) + rx[1].astype(f32) + rx[2].astype(f32)

    def second_sum(sends, summed, recv):
        for copy in sends:
            copy.wait_recv()
        total = summed[a_me].astype(f32)
        for k in range(3):
            total = total + recv[k].astype(f32)
        return total

    s2[...] = second_sum(w2_sends, s1, r2).astype(bf16)
    w3 = []
    for k in (1, 2, 3):
        there = pl.ds(pl.multiple_of(lax.rem(c + k, 4) * D, 128), D)
        w3.append(links.send(s2.at[:, there], r3.at[k - 1], zdev(k)))
    so2[...] = second_sum(o2_sends, so1, ro2).astype(bf16)
    o3 = []
    for k in (1, 2, 3):
        o3.append(links.send(so2.at[lax.rem(c + k, 4)], ro3.at[k - 1], zdev(k)))
    dqkv = second_sum(q2_sends, sq1, rq2)
    xq1[0] = dqkv
    q3 = links.send(xq1.at[0], xq1.at[1], sib)
    for copy in w3:
        copy.wait_recv()
    total = s2[:, own_cols].astype(f32)
    for k in range(3):
        total = total + r3[k].astype(f32)
    x1[0] = total
    w4 = links.send(x1.at[0], x1.at[1], sib)
    for copy in o3:
        copy.wait_recv()
    ototal = so2[c].astype(f32)
    for k in range(3):
        ototal = ototal + ro3[k].astype(f32)
    xo1[0] = ototal
    o4 = links.send(xo1.at[0], xo1.at[1], sib)
    q3.wait_recv()
    dqkv_o[...] = dqkv + xq1[1]
    w4.wait_recv()
    dw2_o[d] = total
    dw2_o[e] = x1[1]
    o4.wait_recv()
    dwo_o[...] = ototal + xo1[1]

    for copy in links.all:
        copy.wait()


def mm_ones(ref):
    ones = jnp.ones((8, LEN), bf16)
    return mt(ones, ref[...])[0:1]


def local_step(
    inputs, teacher, lengths, query_weight, query_bias, key_weight, value_weight, value_bias,
    output_weight, output_bias, first_gain, first_shift, up_weight, up_bias, down_weight,
    down_bias, second_gain, second_shift,
):
    wqkv = jnp.concatenate([query_weight, key_weight, value_weight], axis=1)
    zero = jnp.zeros_like(query_bias)
    up_rows = up_bias.reshape(4, C)
    vec = jnp.stack(
        [output_bias, first_gain, first_shift, down_bias, second_gain, second_shift,
         up_rows[0], up_rows[1], up_rows[2], up_rows[3], query_bias, value_bias,
         zero, zero, zero, zero]
    )
    ub = jnp.broadcast_to(up_bias[None], (8, D))
    anyspec = pl.BlockSpec(memory_space=pl.ANY)
    vm = pl.BlockSpec(memory_space=pltpu.VMEM)
    sds = jax.ShapeDtypeStruct
    V = pltpu.VMEM
    out, gi, dw2, dwo, dqkv, sv, svq = pl.pallas_call(
        layer,
        name="layer",
        out_shape=(
            sds((C, LEN), bf16),
            sds((C, LEN), f32),
            sds((2, RB, D), f32),
            sds((RB, C), f32),
            sds((RB, 3 * C), f32),
            sds((16, D), f32),
            sds((8, D), f32),
        ),
        in_specs=[
            anyspec, anyspec, pl.BlockSpec(memory_space=pltpu.SMEM),
            anyspec, anyspec, anyspec, anyspec, anyspec, anyspec,
        ],
        out_specs=(anyspec, vm, vm, vm, vm, vm, vm),
        scratch_shapes=[
            V((D, LEN), bf16),
            V((4, C, TOK), bf16),
            V((D, 3 * C), bf16),
            V((16, 4, RB, C), bf16),
            V((2, 16, RB, FF), bf16),
            V((4, 16, C), f32),
            V((4, 8, D), f32),
            V((D, 128), f32),
            V((2 * C, LEN), bf16),
            V((HEADS, LEN, 2 * HD), bf16),
            V((HEADS, 2 * HD, LEN), bf16),
            V((HEADS, HD + 16, LEN), bf16),
            V((HEADS, LEN, 2 * HD), bf16),
            V((HEADS, LEN, LEN), bf16),
            V((HEADS, 8, LEN), f32),
            V((C, LEN), bf16),
            V((4, C, TOK), bf16),
            V((D, TOK), f32),
            V((D, TOK), f32),
            V((D, TOK), f32),
            V((2, TOK, FF), bf16),
            V((2, D, TOK), bf16),
            V((TOK, FF), f32),
            V((TOK, FF), bf16),
            V((D, TOK), bf16),
            V((16, RB, FF), bf16),
            V((16, 4, RB, C), bf16),
            V((16, RB, 3 * C), bf16),
            V((C, LEN), bf16),
            V((4, C, TOK), bf16),
            V((TOK, D), bf16),
            V((D, TOK), bf16),
            V((3 * C, LEN), bf16),
            V((3, C, LEN), bf16),
            V((C, LEN), f32),
            V((3, C, LEN), bf16),
            V((3, 4, RB, FF), bf16),
            V((4, RB, FF), bf16),
            V((3, RB, FF), bf16),
            V((RB, FF), bf16),
            V((3, RB, D), bf16),
            V((3, 4, 4, RB, C), bf16),
            V((4, 4, RB, C), bf16),
            V((3, 4, RB, C), bf16),
            V((4, RB, C), bf16),
            V((3, RB, C), bf16),
            V((3, 4, RB, 3 * C), bf16),
            V((4, RB, 3 * C), bf16),
            V((3, RB, 3 * C), bf16),
            V((2, RB, D), f32),
            V((2, RB, C), f32),
            V((2, RB, 3 * C), f32),
            V((D, 128), f32),
            V((16, D), f32),
            V((10, 16, D), f32),
            V((2, RB, D), bf16),
            pltpu.SemaphoreType.DMA((12,)),
            pltpu.SemaphoreType.DMA((N_SEM,)),
            pltpu.SemaphoreType.DMA((N_SEM,)),
        ],
        compiler_params=pltpu.CompilerParams(
            collective_id=0, has_side_effects=True, vmem_limit_bytes=62 * 2**20
        ),
    )(inputs, teacher, lengths, wqkv, output_weight.T, up_weight, down_weight, vec, ub)
    c = lax.axis_index("col")
    count = sv[7, 0] * 0.25
    factor = SLOTS / count
    loss = sv[6, 0] / (2.0 * D * count)
    mine = lax.dynamic_slice_in_dim(sv[0:6], c * C, C, axis=1) * factor
    up_b = lax.dynamic_slice_in_dim(sv[8:12], c, 1, axis=0)[0] * factor
    dqkv = dqkv * factor
    bq = svq[4] * factor
    return (
        out,
        loss,
        gi * factor,
        dqkv[:, :C],
        bq[0:C],
        dqkv[:, C : 2 * C],
        dqkv[:, 2 * C :],
        bq[2 * C : 3 * C],
        dwo.T * factor,
        mine[0],
        mine[1],
        mine[2],
        dw2[0] * factor,
        up_b,
        dw2[1] * factor,
        mine[3],
        mine[4],
        mine[5],
    )


def solution(mesh):
    split = Mesh(
        mesh.devices.reshape(mesh.shape["dp"], 4, 4, mesh.shape["col"]), AXES
    )
    tokens = P("col", DP_ROW)
    weight = P(ROW, "col")
    vector = P("col")
    return jax.shard_map(
        local_step,
        mesh=split,
        in_specs=(
            tokens, tokens, P(DP_ROW), weight, vector, weight, weight, vector,
            P("col", ROW), vector, vector, vector, weight, vector, weight,
            vector, vector, vector,
        ),
        out_specs=(
            tokens, P(), tokens, weight, vector, weight, weight, vector,
            P("col", ROW), vector, vector, vector, weight, vector, weight,
            vector, vector, vector,
        ),
        check_vma=False,
    )
```

```python
import jax
import jax.numpy as jnp
from jax import lax
from jax.experimental import pallas as pl
from jax.experimental.pallas import tpu as pltpu
from jax.sharding import Mesh
from jax.sharding import PartitionSpec as P

D = 768
FF = 3072
LEN = 1024
HD = 64
HEADS = 3
C = 192
TOK = 256
RB = 48
SLOTS = 32768
EPS = 1e-12
MASK = -1e30
ROOT_HALF = 0.7071067811865476
INV_ROOT_TAU = 0.3989422804014327
AXES = ("dp", "row_0", "row_1", "col")
ROW = ("row_0", "row_1")
DP_ROW = ("dp", "row_0", "row_1")
N_SEM = 256
f32 = jnp.float32
bf16 = jnp.bfloat16


def mm(a, b):
    return lax.dot_general(a, b, (((1,), (0,)), ((), ())), preferred_element_type=f32)


def mt(a, b):
    return lax.dot_general(a, b, (((1,), (1,)), ((), ())), preferred_element_type=f32)


def transposed(a):
    return jnp.transpose(a, (1, 0))


class Sent:
    def __init__(self, copy):
        self.copy, self.open_send, self.open_recv = copy, True, True

    def wait_send(self):
        if self.open_send:
            self.copy.wait_send()
        self.open_send = False

    def wait_recv(self):
        if self.open_recv:
            self.copy.wait_recv()
        self.open_recv = False

    def wait(self):
        self.wait_send()
        self.wait_recv()


class Links:
    def __init__(self, ssem, rsem):
        self.ssem, self.rsem, self.n, self.all = ssem, rsem, 0, []

    def send(self, src, dst, dev):
        copy = pltpu.make_async_remote_copy(
            src_ref=src,
            dst_ref=dst,
            send_sem=self.ssem.at[self.n],
            recv_sem=self.rsem.at[self.n],
            device_id=dev,
            device_id_type=pl.DeviceIdType.MESH,
        )
        copy.start()
        self.n += 1
        self.all.append(Sent(copy))
        return self.all[-1]


def layer(
    x_in, t_in, len_in, wq_in, wk_in, wv_in, wo_in, up_in, down_in,
    ob_in, g1_in, b1_in, db_in, g2_in, b2_in, qb_in, vb_in, ub_in,
    out_o, gi_o, dw2_o, dwo_o, dqkv_o, sv_o,
    xf, tf, w2, aux, wo4, wqkvt, vec, ub, vcol, qkvt, ktm, qaug, vaug, vtm, pst, linv,
    ctxt, ctxa, hid, nrm, sg, bstore, astore, slope, brecv, arecv,
    g2, ga, gar, dctx, dct, outt, delta,
    dqkvt, dxp, dxo, rx, im, rm, s1, r2, s2, r3, ia, ra, sa1, ra2, sa2, ra3,
    x1, xa1, xo1, gcol, sv, rsv, wown,
    lsem, ssem, rsem,
):
    d = lax.axis_index("dp")
    y = lax.axis_index("row_0")
    x = lax.axis_index("row_1")
    c = lax.axis_index("col")
    e = 1 - d
    r = 4 * y + x
    a_me = x * e + y * d
    b_me = y * e + x * d
    b_left = lax.rem(b_me + 3, 4)
    b_right = lax.rem(b_me + 1, 4)
    b_far = lax.rem(b_me + 2, 4)

    def ridx(a, b):
        return (4 * b + a) * e + (4 * a + b) * d

    def zdev(k):
        return {"col": lax.rem(c + k, 4)}

    def adev(k):
        return {"row_0": lax.rem(y + k * d, 4), "row_1": lax.rem(x + k * e, 4)}

    def bdev(k):
        return {"row_0": lax.rem(y + k * e, 4), "row_1": lax.rem(x + k * d, 4)}

    sib = {"dp": e}
    links = Links(ssem, rsem)

    def wait_all(copies):
        for copy in copies:
            copy.wait_recv()

    n_local = [0]

    def local(src, dst):
        copy = pltpu.make_async_copy(src, dst, lsem.at[n_local[0]])
        copy.start()
        n_local[0] += 1
        return copy

    xrows = pl.ds(pl.multiple_of(c * C, 16), C)
    tcols = pl.ds(pl.multiple_of(c * TOK, 128), TOK)
    own_cols = pl.ds(pl.multiple_of(c * D, 128), D)
    bar = pltpu.get_barrier_semaphore()
    for k in (1, 2, 3):
        for dev in (zdev(k), adev(k), bdev(k)):
            pl.semaphore_signal(bar, inc=1, device_id=dev, device_id_type=pl.DeviceIdType.MESH)
    pl.semaphore_signal(bar, inc=1, device_id=sib, device_id_type=pl.DeviceIdType.MESH)
    cup = local(up_in, wown.at[0])
    cdn = local(down_in, wown.at[1])
    cx = local(x_in, xf.at[xrows])
    ct = local(t_in.at[:, tcols], tf.at[c])
    wo4[c] = transposed(wo_in[...])
    for i, ref in enumerate((ob_in, g1_in, b1_in, db_in, g2_in, b2_in, qb_in, vb_in)):
        vec[c, i : i + 1, :] = ref[...].reshape(1, C)
    ub[c, 0:1, :] = ub_in[...].reshape(1, D)
    own_qkv = jnp.concatenate(
        [wq_in[...], wk_in[...], wv_in[...], jnp.zeros((RB, C), bf16)], axis=1
    )
    cup.wait()
    cdn.wait()
    pl.semaphore_wait(bar, 10)

    oz = [links.send(wo4.at[c], wo4.at[c], zdev(k)) for k in (1, 3, 2)]
    wz = [links.send(wown.at[d], w2.at[d, r, :, own_cols], zdev(k)) for k in (1, 3, 2)]
    vz = [links.send(vec.at[c], vec.at[c], zdev(k)) for k in (1, 2, 3)]
    uz = [links.send(ub.at[c], ub.at[c], zdev(k)) for k in (1, 2, 3)]
    w2[d, r, :, own_cols] = wown[d]

    def xhalf(i, top):
        return xf.at[pl.ds(pl.multiple_of(i * C + (0 if top else C // 2), 16), C // 2)]

    cx.wait()
    xs = {}
    for k, order in ((1, (True, False)), (3, (False, True))):
        for top in order:
            xs[k, top] = links.send(xhalf(c, top), xhalf(c, top), zdev(k))

    def along_a(buf):
        return [links.send(buf.at[d, r], buf.at[d, r], adev(k)) for k in (1, 3, 2)]

    def block(k, b):
        return ridx(lax.rem(a_me + 4 - k, 4), b)

    def along_b(buf, k):
        ref = buf.at[d, block(k, b_me)]
        return (links.send(ref, ref, bdev(1)), links.send(ref, ref, bdev(3)))

    def to_sibling(buf, k, b):
        ref = buf.at[d, block(k, b)]
        return links.send(ref, ref, sib)

    FWD_PLUS, FWD_MINUS = (0, 2), (1, 3)

    def forward(buf, sent):
        far = {}
        for k in FWD_PLUS:
            sent[k][0].wait_recv()
            ref = buf.at[d, block(k, b_left)]
            far[k] = links.send(ref, ref, bdev(1))
        for k in FWD_MINUS:
            sent[k][1].wait_recv()
            ref = buf.at[d, block(k, b_right)]
            far[k] = links.send(ref, ref, bdev(3))
        return far

    wait_all(oz)
    own_wo = jnp.concatenate([wo4[j] for j in range(4)], axis=1)
    aux[d, r] = jnp.where(d == 0, own_qkv, own_wo)
    aux_a = along_a(aux)
    aux_b = {0: along_b(aux, 0)}
    aux_s = [to_sibling(aux, 0, b_me)]
    wait_all(wz)
    w_a = along_a(w2)
    wait_all(aux_a)
    for k in (1, 3, 2):
        aux_b[k] = along_b(aux, k)
    w_b = {0: along_b(w2, 0)}
    for k in (1, 3, 2):
        aux_s.append(to_sibling(aux, k, b_me))
    xs[1, True].wait_recv()
    left = lax.rem(c + 3, 4)
    xs["f", 1] = links.send(xhalf(left, True), xhalf(left, True), zdev(1))
    xs[3, False].wait_recv()
    right = lax.rem(c + 1, 4)
    xs["f", 3] = links.send(xhalf(right, False), xhalf(right, False), zdev(3))
    w_s = [to_sibling(w2, 0, b_me)]
    aux_far = forward(aux, aux_b)
    for i, k in enumerate((1, 3, 2)):
        w_a[i].wait_recv()
        w_b[k] = along_b(w2, k)
        w_s.append(to_sibling(w2, k, b_me))
    for k in range(4):
        aux_b[k][0].wait_recv()
        aux_s.append(to_sibling(aux, k, b_left))
        aux_b[k][1].wait_recv()
        aux_s.append(to_sibling(aux, k, b_right))
    for k in range(4):
        aux_far[k].wait_recv()
        aux_s.append(to_sibling(aux, k, b_far))

    wait_all(vz + uz)
    for i in range(4):
        vcol[i * C : (i + 1) * C, 0:16] = transposed(vec[i])
    vown = transposed(vec[c])
    length = len_in[0]

    wait_all([xs[key] for key in ((1, False), (3, True), ("f", 1), ("f", 3))])
    wait_all(aux_s)
    for i in range(3):
        wqkvt[i] = transposed(aux[0].reshape(D, D)[:, i * C : (i + 1) * C])
    q_bias = vown[:, 6:7]
    v_bias = vown[:, 7:8]
    lane_iota = lax.broadcasted_iota(jnp.int32, (1, TOK), 1)
    first_row = lax.broadcasted_iota(jnp.int32, (HD, TOK), 0) == 0

    def qkv_chunk(i, carry):
        cols = pl.ds(pl.multiple_of(i * TOK, 128), TOK)
        tok = xf[:, cols]
        q = (mm(wqkvt[0], tok) + q_bias).astype(bf16)
        k = mm(wqkvt[1], tok).astype(bf16)
        v = (mm(wqkvt[2], tok) + v_bias).astype(bf16)
        q = (q.astype(f32) * (HD**-0.5)).astype(bf16)
        qkvt[0:C, cols] = q
        qkvt[C : 2 * C, cols] = k
        bias = jnp.where(lane_iota + i * TOK < length, 0.0, MASK)
        bias = jnp.where(first_row, jnp.broadcast_to(bias, (HD, TOK)), 0.0).astype(bf16)
        ones = jnp.where(first_row, 1.0, 0.0).astype(bf16)
        for h in range(HEADS):
            hs = slice(h * HD, (h + 1) * HD)
            qaug[h, 0:HD, cols] = q[hs]
            qaug[h, HD : 2 * HD, cols] = ones
            vaug[h, 0:HD, cols] = v[hs]
            vaug[h, HD : HD + 16, cols] = ones[0:16]
            ktm[h, cols, :] = transposed(jnp.concatenate([k[hs], bias], axis=0))
            vtm[h, cols, :] = transposed(jnp.concatenate([v[hs], ones], axis=0))
        return carry

    lax.fori_loop(0, 4, qkv_chunk, 0)
    ct.wait()
    tt = []
    for k in (1, 3, 2):
        there = pl.ds(pl.multiple_of(lax.rem(c + k, 4) * TOK, 128), TOK)
        tt.append(links.send(t_in.at[:, there], tf.at[c], zdev(k)))

    def fwd_head(h):
        def fwd_tile(n, carry):
            cols = pl.ds(pl.multiple_of(n * TOK, 128), TOK)
            score = mm(ktm[h], qaug[h, :, cols])
            top = jnp.max(score, axis=0, keepdims=True)
            probs = jnp.exp(score - top).astype(bf16)
            pst[h, :, cols] = probs
            both = mm(vaug[h], probs)
            inv = 1.0 / both[HD : HD + 1]
            linv[h, 0:1, cols] = inv
            ctxt[pl.ds(pl.multiple_of(h * HD, 16), HD), cols] = (both[0:HD] * inv).astype(bf16)
            return carry

        lax.fori_loop(0, 4, fwd_tile, 0)

    def fwd_heads(lo, hi):
        lax.fori_loop(lo, hi, lambda h, carry: (fwd_head(h), carry)[1], 0)

    fwd_heads(0, 1)
    w_far = forward(w2, w_b)
    fwd_heads(1, 3)

    cc = []
    ctxa[c] = ctxt[:, tcols]
    for k in (1, 3, 2):
        there = pl.ds(pl.multiple_of(lax.rem(c + k, 4) * TOK, 128), TOK)
        cc.append(links.send(ctxt.at[:, there], ctxa.at[c], zdev(k)))
    for k in range(4):
        w_b[k][0].wait_recv()
        w_s.append(to_sibling(w2, k, b_left))
        w_b[k][1].wait_recv()
        w_s.append(to_sibling(w2, k, b_right))
    wait_all(cc)

    def proj(i, carry):
        row = pl.ds(pl.multiple_of(i * C, 16), C)
        acc = xf[row, tcols].astype(f32) + vcol[row, 0:1]
        w = aux[1, pl.ds(i * 4, 4)].reshape(C, D)
        hid[row] = acc + mm(w, ctxa[...].reshape(D, TOK))
        return carry

    lax.fori_loop(0, 4, proj, 0)

    def norm_stats(ref):
        v = ref[...]
        mean = jnp.sum(v, axis=0, keepdims=True) * (1.0 / D)
        square = jnp.sum(v * v, axis=0, keepdims=True) * (1.0 / D)
        return mean, lax.rsqrt(square - mean * mean + EPS)

    mean1, inv1 = norm_stats(hid)

    def norm1(i, carry):
        row = pl.ds(pl.multiple_of(i * C, 16), C)
        n = (hid[row] - mean1) * inv1
        nrm[row] = n
        h = n * vcol[row, 1:2] + vcol[row, 2:3]
        hid[row] = h
        astore[0, row] = h.astype(bf16)
        return carry

    lax.fori_loop(0, 4, norm1, 0)
    outt[...] = transposed(astore[0])
    for k in range(4):
        w_far[k].wait_recv()
        w_s.append(to_sibling(w2, k, b_far))

    wait_all(w_s)

    def up_chunk(i, carry):
        cols = pl.ds(pl.multiple_of(i * D, 128), D)
        pre = mm(outt[...], w2[0, :, :, cols].reshape(D, D)) + ub[i, 0:1]
        half = 0.5 * (1.0 + lax.erf(pre * ROOT_HALF))
        bstore[1, :, cols] = (pre * half).astype(bf16)
        slope[:, cols] = half + pre * jnp.exp(-0.5 * pre * pre) * INV_ROOT_TAU
        return carry

    lax.fori_loop(0, 4, up_chunk, 0)

    def down_chunk(i, carry):
        row = pl.ds(pl.multiple_of(i * C, 16), C)
        w = w2[1, pl.ds(i * 4, 4)].reshape(C, FF)
        hid[row] = hid[row] + mt(w, bstore[1]) + vcol[row, 3:4]
        return carry

    lax.fori_loop(0, 4, down_chunk, 0)

    mean2, inv2 = norm_stats(hid)
    wait_all(tt)
    valid = lane_iota + c * TOK < length
    gcol[...] = jnp.zeros(gcol.shape, f32)

    def norm2(i, carry):
        total, crossed, loss = carry
        row = pl.ds(pl.multiple_of(i * C, 16), C)
        n = (hid[row] - mean2) * inv2
        hid[row] = n
        final = n * vcol[row, 4:5] + vcol[row, 5:6]
        delta[row] = final.astype(bf16)
        g = jnp.where(valid, final - tf[i].astype(f32), 0.0)
        gcol[row, 4:5] = jnp.sum(g * n, axis=1, keepdims=True)
        gcol[row, 5:6] = jnp.sum(g, axis=1, keepdims=True)
        s = g * vcol[row, 4:5]
        sg[row] = s
        return (
            total + jnp.sum(s, axis=0, keepdims=True),
            crossed + jnp.sum(s * n, axis=0, keepdims=True),
            loss + jnp.sum(g * g, axis=0, keepdims=True),
        )

    zero = jnp.zeros((1, TOK), f32)
    total2, crossed2, loss_row = lax.fori_loop(0, 4, norm2, (zero, zero, zero))
    fo = []
    out_o_own = local(delta.at[xrows], out_o.at[:, tcols])
    for k in (1, 3, 2):
        there = pl.ds(pl.multiple_of(lax.rem(c + k, 4) * C, 16), C)
        fo.append(links.send(delta.at[there], out_o.at[:, tcols], zdev(k)))

    def norm2_back(i, carry):
        row = pl.ds(pl.multiple_of(i * C, 16), C)
        s = inv2 * (sg[row] - total2 * (1.0 / D) - hid[row] * (crossed2 * (1.0 / D)))
        sg[row] = s
        low = s.astype(bf16)
        astore[1, row] = low
        gcol[row, 3:4] = jnp.sum(low.astype(f32), axis=1, keepdims=True)
        return carry

    lax.fori_loop(0, 4, norm2_back, 0)
    outt[...] = transposed(astore[1])

    def act_chunk(i, carry):
        cols = pl.ds(pl.multiple_of(i * D, 128), D)
        g = mm(outt[...], w2[1, :, :, cols].reshape(D, D)) * slope[:, cols]
        low = g.astype(bf16)
        bstore[0, :, cols] = low
        sv[pl.ds(8 + i, 1)] = jnp.sum(low.astype(f32), axis=0, keepdims=True)
        return carry

    lax.fori_loop(0, 4, act_chunk, 0)
    ex = [
        links.send(astore.at[e], arecv, sib),
        links.send(bstore.at[e], brecv, sib),
    ]

    def hidden_back(i, carry):
        total, crossed = carry
        row = pl.ds(pl.multiple_of(i * C, 16), C)
        w = w2[0, pl.ds(i * 4, 4)].reshape(C, FF)
        g = sg[row] + mt(w, bstore[0])
        n = nrm[row]
        gcol[row, 1:2] = jnp.sum(g * n, axis=1, keepdims=True)
        gcol[row, 2:3] = jnp.sum(g, axis=1, keepdims=True)
        s = g * vcol[row, 1:2]
        sg[row] = s
        return (
            total + jnp.sum(s, axis=0, keepdims=True),
            crossed + jnp.sum(s * n, axis=0, keepdims=True),
        )

    total1, crossed1 = lax.fori_loop(0, 4, hidden_back, (zero, zero))

    def norm1_back(i, carry):
        row = pl.ds(pl.multiple_of(i * C, 16), C)
        s = inv1 * (sg[row] - total1 * (1.0 / D) - nrm[row] * (crossed1 * (1.0 / D)))
        sg[row] = s
        low = s.astype(bf16)
        delta[row] = low
        gcol[row, 0:1] = jnp.sum(low.astype(f32), axis=1, keepdims=True)
        return carry

    for copy in fo:
        copy.wait_send()
    out_o_own.wait()
    lax.fori_loop(0, 4, norm1_back, 0)
    outt[...] = transposed(delta[...])

    dc = []
    for j in range(4):
        w = aux[1].reshape(D, D)[:, j * C : (j + 1) * C]
        dct[j] = transposed(mm(outt[...], w).astype(bf16))
    dctx[:, tcols] = dct[c]
    for k in (1, 3, 2):
        dc.append(links.send(dct.at[lax.rem(c + k, 4)], dctx.at[:, tcols], zdev(k)))

    sv[0:8] = transposed(gcol[...])[0:8]
    sv[6:7] = jnp.broadcast_to(jnp.sum(loss_row, axis=1, keepdims=True), (1, D))
    sv[7:8] = jnp.broadcast_to(length.astype(f32), (1, D))
    sv[12:16] = jnp.zeros((4, D), f32)
    n_sv = [1]
    v_sent = [links.send(sv, rsv.at[0], sib)]

    def sv_add():
        got = []
        for copy in v_sent:
            copy.wait()
        lo = n_sv[0] - len(v_sent)
        total = sv[...]
        for i in range(len(v_sent)):
            total = total + rsv[lo + i]
        sv[...] = total
        v_sent.clear()

    def sv_send(dev):
        for k in (1, 3, 2):
            v_sent.append(links.send(sv, rsv.at[n_sv[0]], dev(k)))
            n_sv[0] += 1

    wait_all(ex)

    def g2_block(i, carry):
        for j in range(4):
            cols = slice(j * D, (j + 1) * D)
            row = pl.ds(pl.multiple_of(i * C, 16), C)
            g = mm(astore[d, row], bstore[d, :, cols]) + mm(arecv[row], brecv[:, cols])
            g2[pl.ds(i * 4, 4), :, cols] = g.astype(bf16).reshape(4, RB, D)
        return carry

    lax.fori_loop(0, 4, g2_block, 0)
    sv_add()
    sv_send(bdev)

    VIA_PLUS, VIA_MINUS = (0, 1), (2, 3)

    def sum_start(own, mid, recv):
        m = {}
        for j in VIA_PLUS:
            m[j] = links.send(own(ridx(j, b_far)), mid.at[j], bdev(1))
        for j in VIA_MINUS:
            m[j] = links.send(own(ridx(j, b_far)), mid.at[j], bdev(3))
        got = {}
        for j in VIA_MINUS:
            got[0, j] = links.send(own(ridx(j, b_right)), recv.at[0, j], bdev(1))
        for j in VIA_PLUS:
            got[1, j] = links.send(own(ridx(j, b_left)), recv.at[1, j], bdev(3))
        return m, got

    def sum_mid(own, mid, recv, m, got):
        for j in VIA_PLUS:
            m[j].wait_recv()
            mid[j] = (own(ridx(j, b_right))[...].astype(f32) + mid[j].astype(f32)).astype(bf16)
            got[0, j] = links.send(mid.at[j], recv.at[0, j], bdev(1))
        for j in VIA_MINUS:
            m[j].wait_recv()
            mid[j] = (own(ridx(j, b_left))[...].astype(f32) + mid[j].astype(f32)).astype(bf16)
            got[1, j] = links.send(mid.at[j], recv.at[1, j], bdev(3))

    def sum_end(own, recv, got, summed, peer_recv):
        for j in range(4):
            got[0, j].wait_recv()
            got[1, j].wait_recv()
            total = own(ridx(j, b_me))[...].astype(f32)
            total = total + recv[0, j].astype(f32) + recv[1, j].astype(f32)
            summed[j] = total.astype(bf16)
        return [
            links.send(summed.at[lax.rem(a_me + k, 4)], peer_recv.at[k - 1], adev(k))
            for k in (1, 3, 2)
        ]

    def sum_a(sends, summed, recv):
        wait_all(sends)
        total = summed[a_me].astype(f32)
        for k in range(3):
            total = total + recv[k].astype(f32)
        return total

    def own_w(i):
        return g2.at[i]

    def own_aux(i):
        return ga.at[d, i]

    w_mid, w_got = sum_start(own_w, im, rm)
    g = mt(delta[...], ctxa[...].reshape(D, TOK)).astype(bf16)
    ga[1] = g.reshape(16, RB, D)

    wait_all(dc)

    def bwd_head(h, carry):
        hrow = pl.ds(pl.multiple_of(h * HD, 16), HD)
        krow = pl.ds(pl.multiple_of(C + h * HD, 16), HD)
        vrow = pl.ds(pl.multiple_of(2 * C + h * HD, 16), HD)

        def bwd_tile(n, acc):
            dk, dv = acc
            cols = pl.ds(pl.multiple_of(n * TOK, 128), TOK)
            inv = linv[h, 0:1, cols]
            dc = dctx[hrow, cols].astype(f32)
            inner = jnp.sum(dc * ctxt[hrow, cols].astype(f32), axis=0, keepdims=True) * inv
            dcs = (dc * inv).astype(bf16)
            probs = pst[h, :, cols]
            dp = mm(vtm[h, :, 0:HD], dcs) - inner
            ds = (probs.astype(f32) * dp).astype(bf16)
            dqkvt[hrow, cols] = (mm(qkvt[krow, :], ds) * (HD**-0.5)).astype(bf16)
            dk = dk + mt(qkvt[hrow, cols], ds)
            dv = dv + mt(dcs, probs)
            return dk, dv

        dk, dv = lax.fori_loop(
            0, 4, bwd_tile, (jnp.zeros((HD, LEN), f32), jnp.zeros((HD, LEN), f32))
        )
        dqkvt[krow] = dk.astype(bf16)
        dqkvt[vrow] = dv.astype(bf16)
        return carry

    lax.fori_loop(0, 1, bwd_head, 0)
    sv_add()
    sv_send(adev)
    lax.fori_loop(1, 2, bwd_head, 0)
    sum_mid(own_w, im, rm, w_mid, w_got)
    sv_add()
    sv_send(zdev)
    lax.fori_loop(2, 3, bwd_head, 0)

    ones = jnp.ones((8, LEN), bf16)
    bias_sum = mt(ones, dqkvt[...])[0:1]
    row_iota = lax.broadcasted_iota(jnp.int32, (RB, C), 0)
    bias_rows = jnp.where(
        row_iota == 0,
        jnp.broadcast_to(bias_sum[:, 0:C], (RB, C)),
        jnp.where(row_iota == 1, jnp.broadcast_to(bias_sum[:, 2 * C :], (RB, C)), 0.0),
    ).astype(bf16)

    def dqkv_block(i, carry):
        row = pl.ds(pl.multiple_of(i * C, 16), C)
        g = mt(xf[row], dqkvt[...])
        ga[0, pl.ds(i * 4, 4), :, 0 : 3 * C] = g.astype(bf16).reshape(4, RB, 3 * C)
        ga[0, pl.ds(i * 4, 4), :, 3 * C :] = jnp.broadcast_to(bias_rows[None], (4, RB, C))
        return carry

    lax.fori_loop(0, 4, dqkv_block, 0)
    gx = links.send(ga.at[e], gar, sib)

    xsend = []

    def dx_part(i):
        row = pl.ds(pl.multiple_of(i * C, 16), C)
        w = aux[0, pl.ds(i * 4, 4)].reshape(C, D)[:, 0 : 3 * C]
        return row, mm(w, dqkvt[...])

    for k in (2, 1, 3):
        i = lax.rem(c + k, 4)
        row, g = dx_part(i)
        dxo[...] = g
        dxo[:, tcols] = dxo[:, tcols] + sg[row]
        dxp[k - 1] = dxo[...].astype(bf16)
        xsend.append(links.send(dxp.at[k - 1], rx.at[k - 1], zdev(k)))
    row, g = dx_part(c)
    dxo[...] = g
    dxo[:, tcols] = dxo[:, tcols] + sg[row]

    gx.wait_recv()

    def add_sibling(i, carry):
        ga[d, i] = (ga[d, i].astype(f32) + gar[i].astype(f32)).astype(bf16)
        return carry

    lax.fori_loop(0, 16, add_sibling, 0)
    a_mid, a_got = sum_start(own_aux, ia, ra)
    w_sum = sum_end(own_w, rm, w_got, s1, r2)
    sv_add()
    sv_o[...] = sv[...]
    sum_mid(own_aux, ia, ra, a_mid, a_got)
    s2[...] = sum_a(w_sum, s1, r2).astype(bf16)
    w3 = []
    for k in (1, 3, 2):
        there = pl.ds(pl.multiple_of(lax.rem(c + k, 4) * D, 128), D)
        w3.append(links.send(s2.at[:, there], r3.at[k - 1], zdev(k)))
    a_sum = sum_end(own_aux, ra, a_got, sa1, ra2)
    wait_all(xsend)
    gi_o[...] = dxo[...] + rx[0].astype(f32) + rx[1].astype(f32) + rx[2].astype(f32)
    dqkv = sum_a(a_sum, sa1, ra2)
    xa1[0] = dqkv
    for j in range(4):
        sa2[j] = dqkv[:, j * C : (j + 1) * C].astype(bf16)
    o3 = [links.send(sa2.at[lax.rem(c + k, 4)], ra3.at[k - 1], zdev(k)) for k in (1, 3, 2)]
    q3 = links.send(xa1.at[0], xa1.at[1], sib)
    wait_all(w3)
    total = s2[:, own_cols].astype(f32)
    for k in range(3):
        total = total + r3[k].astype(f32)
    x1[0] = total
    w4 = links.send(x1.at[0], x1.at[1], sib)
    wait_all(o3)
    ototal = sa2[c].astype(f32)
    for k in range(3):
        ototal = ototal + ra3[k].astype(f32)
    xo1[0] = ototal
    o4 = links.send(xo1.at[0], xo1.at[1], sib)
    q3.wait_recv()
    dqkv_o[...] = jnp.where(d == 0, dqkv, xa1[1])
    w4.wait_recv()
    dw2_o[d] = total
    dw2_o[e] = x1[1]
    o4.wait_recv()
    dwo_o[...] = jnp.where(d == 1, ototal, xo1[1])
    for copy in links.all:
        copy.wait()


def finish(
    out_i, gi_i, dw2_i, dwo_i, dqkv_i, sv_i,
    out, loss, gi, gwq, gbq, gwk, gwv, gbv, gwo, gob, gg1, gb1, gup, gub, gdn, gdb, gg2, gb2,
    sem,
):
    c = lax.axis_index("col")
    copy = pltpu.make_async_copy(out_i, out, sem)
    copy.start()
    count = sv_i[7:8, 0:1] * 0.25
    factor = SLOTS / count
    loss[...] = sv_i[6:7, 0:1] / (2.0 * D * count)
    gi[...] = gi_i[...] * factor
    dqkv = dqkv_i[...] * factor
    gwq[...] = dqkv[:, 0:C]
    gwk[...] = dqkv[:, C : 2 * C]
    gwv[...] = dqkv[:, 2 * C : 3 * C]
    gbq[...] = dqkv[0:1, 3 * C :]
    gbv[...] = dqkv[1:2, 3 * C :]
    gwo[...] = transposed(dwo_i[...] * factor)
    gup[...] = dw2_i[0] * factor
    gdn[...] = dw2_i[1] * factor
    sums = sv_i[...] * factor
    for j in range(4):

        @pl.when(c == j)
        def _(j=j):
            gub[...] = sums[8 + j : 9 + j]
            for i, ref in enumerate((gob, gg1, gb1, gdb, gg2, gb2)):
                ref[...] = sums[i : i + 1, j * C : (j + 1) * C]

    copy.wait()


def local_step(
    inputs, teacher, lengths, query_weight, query_bias, key_weight, value_weight, value_bias,
    output_weight, output_bias, first_gain, first_shift, up_weight, up_bias, down_weight,
    down_bias, second_gain, second_shift,
):
    anyspec = pl.BlockSpec(memory_space=pl.ANY)
    vm = pl.BlockSpec(memory_space=pltpu.VMEM)
    sds = jax.ShapeDtypeStruct
    V = pltpu.VMEM
    vectors = [
        v.reshape(1, -1)
        for v in (
            output_bias, first_gain, first_shift, down_bias, second_gain, second_shift,
            query_bias, value_bias, up_bias,
        )
    ]
    got = pl.pallas_call(
        layer,
        name="layer",
        out_shape=(
            sds((C, LEN), bf16),
            sds((C, LEN), f32),
            sds((2, RB, D), f32),
            sds((RB, C), f32),
            sds((RB, D), f32),
            sds((16, D), f32),
        ),
        in_specs=[anyspec, anyspec, pl.BlockSpec(memory_space=pltpu.SMEM)]
        + [vm] * 4
        + [anyspec] * 2
        + [vm] * 9,
        out_specs=(anyspec, vm, vm, vm, vm, vm),
        scratch_shapes=[
            V((D, LEN), bf16),
            V((4, C, TOK), bf16),
            V((2, 16, RB, FF), bf16),
            V((2, 16, RB, D), bf16),
            V((4, RB, C), bf16),
            V((3, C, D), bf16),
            V((4, 16, C), f32),
            V((4, 8, D), f32),
            V((D, 128), f32),
            V((2 * C, LEN), bf16),
            V((HEADS, LEN, 2 * HD), bf16),
            V((HEADS, 2 * HD, LEN), bf16),
            V((HEADS, HD + 16, LEN), bf16),
            V((HEADS, LEN, 2 * HD), bf16),
            V((HEADS, LEN, LEN), bf16),
            V((HEADS, 8, LEN), f32),
            V((C, LEN), bf16),
            V((4, C, TOK), bf16),
            V((D, TOK), f32),
            V((D, TOK), f32),
            V((D, TOK), f32),
            V((2, TOK, FF), bf16),
            V((2, D, TOK), bf16),
            V((TOK, FF), f32),
            V((TOK, FF), bf16),
            V((D, TOK), bf16),
            V((16, RB, FF), bf16),
            V((2, 16, RB, D), bf16),
            V((16, RB, D), bf16),
            V((C, LEN), bf16),
            V((4, C, TOK), bf16),
            V((TOK, D), bf16),
            V((D, TOK), bf16),
            V((3 * C, LEN), bf16),
            V((3, C, LEN), bf16),
            V((C, LEN), f32),
            V((3, C, LEN), bf16),
            V((4, RB, FF), bf16),
            V((2, 4, RB, FF), bf16),
            V((4, RB, FF), bf16),
            V((3, RB, FF), bf16),
            V((RB, FF), bf16),
            V((3, RB, D), bf16),
            V((4, RB, D), bf16),
            V((2, 4, RB, D), bf16),
            V((4, RB, D), bf16),
            V((3, RB, D), bf16),
            V((4, RB, C), bf16),
            V((3, RB, C), bf16),
            V((2, RB, D), f32),
            V((2, RB, D), f32),
            V((2, RB, C), f32),
            V((D, 128), f32),
            V((16, D), f32),
            V((10, 16, D), f32),
            V((2, RB, D), bf16),
            pltpu.SemaphoreType.DMA((12,)),
            pltpu.SemaphoreType.DMA((N_SEM,)),
            pltpu.SemaphoreType.DMA((N_SEM,)),
        ],
        compiler_params=pltpu.CompilerParams(
            collective_id=0, has_side_effects=True, vmem_limit_bytes=62 * 2**20
        ),
    )(
        inputs, teacher, lengths, query_weight, key_weight, value_weight, output_weight,
        up_weight, down_weight, *vectors,
    )
    vector = sds((1, C), f32)
    weight = sds((RB, C), f32)
    wide = sds((RB, D), f32)
    done = pl.pallas_call(
        finish,
        name="finish",
        out_shape=(
            sds((C, LEN), bf16), sds((1, 1), f32), sds((C, LEN), f32),
            weight, vector, weight, weight, vector, sds((C, RB), f32),
            vector, vector, vector, wide, sds((1, D), f32), wide, vector, vector, vector,
        ),
        in_specs=[anyspec] + [vm] * 5,
        out_specs=(anyspec,) + (vm,) * 17,
        scratch_shapes=[pltpu.SemaphoreType.DMA],
    )(*got)
    shapes = [
        (C, LEN), (), (C, LEN), (RB, C), (C,), (RB, C), (RB, C), (C,), (C, RB), (C,), (C,), (C,),
        (RB, D), (D,), (RB, D), (C,), (C,), (C,),
    ]
    return tuple(o.reshape(shape) for o, shape in zip(done, shapes))


def solution(mesh):
    split = Mesh(
        mesh.devices.reshape(mesh.shape["dp"], 4, 4, mesh.shape["col"]), AXES
    )
    tokens = P("col", DP_ROW)
    weight = P(ROW, "col")
    vector = P("col")
    return jax.shard_map(
        local_step,
        mesh=split,
        in_specs=(
            tokens, tokens, P(DP_ROW), weight, vector, weight, weight, vector,
            P("col", ROW), vector, vector, vector, weight, vector, weight,
            vector, vector, vector,
        ),
        out_specs=(
            tokens, P(), tokens, weight, vector, weight, weight, vector,
            P("col", ROW), vector, vector, vector, weight, vector, weight,
            vector, vector, vector,
        ),
        check_vma=False,
    )
```

```python
import jax
import jax.numpy as jnp
from jax import lax
from jax.experimental import pallas as pl
from jax.experimental.pallas import tpu as pltpu
from jax.sharding import Mesh
from jax.sharding import PartitionSpec as P

D = 768
FF = 3072
LEN = 1024
HD = 64
HEADS = 3
C = 192
TOK = 256
RB = 48
SLOTS = 32768
EPS = 1e-12
MASK = -1e30
ROOT_HALF = 0.7071067811865476
INV_ROOT_TAU = 0.3989422804014327
AXES = ("dp", "row_0", "row_1", "col")
ROW = ("row_0", "row_1")
DP_ROW = ("dp", "row_0", "row_1")
N_SEM = 256
QH = 288
HW = 384
f32 = jnp.float32
bf16 = jnp.bfloat16


def mm(a, b):
    return lax.dot_general(a, b, (((1,), (0,)), ((), ())), preferred_element_type=f32)


def mt(a, b):
    return lax.dot_general(a, b, (((1,), (1,)), ((), ())), preferred_element_type=f32)


def transposed(a):
    return jnp.transpose(a, (1, 0))


class Sent:
    def __init__(self, copy):
        self.copy, self.open_send, self.open_recv = copy, True, True

    def wait_send(self):
        if self.open_send:
            self.copy.wait_send()
        self.open_send = False

    def wait_recv(self):
        if self.open_recv:
            self.copy.wait_recv()
        self.open_recv = False

    def wait(self):
        self.wait_send()
        self.wait_recv()


class Links:
    def __init__(self, ssem, rsem):
        self.ssem, self.rsem, self.n, self.all = ssem, rsem, 0, []

    def send(self, src, dst, dev):
        copy = pltpu.make_async_remote_copy(
            src_ref=src,
            dst_ref=dst,
            send_sem=self.ssem.at[self.n],
            recv_sem=self.rsem.at[self.n],
            device_id=dev,
            device_id_type=pl.DeviceIdType.MESH,
        )
        copy.start()
        self.n += 1
        self.all.append(Sent(copy))
        return self.all[-1]


def layer(
    x_in, t_in, len_in, wq_in, wk_in, wv_in, wo_in, up_in, down_in,
    ob_in, g1_in, b1_in, db_in, g2_in, b2_in, qb_in, vb_in, ub_in,
    out_o, gi_o, dw2_o, dwo_o, dqkv_o, sv_o,
    xf, tf, w2, wq2, wo2, wo4, wqkvt, wqkv, vec, ub, vcol, qkvt, ktm, qaug, vaug, vtm, pst, linv,
    ctxt, ctxa, hid, nrm, sg, bstore, astore, slope, brecv, arecv,
    g2, gaq, gqr, gao, gor, dctx, dct, outt, delta,
    dqkvt, dxp, rxi, rx, im, rm, s1, r2, s2, r3, iq, rq, sq1, rq2, io, ro, so1, ro2, so2, so4, ro3,
    x1, xq1, gcol, sv, rsv, wown,
    lsem, ssem, rsem,
):
    d = lax.axis_index("dp")
    y = lax.axis_index("row_0")
    x = lax.axis_index("row_1")
    c = lax.axis_index("col")
    e = 1 - d
    r = 4 * y + x
    a_me = x * e + y * d
    b_me = y * e + x * d
    b_left = lax.rem(b_me + 3, 4)
    b_right = lax.rem(b_me + 1, 4)
    b_far = lax.rem(b_me + 2, 4)

    def ridx(a, b):
        return (4 * b + a) * e + (4 * a + b) * d

    def zdev(k):
        return {"col": lax.rem(c + k, 4)}

    def adev(k):
        return {"row_0": lax.rem(y + k * d, 4), "row_1": lax.rem(x + k * e, 4)}

    def bdev(k):
        return {"row_0": lax.rem(y + k * e, 4), "row_1": lax.rem(x + k * d, 4)}

    sib = {"dp": e}
    links = Links(ssem, rsem)

    def wait_all(copies):
        for copy in copies:
            copy.wait_recv()

    n_local = [0]

    def local(src, dst):
        copy = pltpu.make_async_copy(src, dst, lsem.at[n_local[0]])
        copy.start()
        n_local[0] += 1
        return copy

    xrows = pl.ds(pl.multiple_of(c * C, 16), C)
    tcols = pl.ds(pl.multiple_of(c * TOK, 128), TOK)
    own_cols = pl.ds(pl.multiple_of(c * D, 128), D)
    bar = pltpu.get_barrier_semaphore()
    for k in (1, 2, 3):
        for dev in (zdev(k), adev(k), bdev(k)):
            pl.semaphore_signal(bar, inc=1, device_id=dev, device_id_type=pl.DeviceIdType.MESH)
    pl.semaphore_signal(bar, inc=1, device_id=sib, device_id_type=pl.DeviceIdType.MESH)
    cup = local(up_in, wown.at[0])
    cdn = local(down_in, wown.at[1])
    cx = local(x_in, xf.at[xrows])
    ct = local(t_in.at[:, tcols], tf.at[c])
    wo4[c] = wo_in[...]
    for i, ref in enumerate((ob_in, g1_in, b1_in, db_in, g2_in, b2_in, qb_in, vb_in)):
        vec[c, i : i + 1, :] = ref[...].reshape(1, C)
    ub[c, 0:1, :] = jnp.concatenate([ub_in[i : i + 1] for i in range(6)], axis=1)
    own_qkv = jnp.concatenate([wq_in[...], wk_in[...], wv_in[...]], axis=1)
    own_qkv = jnp.where(d == 0, own_qkv[:, 0:QH], own_qkv[:, QH:])
    wq2[d, r] = jnp.concatenate([own_qkv, jnp.zeros((RB, HW - QH), bf16)], axis=1)
    cup.wait()
    cdn.wait()
    pl.semaphore_wait(bar, 10)

    def along_a(buf):
        return [links.send(buf.at[d, r], buf.at[d, r], adev(k)) for k in (1, 3, 2)]

    def block(k, b):
        return ridx(lax.rem(a_me + 4 - k, 4), b)

    def along_b(buf, k):
        ref = buf.at[d, block(k, b_me)]
        return (links.send(ref, ref, bdev(1)), links.send(ref, ref, bdev(3)))

    def to_sibling(buf, k, b):
        ref = buf.at[d, block(k, b)]
        return links.send(ref, ref, sib)

    FWD_PLUS, FWD_MINUS = (0, 2), (1, 3)

    def forward(buf, sent):
        far = {}
        for k in FWD_PLUS:
            sent[k][0].wait_recv()
            ref = buf.at[d, block(k, b_left)]
            far[k] = links.send(ref, ref, bdev(1))
        for k in FWD_MINUS:
            sent[k][1].wait_recv()
            ref = buf.at[d, block(k, b_right)]
            far[k] = links.send(ref, ref, bdev(3))
        return far

    wq_a = along_a(wq2)
    wq_b = {0: along_b(wq2, 0)}

    oz = [links.send(wo4.at[c], wo4.at[c], zdev(k)) for k in (1, 3, 2)]
    wz = [links.send(wown.at[d], w2.at[d, r, :, own_cols], zdev(k)) for k in (1, 3, 2)]
    vz = [links.send(vec.at[c], vec.at[c], zdev(k)) for k in (1, 2, 3)]
    uz = [links.send(ub.at[c], ub.at[c], zdev(k)) for k in (1, 2, 3)]
    w2[d, r, :, own_cols] = wown[d]

    def xhalf(i, top):
        return xf.at[pl.ds(pl.multiple_of(i * C + (0 if top else C // 2), 16), C // 2)]

    cx.wait()
    xs = {}
    for k, order in ((1, (True, False)), (3, (False, True))):
        for top in order:
            xs[k, top] = links.send(xhalf(c, top), xhalf(c, top), zdev(k))

    wait_all(wq_a)
    for k in (1, 3, 2):
        wq_b[k] = along_b(wq2, k)
    wait_all(wz)
    w_a = along_a(w2)
    wq_s = [to_sibling(wq2, k, b_me) for k in range(4)]
    wait_all(oz)
    own_wo = jnp.concatenate([wo4[j] for j in range(4)], axis=1)
    wo2[d, r] = jnp.where(d == 0, own_wo[:, 0:HW], own_wo[:, HW:])
    wo_a = along_a(wo2)
    wq_far = forward(wq2, wq_b)
    xs[1, True].wait_recv()
    left = lax.rem(c + 3, 4)
    xs["f", 1] = links.send(xhalf(left, True), xhalf(left, True), zdev(1))
    xs[3, False].wait_recv()
    right = lax.rem(c + 1, 4)
    xs["f", 3] = links.send(xhalf(right, False), xhalf(right, False), zdev(3))
    w_b = {0: along_b(w2, 0)}
    wo_b = {0: along_b(wo2, 0)}
    for k in range(4):
        wq_b[k][0].wait_recv()
        wq_s.append(to_sibling(wq2, k, b_left))
        wq_b[k][1].wait_recv()
        wq_s.append(to_sibling(wq2, k, b_right))
    w_s = [to_sibling(w2, 0, b_me)]
    for i, k in enumerate((1, 3, 2)):
        w_a[i].wait_recv()
        w_b[k] = along_b(w2, k)
        w_s.append(to_sibling(w2, k, b_me))
    for k in range(4):
        wq_far[k].wait_recv()
        wq_s.append(to_sibling(wq2, k, b_far))
    wait_all(wo_a)
    for k in (1, 3, 2):
        wo_b[k] = along_b(wo2, k)
    wo_s = [to_sibling(wo2, k, b_me) for k in range(4)]

    wait_all(vz + uz)
    for i in range(4):
        vcol[i * C : (i + 1) * C, 0:16] = transposed(vec[i])
    vown = transposed(vec[c])
    length = len_in[0]

    wait_all([xs[key] for key in ((1, False), (3, True), ("f", 1), ("f", 3))])
    wait_all(wq_s)
    for i in range(2):
        wqkvt[i * QH : (i + 1) * QH] = transposed(wq2[i].reshape(D, HW))[0:QH]
    q_bias = vown[:, 6:7]
    v_bias = vown[:, 7:8]
    lane_iota = lax.broadcasted_iota(jnp.int32, (1, TOK), 1)
    first_row = lax.broadcasted_iota(jnp.int32, (HD, TOK), 0) == 0

    def qkv_chunk(i, carry):
        cols = pl.ds(pl.multiple_of(i * TOK, 128), TOK)
        tok = xf[:, cols]
        qkv = mm(wqkvt[...], tok)
        q = (qkv[0:C] + q_bias).astype(bf16)
        k = qkv[C : 2 * C].astype(bf16)
        v = (qkv[2 * C :] + v_bias).astype(bf16)
        q = (q.astype(f32) * (HD**-0.5)).astype(bf16)
        qkvt[0:C, cols] = q
        qkvt[C : 2 * C, cols] = k
        bias = jnp.where(lane_iota + i * TOK < length, 0.0, MASK)
        bias = jnp.where(first_row, jnp.broadcast_to(bias, (HD, TOK)), 0.0).astype(bf16)
        ones = jnp.where(first_row, 1.0, 0.0).astype(bf16)
        for h in range(HEADS):
            hs = slice(h * HD, (h + 1) * HD)
            qaug[h, 0:HD, cols] = q[hs]
            qaug[h, HD : 2 * HD, cols] = ones
            vaug[h, 0:HD, cols] = v[hs]
            vaug[h, HD : HD + 16, cols] = ones[0:16]
            ktm[h, cols, :] = transposed(jnp.concatenate([k[hs], bias], axis=0))
            vtm[h, cols, :] = transposed(jnp.concatenate([v[hs], ones], axis=0))
        return carry

    lax.fori_loop(0, 4, qkv_chunk, 0)
    ct.wait()
    tt = []
    for k in (1, 3, 2):
        there = pl.ds(pl.multiple_of(lax.rem(c + k, 4) * TOK, 128), TOK)
        tt.append(links.send(t_in.at[:, there], tf.at[c], zdev(k)))

    def fwd_head(h):
        def fwd_tile(n, carry):
            cols = pl.ds(pl.multiple_of(n * TOK, 128), TOK)
            score = mm(ktm[h], qaug[h, :, cols])
            top = jnp.max(score, axis=0, keepdims=True)
            probs = jnp.exp(score - top).astype(bf16)
            pst[h, :, cols] = probs
            both = mm(vaug[h], probs)
            inv = 1.0 / both[HD : HD + 1]
            linv[h, 0:1, cols] = inv
            ctxt[pl.ds(pl.multiple_of(h * HD, 16), HD), cols] = (both[0:HD] * inv).astype(bf16)
            return carry

        lax.fori_loop(0, 4, fwd_tile, 0)

    def fwd_heads(lo, hi):
        lax.fori_loop(lo, hi, lambda h, carry: (fwd_head(h), carry)[1], 0)

    cc = []

    def context_out(h):
        hrow = pl.ds(h * HD, HD)
        ctxa[c, hrow] = ctxt[hrow, tcols]
        for k in (1, 3, 2):
            there = pl.ds(pl.multiple_of(lax.rem(c + k, 4) * TOK, 128), TOK)
            cc.append(links.send(ctxt.at[hrow, there], ctxa.at[c, hrow], zdev(k)))

    fwd_heads(0, 1)
    context_out(0)
    w_far = forward(w2, w_b)
    wo_far = forward(wo2, wo_b)
    fwd_heads(1, 2)
    context_out(1)
    for k in range(4):
        w_b[k][0].wait_recv()
        w_s.append(to_sibling(w2, k, b_left))
        w_b[k][1].wait_recv()
        w_s.append(to_sibling(w2, k, b_right))
    for k in range(4):
        wo_b[k][0].wait_recv()
        wo_s.append(to_sibling(wo2, k, b_left))
        wo_b[k][1].wait_recv()
        wo_s.append(to_sibling(wo2, k, b_right))
    fwd_heads(2, 3)
    context_out(2)
    for i in range(2):
        wqkv[:, i * QH : (i + 1) * QH] = wq2[i].reshape(D, HW)[:, 0:QH]
    for k in range(4):
        wo_far[k].wait_recv()
        wo_s.append(to_sibling(wo2, k, b_far))
    wait_all(cc)
    wait_all(wo_s)

    def proj(i, carry):
        row = pl.ds(pl.multiple_of(i * C, 16), C)
        acc = xf[row, tcols].astype(f32) + vcol[row, 0:1]
        for j in range(2):
            w = wo2[j, pl.ds(i * 4, 4)].reshape(C, HW)
            acc = acc + mm(w, ctxa[2 * j : 2 * j + 2].reshape(HW, TOK))
        hid[row] = acc
        return carry

    lax.fori_loop(0, 4, proj, 0)

    def norm_stats(ref):
        v = ref[...]
        mean = jnp.sum(v, axis=0, keepdims=True) * (1.0 / D)
        square = jnp.sum(v * v, axis=0, keepdims=True) * (1.0 / D)
        return mean, lax.rsqrt(square - mean * mean + EPS)

    mean1, inv1 = norm_stats(hid)

    def norm1(i, carry):
        row = pl.ds(pl.multiple_of(i * C, 16), C)
        n = (hid[row] - mean1) * inv1
        nrm[row] = n
        h = n * vcol[row, 1:2] + vcol[row, 2:3]
        hid[row] = h
        astore[0, row] = h.astype(bf16)
        return carry

    lax.fori_loop(0, 4, norm1, 0)
    outt[...] = transposed(astore[0])
    for k in range(4):
        w_far[k].wait_recv()
        w_s.append(to_sibling(w2, k, b_far))

    wait_all(w_s)

    def up_chunk(i, carry):
        cols = pl.ds(pl.multiple_of(i * D, 128), D)
        pre = mm(outt[...], w2[0, :, :, cols].reshape(D, D)) + ub[i, 0:1]
        half = 0.5 * (1.0 + lax.erf(pre * ROOT_HALF))
        bstore[1, :, cols] = (pre * half).astype(bf16)
        slope[:, cols] = half + pre * jnp.exp(-0.5 * pre * pre) * INV_ROOT_TAU
        return carry

    lax.fori_loop(0, 4, up_chunk, 0)

    def down_chunk(i, carry):
        row = pl.ds(pl.multiple_of(i * C, 16), C)
        w = w2[1, pl.ds(i * 4, 4)].reshape(C, FF)
        hid[row] = hid[row] + mt(w, bstore[1]) + vcol[row, 3:4]
        return carry

    lax.fori_loop(0, 4, down_chunk, 0)

    mean2, inv2 = norm_stats(hid)
    wait_all(tt)
    valid = lane_iota + c * TOK < length
    gcol[...] = jnp.zeros(gcol.shape, f32)

    def norm2(i, carry):
        total, crossed, loss = carry
        row = pl.ds(pl.multiple_of(i * C, 16), C)
        n = (hid[row] - mean2) * inv2
        hid[row] = n
        final = n * vcol[row, 4:5] + vcol[row, 5:6]
        delta[row] = final.astype(bf16)
        g = jnp.where(valid, final - tf[i].astype(f32), 0.0)
        gcol[row, 4:5] = jnp.sum(g * n, axis=1, keepdims=True)
        gcol[row, 5:6] = jnp.sum(g, axis=1, keepdims=True)
        s = g * vcol[row, 4:5]
        sg[row] = s
        return (
            total + jnp.sum(s, axis=0, keepdims=True),
            crossed + jnp.sum(s * n, axis=0, keepdims=True),
            loss + jnp.sum(g * g, axis=0, keepdims=True),
        )

    zero = jnp.zeros((1, TOK), f32)
    total2, crossed2, loss_row = lax.fori_loop(0, 4, norm2, (zero, zero, zero))
    fo = []
    out_o_own = local(delta.at[xrows], out_o.at[:, tcols])
    for k in (1, 3, 2):
        there = pl.ds(pl.multiple_of(lax.rem(c + k, 4) * C, 16), C)
        fo.append(links.send(delta.at[there], out_o.at[:, tcols], zdev(k)))

    def norm2_back(i, carry):
        row = pl.ds(pl.multiple_of(i * C, 16), C)
        s = inv2 * (sg[row] - total2 * (1.0 / D) - hid[row] * (crossed2 * (1.0 / D)))
        sg[row] = s
        low = s.astype(bf16)
        astore[1, row] = low
        gcol[row, 3:4] = jnp.sum(low.astype(f32), axis=1, keepdims=True)
        return carry

    lax.fori_loop(0, 4, norm2_back, 0)
    outt[...] = transposed(astore[1])

    def act_chunk(i, carry):
        cols = pl.ds(pl.multiple_of(i * D, 128), D)
        g = mm(outt[...], w2[1, :, :, cols].reshape(D, D)) * slope[:, cols]
        low = g.astype(bf16)
        bstore[0, :, cols] = low
        sv[pl.ds(8 + i, 1)] = jnp.sum(low.astype(f32), axis=0, keepdims=True)
        return carry

    lax.fori_loop(0, 4, act_chunk, 0)
    ex = [
        links.send(astore.at[e], arecv, sib),
        links.send(bstore.at[e], brecv, sib),
    ]

    def hidden_back(i, carry):
        total, crossed = carry
        row = pl.ds(pl.multiple_of(i * C, 16), C)
        w = w2[0, pl.ds(i * 4, 4)].reshape(C, FF)
        g = sg[row] + mt(w, bstore[0])
        n = nrm[row]
        gcol[row, 1:2] = jnp.sum(g * n, axis=1, keepdims=True)
        gcol[row, 2:3] = jnp.sum(g, axis=1, keepdims=True)
        s = g * vcol[row, 1:2]
        sg[row] = s
        return (
            total + jnp.sum(s, axis=0, keepdims=True),
            crossed + jnp.sum(s * n, axis=0, keepdims=True),
        )

    total1, crossed1 = lax.fori_loop(0, 4, hidden_back, (zero, zero))

    def norm1_back(i, carry):
        row = pl.ds(pl.multiple_of(i * C, 16), C)
        s = inv1 * (sg[row] - total1 * (1.0 / D) - nrm[row] * (crossed1 * (1.0 / D)))
        sg[row] = s
        low = s.astype(bf16)
        delta[row] = low
        gcol[row, 0:1] = jnp.sum(low.astype(f32), axis=1, keepdims=True)
        return carry

    for copy in fo:
        copy.wait_send()
    out_o_own.wait()
    lax.fori_loop(0, 4, norm1_back, 0)
    outt[...] = transposed(delta[...])

    dc = []
    for i in range(2):
        part = transposed(mm(outt[...], wo2[i].reshape(D, HW)).astype(bf16))
        dct[2 * i : 2 * i + 2] = part.reshape(2, C, TOK)
    dctx[:, tcols] = dct[c]
    for h in range(HEADS):
        hrow = pl.ds(h * HD, HD)
        dc.append(
            [
                links.send(dct.at[lax.rem(c + k, 4), hrow], dctx.at[hrow, tcols], zdev(k))
                for k in (1, 3, 2)
            ]
        )
    g = mt(delta[...], ctxa[...].reshape(D, TOK)).astype(bf16)
    for i in range(2):
        gao[i] = g[:, i * HW : (i + 1) * HW].reshape(16, RB, HW)
    go_x = links.send(gao.at[e], gor, sib)

    sv[0:8] = transposed(gcol[...])[0:8]
    sv[6:7] = jnp.broadcast_to(jnp.sum(loss_row, axis=1, keepdims=True), (1, D))
    sv[7:8] = jnp.broadcast_to(length.astype(f32), (1, D))
    sv[12:16] = jnp.zeros((4, D), f32)
    n_sv = [1]
    v_sent = [links.send(sv, rsv.at[0], sib)]

    def sv_add():
        got = []
        for copy in v_sent:
            copy.wait()
        lo = n_sv[0] - len(v_sent)
        total = sv[...]
        for i in range(len(v_sent)):
            total = total + rsv[lo + i]
        sv[...] = total
        v_sent.clear()

    def sv_send(dev):
        for k in (1, 3, 2):
            v_sent.append(links.send(sv, rsv.at[n_sv[0]], dev(k)))
            n_sv[0] += 1

    wait_all(ex)

    def g2_block(i, carry):
        for j in range(4):
            cols = slice(j * D, (j + 1) * D)
            row = pl.ds(pl.multiple_of(i * C, 16), C)
            g = mm(astore[d, row], bstore[d, :, cols]) + mm(arecv[row], brecv[:, cols])
            g2[pl.ds(i * 4, 4), :, cols] = g.astype(bf16).reshape(4, RB, D)
        return carry

    lax.fori_loop(0, 4, g2_block, 0)
    sv_add()
    sv_send(bdev)

    VIA_PLUS, VIA_MINUS = (0, 1), (2, 3)

    def sum_start(own, mid, recv):
        m = {}
        for j in VIA_PLUS:
            m[j] = links.send(own(ridx(j, b_far)), mid.at[j], bdev(1))
        for j in VIA_MINUS:
            m[j] = links.send(own(ridx(j, b_far)), mid.at[j], bdev(3))
        got = {}
        for j in VIA_MINUS:
            got[0, j] = links.send(own(ridx(j, b_right)), recv.at[0, j], bdev(1))
        for j in VIA_PLUS:
            got[1, j] = links.send(own(ridx(j, b_left)), recv.at[1, j], bdev(3))
        return m, got

    def sum_mid(own, mid, recv, m, got):
        for j in VIA_PLUS:
            m[j].wait_recv()
            mid[j] = (own(ridx(j, b_right))[...].astype(f32) + mid[j].astype(f32)).astype(bf16)
            got[0, j] = links.send(mid.at[j], recv.at[0, j], bdev(1))
        for j in VIA_MINUS:
            m[j].wait_recv()
            mid[j] = (own(ridx(j, b_left))[...].astype(f32) + mid[j].astype(f32)).astype(bf16)
            got[1, j] = links.send(mid.at[j], recv.at[1, j], bdev(3))

    def sum_end(own, recv, got, summed, peer_recv):
        for j in range(4):
            got[0, j].wait_recv()
            got[1, j].wait_recv()
            total = own(ridx(j, b_me))[...].astype(f32)
            total = total + recv[0, j].astype(f32) + recv[1, j].astype(f32)
            summed[j] = total.astype(bf16)
        return [
            links.send(summed.at[lax.rem(a_me + k, 4)], peer_recv.at[k - 1], adev(k))
            for k in (1, 3, 2)
        ]

    def sum_a(sends, summed, recv):
        wait_all(sends)
        total = summed[a_me].astype(f32)
        for k in range(3):
            total = total + recv[k].astype(f32)
        return total

    def own_w(i):
        return g2.at[i]

    def own_q(i):
        return gaq.at[d, i]

    def own_o(i):
        return gao.at[d, i]

    def add_sibling(ref, other):
        def add(i, carry):
            ref[d, i] = (ref[d, i].astype(f32) + other[i].astype(f32)).astype(bf16)
            return carry

        lax.fori_loop(0, 16, add, 0)

    w_mid, w_got = sum_start(own_w, im, rm)

    wait_all(dc[0])

    def bwd_head(h, carry):
        hrow = pl.ds(pl.multiple_of(h * HD, 16), HD)
        krow = pl.ds(pl.multiple_of(C + h * HD, 16), HD)
        vrow = pl.ds(pl.multiple_of(2 * C + h * HD, 16), HD)

        def bwd_tile(n, acc):
            dk, dv = acc
            cols = pl.ds(pl.multiple_of(n * TOK, 128), TOK)
            inv = linv[h, 0:1, cols]
            dc = dctx[hrow, cols].astype(f32)
            inner = jnp.sum(dc * ctxt[hrow, cols].astype(f32), axis=0, keepdims=True) * inv
            dcs = (dc * inv).astype(bf16)
            probs = pst[h, :, cols]
            dp = mm(vtm[h, :, 0:HD], dcs) - inner
            ds = (probs.astype(f32) * dp).astype(bf16)
            dqkvt[hrow, cols] = (mm(qkvt[krow, :], ds) * (HD**-0.5)).astype(bf16)
            dk = dk + mt(qkvt[hrow, cols], ds)
            dv = dv + mt(dcs, probs)
            return dk, dv

        dk, dv = lax.fori_loop(
            0, 4, bwd_tile, (jnp.zeros((HD, LEN), f32), jnp.zeros((HD, LEN), f32))
        )
        dqkvt[krow] = dk.astype(bf16)
        dqkvt[vrow] = dv.astype(bf16)
        return carry

    lax.fori_loop(0, 1, bwd_head, 0)
    sv_add()
    sv_send(adev)
    go_x.wait_recv()
    add_sibling(gao, gor)
    o_mid, o_got = sum_start(own_o, io, ro)
    wait_all(dc[1])
    lax.fori_loop(1, 2, bwd_head, 0)
    sum_mid(own_w, im, rm, w_mid, w_got)
    sv_add()
    sv_send(zdev)
    wait_all(dc[2])
    lax.fori_loop(2, 3, bwd_head, 0)
    sum_mid(own_o, io, ro, o_mid, o_got)

    ones = jnp.ones((8, LEN), bf16)
    bias_sum = mt(ones, dqkvt[...])[0:1]
    spare = HW - QH
    row_iota = lax.broadcasted_iota(jnp.int32, (RB, spare), 0)
    bias_rows = []
    for i in range(2):
        rows = jnp.zeros((RB, spare), f32)
        for j in range(3):
            at = i * QH + j * spare
            part = jnp.broadcast_to(bias_sum[:, at : at + spare], (RB, spare))
            rows = jnp.where(row_iota == j, part, rows)
        bias_rows.append(jnp.broadcast_to(rows.astype(bf16)[None], (4, RB, spare)))

    def dqkv_block(n, carry):
        row = pl.ds(pl.multiple_of(n * C, 16), C)
        blocks = pl.ds(n * 4, 4)
        for i in range(2):
            g = mt(xf[row], dqkvt[i * QH : (i + 1) * QH])
            gaq[i, blocks, :, 0:QH] = g.astype(bf16).reshape(4, RB, QH)
            gaq[i, blocks, :, QH:] = bias_rows[i]
        return carry

    lax.fori_loop(0, 4, dqkv_block, 0)
    gx = links.send(gaq.at[e], gqr, sib)

    def dx_part(i):
        row = pl.ds(pl.multiple_of(i * C, 16), C)
        gi_o[...] = mm(wqkv[row], dqkvt[...])
        gi_o[:, tcols] = gi_o[:, tcols] + sg[row]

    H2 = C // 2
    top, bottom = pl.ds(0, H2), pl.ds(H2, H2)
    dx_part(lax.rem(c + 2, 4))
    dxp[0] = gi_o[...].astype(bf16)
    x_mid = [
        links.send(dxp.at[0, top], rxi.at[0], zdev(1)),
        links.send(dxp.at[0, bottom], rxi.at[1], zdev(3)),
    ]
    dx_part(right)
    dxp[1] = gi_o[...].astype(bf16)
    x_got = [links.send(dxp.at[1, bottom], rx.at[0, bottom], zdev(1))]
    dx_part(left)
    dxp[2] = gi_o[...].astype(bf16)
    x_got.append(links.send(dxp.at[2, top], rx.at[1, top], zdev(3)))
    dx_part(c)

    gx.wait_recv()
    add_sibling(gaq, gqr)
    q_mid, q_got = sum_start(own_q, iq, rq)
    x_mid[0].wait_recv()
    dxp[1, top] = (dxp[1, top].astype(f32) + rxi[0].astype(f32)).astype(bf16)
    x_got.append(links.send(dxp.at[1, top], rx.at[0, top], zdev(1)))
    x_mid[1].wait_recv()
    dxp[2, bottom] = (dxp[2, bottom].astype(f32) + rxi[1].astype(f32)).astype(bf16)
    x_got.append(links.send(dxp.at[2, bottom], rx.at[1, bottom], zdev(3)))
    w_sum = sum_end(own_w, rm, w_got, s1, r2)
    o_sum = sum_end(own_o, ro, o_got, so1, ro2)
    sv_add()
    sv_o[...] = sv[...]
    sum_mid(own_q, iq, rq, q_mid, q_got)
    so2[0] = sum_a(o_sum, so1, ro2).astype(bf16)
    o_x = links.send(so2.at[0], so2.at[1], sib)
    s2[...] = sum_a(w_sum, s1, r2).astype(bf16)
    w3 = []
    for k in (1, 3, 2):
        there = pl.ds(pl.multiple_of(lax.rem(c + k, 4) * D, 128), D)
        w3.append(links.send(s2.at[:, there], r3.at[k - 1], zdev(k)))
    o_x.wait_recv()
    mine, other = so2[0], so2[1]
    low, high = jnp.where(d == 0, mine, other), jnp.where(d == 0, other, mine)
    so4[0], so4[1] = low[:, 0:C], low[:, C:]
    so4[2], so4[3] = high[:, 0:C], high[:, C:]
    o3 = [links.send(so4.at[lax.rem(c + k, 4)], ro3.at[k - 1], zdev(k)) for k in (1, 3, 2)]
    q_sum = sum_end(own_q, rq, q_got, sq1, rq2)
    wait_all(x_got)
    gi_o[...] = gi_o[...] + rx[0].astype(f32) + rx[1].astype(f32)
    dqkv = sum_a(q_sum, sq1, rq2)
    xq1[0] = dqkv
    q3 = links.send(xq1.at[0], xq1.at[1], sib)
    wait_all(w3)
    total = s2[:, own_cols].astype(f32)
    for k in range(3):
        total = total + r3[k].astype(f32)
    x1[0] = total
    w4 = links.send(x1.at[0], x1.at[1], sib)
    wait_all(o3)
    ototal = so4[c].astype(f32)
    for k in range(3):
        ototal = ototal + ro3[k].astype(f32)
    dwo_o[...] = ototal
    q3.wait_recv()
    dqkv_o[d] = dqkv
    dqkv_o[e] = xq1[1]
    w4.wait_recv()
    dw2_o[d] = total
    dw2_o[e] = x1[1]
    for copy in links.all:
        copy.wait()


def finish(
    out_i, gi_i, dw2_i, dwo_i, dqkv_i, sv_i,
    out, loss, gi, gwq, gbq, gwk, gwv, gbv, gwo, gob, gg1, gb1, gup, gub, gdn, gdb, gg2, gb2,
):
    c = lax.axis_index("col")
    out[...] = out_i[...]
    count = sv_i[7:8, 0:1] * 0.25
    factor = SLOTS / count
    loss[0] = jnp.sum(sv_i[6:7, 0:1] / (2.0 * D * count))
    gi[...] = gi_i[...] * factor
    low, high = dqkv_i[0] * factor, dqkv_i[1] * factor
    gwq[...] = low[:, 0:C]
    gwk[...] = jnp.concatenate([low[:, C:QH], high[:, 0 : QH - C]], axis=1)
    gwv[...] = high[:, QH - C : QH]
    gbq[...] = jnp.concatenate([low[0:1, QH:], low[1:2, QH:]], axis=1)
    gbv[...] = jnp.concatenate([high[1:2, QH:], high[2:3, QH:]], axis=1)
    gwo[...] = dwo_i[...] * factor
    gup[...] = dw2_i[0] * factor
    gdn[...] = dw2_i[1] * factor
    sums = sv_i[...] * factor
    for j in range(4):

        @pl.when(c == j)
        def _(j=j):
            for i in range(6):
                gub[i : i + 1] = sums[8 + j : 9 + j, i * 128 : (i + 1) * 128]
            for i, ref in enumerate((gob, gg1, gb1, gdb, gg2, gb2)):
                ref[...] = sums[i : i + 1, j * C : (j + 1) * C]


def local_step(
    inputs, teacher, lengths, query_weight, query_bias, key_weight, value_weight, value_bias,
    output_weight, output_bias, first_gain, first_shift, up_weight, up_bias, down_weight,
    down_bias, second_gain, second_shift,
):
    anyspec = pl.BlockSpec(memory_space=pl.ANY)
    vm = pl.BlockSpec(memory_space=pltpu.VMEM)
    sds = jax.ShapeDtypeStruct
    V = pltpu.VMEM
    vectors = [
        v.reshape(1, -1)
        for v in (
            output_bias, first_gain, first_shift, down_bias, second_gain, second_shift,
            query_bias, value_bias,
        )
    ]
    vectors.append(up_bias.reshape(6, 128))
    got = pl.pallas_call(
        layer,
        name="layer",
        out_shape=(
            sds((C, LEN), bf16),
            sds((C, LEN), f32),
            sds((2, RB, D), f32),
            sds((RB, C), f32),
            sds((2, RB, HW), f32),
            sds((16, D), f32),
        ),
        in_specs=[anyspec, anyspec, pl.BlockSpec(memory_space=pltpu.SMEM)]
        + [vm] * 4
        + [anyspec] * 2
        + [vm] * 9,
        out_specs=(anyspec, vm, vm, vm, vm, vm),
        scratch_shapes=[
            V((D, LEN), bf16),
            V((4, C, TOK), bf16),
            V((2, 16, RB, FF), bf16),
            V((2, 16, RB, HW), bf16),
            V((2, 16, RB, HW), bf16),
            V((4, RB, C), bf16),
            V((3 * C, D), bf16),
            V((D, 3 * C), bf16),
            V((4, 16, C), f32),
            V((4, 8, D), f32),
            V((D, 128), f32),
            V((2 * C, LEN), bf16),
            V((HEADS, LEN, 2 * HD), bf16),
            V((HEADS, 2 * HD, LEN), bf16),
            V((HEADS, HD + 16, LEN), bf16),
            V((HEADS, LEN, 2 * HD), bf16),
            V((HEADS, LEN, LEN), bf16),
            V((HEADS, 8, LEN), f32),
            V((C, LEN), bf16),
            V((4, C, TOK), bf16),
            V((D, TOK), f32),
            V((D, TOK), f32),
            V((D, TOK), f32),
            V((2, TOK, FF), bf16),
            V((2, D, TOK), bf16),
            V((TOK, FF), f32),
            V((TOK, FF), bf16),
            V((D, TOK), bf16),
            V((16, RB, FF), bf16),
            V((2, 16, RB, HW), bf16),
            V((16, RB, HW), bf16),
            V((2, 16, RB, HW), bf16),
            V((16, RB, HW), bf16),
            V((C, LEN), bf16),
            V((4, C, TOK), bf16),
            V((TOK, D), bf16),
            V((D, TOK), bf16),
            V((3 * C, LEN), bf16),
            V((3, C, LEN), bf16),
            V((2, C // 2, LEN), bf16),
            V((2, C, LEN), bf16),
            V((4, RB, FF), bf16),
            V((2, 4, RB, FF), bf16),
            V((4, RB, FF), bf16),
            V((3, RB, FF), bf16),
            V((RB, FF), bf16),
            V((3, RB, D), bf16),
            V((4, RB, HW), bf16),
            V((2, 4, RB, HW), bf16),
            V((4, RB, HW), bf16),
            V((3, RB, HW), bf16),
            V((4, RB, HW), bf16),
            V((2, 4, RB, HW), bf16),
            V((4, RB, HW), bf16),
            V((3, RB, HW), bf16),
            V((2, RB, HW), bf16),
            V((4, RB, C), bf16),
            V((3, RB, C), bf16),
            V((2, RB, D), f32),
            V((2, RB, HW), f32),
            V((D, 128), f32),
            V((16, D), f32),
            V((10, 16, D), f32),
            V((2, RB, D), bf16),
            pltpu.SemaphoreType.DMA((12,)),
            pltpu.SemaphoreType.DMA((N_SEM,)),
            pltpu.SemaphoreType.DMA((N_SEM,)),
        ],
        compiler_params=pltpu.CompilerParams(
            collective_id=0, has_side_effects=True, vmem_limit_bytes=62 * 2**20
        ),
    )(
        inputs, teacher, lengths, query_weight, key_weight, value_weight, output_weight.T,
        up_weight, down_weight, *vectors,
    )
    vector = sds((1, C), f32)
    weight = sds((RB, C), f32)
    wide = sds((RB, D), f32)
    done = pl.pallas_call(
        finish,
        name="finish",
        out_shape=(
            sds((C, LEN), bf16), sds((1,), f32), sds((C, LEN), f32),
            weight, vector, weight, weight, vector, weight,
            vector, vector, vector, wide, sds((6, 128), f32), wide, vector, vector, vector,
        ),
        in_specs=[vm] * 6,
        out_specs=(vm, pl.BlockSpec(memory_space=pltpu.SMEM)) + (vm,) * 16,
    )(*got)
    shapes = [
        (C, LEN), (), (C, LEN), (RB, C), (C,), (RB, C), (RB, C), (C,), (RB, C), (C,), (C,), (C,),
        (RB, D), (D,), (RB, D), (C,), (C,), (C,),
    ]
    done = [o.reshape(shape) for o, shape in zip(done, shapes)]
    done[8] = done[8].T
    return tuple(done)


def solution(mesh):
    split = Mesh(
        mesh.devices.reshape(mesh.shape["dp"], 4, 4, mesh.shape["col"]), AXES
    )
    tokens = P("col", DP_ROW)
    weight = P(ROW, "col")
    vector = P("col")
    return jax.shard_map(
        local_step,
        mesh=split,
        in_specs=(
            tokens, tokens, P(DP_ROW), weight, vector, weight, weight, vector,
            P("col", ROW), vector, vector, vector, weight, vector, weight,
            vector, vector, vector,
        ),
        out_specs=(
            tokens, P(), tokens, weight, vector, weight, weight, vector,
            P("col", ROW), vector, vector, vector, weight, vector, weight,
            vector, vector, vector,
        ),
        check_vma=False,
    )
```

```python
import jax
import jax.numpy as jnp
from jax import lax
from jax.experimental import pallas as pl
from jax.experimental.pallas import tpu as pltpu
from jax.sharding import Mesh
from jax.sharding import PartitionSpec as P

D = 768
FF = 3072
LEN = 1024
HD = 64
HEADS = 3
C = 192
TOK = 256
RB = 48
SLOTS = 32768
EPS = 1e-12
MASK = -1e30
ROOT_HALF = 0.7071067811865476
INV_ROOT_TAU = 0.3989422804014327
AXES = ("dp", "row_0", "row_1", "col")
ROW = ("row_0", "row_1")
DP_ROW = ("dp", "row_0", "row_1")
N_SEM = 256
FA = 512
FB = 256
QH = 288
HW = 384
f32 = jnp.float32
bf16 = jnp.bfloat16


def mm(a, b):
    return lax.dot_general(a, b, (((1,), (0,)), ((), ())), preferred_element_type=f32)


def mt(a, b):
    return lax.dot_general(a, b, (((1,), (1,)), ((), ())), preferred_element_type=f32)


def transposed(a):
    return jnp.transpose(a, (1, 0))


class Sent:
    def __init__(self, copy):
        self.copy, self.open_send, self.open_recv = copy, True, True

    def wait_send(self):
        if self.open_send:
            self.copy.wait_send()
        self.open_send = False

    def wait_recv(self):
        if self.open_recv:
            self.copy.wait_recv()
        self.open_recv = False

    def wait(self):
        self.wait_send()
        self.wait_recv()


class Links:
    def __init__(self, ssem, rsem):
        self.ssem, self.rsem, self.n, self.all = ssem, rsem, 0, []

    def send(self, src, dst, dev):
        copy = pltpu.make_async_remote_copy(
            src_ref=src,
            dst_ref=dst,
            send_sem=self.ssem.at[self.n],
            recv_sem=self.rsem.at[self.n],
            device_id=dev,
            device_id_type=pl.DeviceIdType.MESH,
        )
        copy.start()
        self.n += 1
        self.all.append(Sent(copy))
        return self.all[-1]


class RingGather:
    def __init__(self, links, ref, plus, minus, via_plus, via_minus):
        self.links, self.ref, self.plus, self.minus = links, ref, plus, minus
        self.via_plus, self.via_minus = via_plus, via_minus
        self.from_left, self.from_right, self.far = {}, {}, {}

    def send(self, part):
        own = self.ref("me", part)
        self.from_left[part] = self.links.send(own, own, self.plus)
        self.from_right[part] = self.links.send(own, own, self.minus)

    def first(self):
        for part in self.via_plus:
            own = self.ref("me", part)
            self.from_left[part] = self.links.send(own, own, self.plus)
        for part in self.via_minus:
            own = self.ref("me", part)
            self.from_right[part] = self.links.send(own, own, self.minus)

    def rest(self):
        for part in self.via_minus:
            own = self.ref("me", part)
            self.from_left[part] = self.links.send(own, own, self.plus)
        for part in self.via_plus:
            own = self.ref("me", part)
            self.from_right[part] = self.links.send(own, own, self.minus)

    def forward(self):
        for part in self.via_plus:
            self.from_left[part].wait_recv()
            ref = self.ref("left", part)
            self.far[part] = self.links.send(ref, ref, self.plus)
        for part in self.via_minus:
            self.from_right[part].wait_recv()
            ref = self.ref("right", part)
            self.far[part] = self.links.send(ref, ref, self.minus)

    def wait(self):
        for copies in (self.from_left, self.from_right, self.far):
            for copy in copies.values():
                copy.wait_recv()


class RingSum:
    def __init__(self, links, own, mid, recv, plus, minus, via_plus, via_minus):
        self.links, self.own, self.mid, self.recv = links, own, mid, recv
        self.plus, self.minus, self.via_plus, self.via_minus = plus, minus, via_plus, via_minus
        self.m, self.got = {}, {}

    def first(self):
        for p in self.via_plus:
            self.m[p] = self.links.send(self.own("far", p), self.mid.at[p], self.plus)
        for p in self.via_minus:
            self.m[p] = self.links.send(self.own("far", p), self.mid.at[p], self.minus)

    def direct(self, right=True, left=True):
        if right:
            for p in self.via_minus:
                self.got[0, p] = self.links.send(
                    self.own("right", p), self.recv.at[0, p], self.plus
                )
        if left:
            for p in self.via_plus:
                self.got[1, p] = self.links.send(
                    self.own("left", p), self.recv.at[1, p], self.minus
                )

    def middle(self):
        for p in self.via_plus:
            self.m[p].wait_recv()
            self.mid[p] = self.plus_f32(self.own("right", p)[...], self.mid[p])
            self.got[0, p] = self.links.send(self.mid.at[p], self.recv.at[0, p], self.plus)
        for p in self.via_minus:
            self.m[p].wait_recv()
            self.mid[p] = self.plus_f32(self.own("left", p)[...], self.mid[p])
            self.got[1, p] = self.links.send(self.mid.at[p], self.recv.at[1, p], self.minus)

    @staticmethod
    def plus_f32(a, b):
        return (a.astype(f32) + b.astype(f32)).astype(bf16)

    def total(self, p):
        self.got[0, p].wait_recv()
        self.got[1, p].wait_recv()
        total = self.own("me", p)[...].astype(f32)
        return total + self.recv[0, p].astype(f32) + self.recv[1, p].astype(f32)


def layer(
    x_in, t_in, len_in, wq_in, wk_in, wv_in, wo_in, up_in, down_in,
    ob_in, g1_in, b1_in, db_in, g2_in, b2_in, qb_in, vb_in, ub_in,
    out_o, gi_o, dwa_o, dwb_o, dwo_o, dqkv_o, sv_o,
    xf, tf, wa, wb, wq2, wo2, wo4, wqkv, vec, ub, vcol, qkvt, ktm, qaug, vaug, vtm, pst, linv,
    ctxt, ctxa, hid, nrm, sg, bstore, astore, slope, brecv, arecv,
    ga, gb, gaq, gqr, gao, gor, dctx, dct, outt, delta,
    dqkvt, dxp, rxi, rx, im, rm, s1, r2, s2, r3, zi, zr, sb0, bi, br, sb1, rb2,
    iq, rq, sq1, rq2, io, ro, so1, ro2, so2, so4, ro3,
    x1, xb1, xq1, gcol, sv, rsv, wown,
    lsem, ssem, rsem,
):
    d = lax.axis_index("dp")
    y = lax.axis_index("row_0")
    x = lax.axis_index("row_1")
    c = lax.axis_index("col")
    e = 1 - d
    r = 4 * y + x
    a_me = x * e + y * d
    b_me = y * e + x * d

    def around(me):
        return {
            "me": me,
            "left": lax.rem(me + 3, 4),
            "right": lax.rem(me + 1, 4),
            "far": lax.rem(me + 2, 4),
        }

    b_at, c_at = around(b_me), around(c)

    def ridx(a, b):
        return (4 * b + a) * e + (4 * a + b) * d

    def zdev(k):
        return {"col": lax.rem(c + k, 4)}

    def adev(k):
        return {"row_0": lax.rem(y + k * d, 4), "row_1": lax.rem(x + k * e, 4)}

    def bdev(k):
        return {"row_0": lax.rem(y + k * e, 4), "row_1": lax.rem(x + k * d, 4)}

    sib = {"dp": e}
    links = Links(ssem, rsem)

    def wait_all(copies):
        for copy in copies:
            copy.wait_recv()

    def cols(i, width):
        return pl.ds(pl.multiple_of(i * width, 128), width)

    def rows(i, height):
        return pl.ds(pl.multiple_of(i * height, 16), height)

    n_local = [0]

    def local(src, dst):
        copy = pltpu.make_async_copy(src, dst, lsem.at[n_local[0]])
        copy.start()
        n_local[0] += 1
        return copy

    xrows = rows(c, C)
    tcols = cols(c, TOK)
    bar = pltpu.get_barrier_semaphore()
    for k in (1, 2, 3):
        for dev in (zdev(k), adev(k), bdev(k)):
            pl.semaphore_signal(bar, inc=1, device_id=dev, device_id_type=pl.DeviceIdType.MESH)
    pl.semaphore_signal(bar, inc=1, device_id=sib, device_id_type=pl.DeviceIdType.MESH)
    cup = local(up_in, wown.at[0])
    cdn = local(down_in, wown.at[1])
    cx = local(x_in, xf.at[xrows])
    ct = local(t_in.at[:, tcols], tf.at[c])
    wo4[c] = wo_in[...]
    for i, ref in enumerate((ob_in, g1_in, b1_in, db_in, g2_in, b2_in, qb_in, vb_in)):
        vec[c, i : i + 1, :] = ref[...].reshape(1, C)
    ub[c, 0:1, :] = jnp.concatenate([ub_in[i : i + 1] for i in range(6)], axis=1)
    own_qkv = jnp.concatenate([wq_in[...], wk_in[...], wv_in[...]], axis=1)
    own_qkv = jnp.where(d == 0, own_qkv[:, 0:QH], own_qkv[:, QH:])
    wq2[d, r] = jnp.concatenate([own_qkv, jnp.zeros((RB, HW - QH), bf16)], axis=1)
    cup.wait()
    cdn.wait()
    wa[d, r, :, cols(c, FA)] = wown[d, :, 0:FA]
    wb[d, r, :, cols(c, FB)] = wown[d, :, FA:]
    pl.semaphore_wait(bar, 10)

    def along_a(ref):
        return [links.send(ref, ref, adev(k)) for k in (1, 3, 2)]

    def gather_b(ref):
        return RingGather(
            links,
            lambda at, k: ref(ridx(lax.rem(a_me + 4 - k, 4), b_at[at])),
            bdev(1), bdev(3), (0, 2), (1, 3),
        )

    def to_sibling(ref):
        return links.send(ref, ref, sib)

    def wq_ref(i):
        return wq2.at[d, i]

    def wo_ref(i):
        return wo2.at[d, i]

    def wa_ref(i):
        return wa.at[d, i]

    def wb_ref(i):
        return wb.at[d, i, :, cols(c, FB)]

    wq_a = along_a(wq_ref(r))
    wq_b = gather_b(wq_ref)
    wq_b.send(0)
    wz = []
    for k in (1, 3, 2):
        wz.append(
            links.send(wown.at[d, :, pl.ds(0, FA)], wa.at[d, r, :, cols(c, FA)], zdev(k))
        )
    cx.wait()
    x_z = RingGather(
        links,
        lambda at, half: xf.at[rows(2 * c_at[at] + half, C // 2)],
        zdev(1), zdev(3), (0,), (1,),
    )
    x_z.first()
    wb_a = along_a(wb_ref(r))
    wb_b = gather_b(wb_ref)
    wb_b.send(0)

    wait_all(wq_a)
    for k in (1, 3, 2):
        wq_b.send(k)
    wq_s = [to_sibling(wq_ref(ridx(j, b_me))) for j in range(4)]
    wait_all(wb_a)
    for k in (1, 3, 2):
        wb_b.send(k)
    x_z.rest()
    wait_all(wz)
    wa_a = along_a(wa_ref(r))
    wa_b = gather_b(wa_ref)
    wa_b.send(0)
    wq_b.forward()
    for at in ("left", "right"):
        for k in range(4):
            (wq_b.from_left if at == "left" else wq_b.from_right)[k].wait_recv()
            wq_s.append(to_sibling(wq_b.ref(at, k)))
    wb_b.forward()
    x_z.forward()
    oz = [links.send(wo4.at[c], wo4.at[c], zdev(k)) for k in (1, 3, 2)]
    for k in range(4):
        wq_b.far[k].wait_recv()
        wq_s.append(to_sibling(wq_b.ref("far", k)))
    wa_s = [to_sibling(wa_ref(r))]
    for i, k in enumerate((1, 3, 2)):
        wa_a[i].wait_recv()
        wa_b.send(k)
        wa_s.append(to_sibling(wa_b.ref("me", k)))
    vown = transposed(vec[c])
    length = len_in[0]

    x_z.wait()
    wb_b.wait()

    def wb_z(at, half):
        return wb.at[d, pl.ds(half * 8, 8), :, cols(c_at[at], FB)]

    wb_zg = RingGather(links, wb_z, zdev(1), zdev(3), (0,), (1,))
    wb_zg.send(0)
    wb_zg.send(1)
    vz = [links.send(vec.at[c], vec.at[c], zdev(k)) for k in (1, 2, 3)]
    uz = [links.send(ub.at[c, 0:1], ub.at[c, 0:1], zdev(k)) for k in (1, 2, 3)]
    wb_s = [to_sibling(wb.at[d, :, :, cols(c, FB)])]
    wait_all(oz)
    own_wo = jnp.concatenate([wo4[j] for j in range(4)], axis=1)
    wo2[d, r] = jnp.where(d == 0, own_wo[:, 0:HW], own_wo[:, HW:])
    wo_a = along_a(wo_ref(r))
    wo_b = gather_b(wo_ref)
    wo_b.send(0)
    wo_s = [to_sibling(wo_ref(r))]
    wait_all(wq_s)
    w_low = transposed(wq2[0].reshape(D, HW))[0:QH]
    w_high = transposed(wq2[1].reshape(D, HW))[0:QH]
    dxp[0, :, 0:D] = w_low[0:C]
    dxp[1, 0 : QH - C, 0:D] = w_low[C:]
    dxp[1, QH - C :, 0:D] = w_high[0 : QH - C]
    dxp[2, :, 0:D] = w_high[QH - C :]
    q_bias = vown[:, 6:7]
    v_bias = vown[:, 7:8]
    lane_iota = lax.broadcasted_iota(jnp.int32, (1, TOK), 1)
    first_row = lax.broadcasted_iota(jnp.int32, (HD, TOK), 0) == 0

    def qkv_chunk(i, carry):
        at = cols(i, TOK)
        tok = xf[:, at]
        q = (mm(dxp[0, :, 0:D], tok) + q_bias).astype(bf16)
        k = mm(dxp[1, :, 0:D], tok).astype(bf16)
        v = (mm(dxp[2, :, 0:D], tok) + v_bias).astype(bf16)
        q = (q.astype(f32) * (HD**-0.5)).astype(bf16)
        qkvt[0:C, at] = q
        qkvt[C : 2 * C, at] = k
        bias = jnp.where(lane_iota + i * TOK < length, 0.0, MASK)
        bias = jnp.where(first_row, jnp.broadcast_to(bias, (HD, TOK)), 0.0).astype(bf16)
        ones = jnp.where(first_row, 1.0, 0.0).astype(bf16)
        for h in range(HEADS):
            hs = slice(h * HD, (h + 1) * HD)
            qaug[h, 0:HD, at] = q[hs]
            qaug[h, HD : 2 * HD, at] = ones
            vaug[h, 0:HD, at] = v[hs]
            vaug[h, HD : HD + 16, at] = ones[0:16]
            ktm[h, at, :] = transposed(jnp.concatenate([k[hs], bias], axis=0))
            vtm[h, at, :] = transposed(jnp.concatenate([v[hs], ones], axis=0))
        return carry

    lax.fori_loop(0, 4, qkv_chunk, 0)

    def fwd_head(h):
        def fwd_tile(n, carry):
            at = cols(n, TOK)
            score = mm(ktm[h], qaug[h, :, at])
            top = jnp.max(score, axis=0, keepdims=True)
            probs = jnp.exp(score - top).astype(bf16)
            pst[h, :, at] = probs
            both = mm(vaug[h], probs)
            inv = 1.0 / both[HD : HD + 1]
            linv[h, 0:1, at] = inv
            ctxt[h * HD : (h + 1) * HD, at] = (both[0:HD] * inv).astype(bf16)
            return carry

        lax.fori_loop(0, 4, fwd_tile, 0)

    cc = []

    def context_out(h):
        hrow = pl.ds(h * HD, HD)
        ctxa[c, hrow] = ctxt[hrow, tcols]
        for k in (1, 3, 2):
            there = cols(lax.rem(c + k, 4), TOK)
            cc.append(links.send(ctxt.at[hrow, there], ctxa.at[c, hrow], zdev(k)))

    for i, k in enumerate((1, 3, 2)):
        wo_a[i].wait_recv()
        wo_b.send(k)
        wo_s.append(to_sibling(wo_b.ref("me", k)))
    fwd_head(0)
    context_out(0)
    wa_b.forward()
    for k in range(4):
        wa_b.from_left[k].wait_recv()
        wa_s.append(to_sibling(wa_b.ref("left", k)))
        wa_b.from_right[k].wait_recv()
        wa_s.append(to_sibling(wa_b.ref("right", k)))
    fwd_head(1)
    context_out(1)
    wo_b.forward()
    wb_zg.forward()
    for k in range(4):
        wo_b.from_left[k].wait_recv()
        wo_s.append(to_sibling(wo_b.ref("left", k)))
        wo_b.from_right[k].wait_recv()
        wo_s.append(to_sibling(wo_b.ref("right", k)))
    wait_all(vz + uz)
    for i in range(4):
        vcol[i * C : (i + 1) * C, 0:16] = transposed(vec[i])
    fwd_head(2)
    context_out(2)
    for k in range(4):
        wo_b.far[k].wait_recv()
        wo_s.append(to_sibling(wo_b.ref("far", k)))
    for k in range(4):
        wa_b.far[k].wait_recv()
        wa_s.append(to_sibling(wa_b.ref("far", k)))
    for i in range(2):
        wqkv[:, i * QH : (i + 1) * QH] = wq2[i].reshape(D, HW)[:, 0:QH]
    wait_all(wo_s)
    wait_all(cc)
    ct.wait()
    tt = []
    for k in (1, 3, 2):
        there = cols(lax.rem(c + k, 4), TOK)
        tt.append(links.send(t_in.at[:, there], tf.at[c], zdev(k)))

    def proj(i, carry):
        row = rows(i, C)
        acc = xf[row, tcols].astype(f32) + vcol[row, 0:1]
        for j in range(2):
            w = wo2[j, pl.ds(i * 4, 4)].reshape(C, HW)
            acc = acc + mm(w, ctxa[2 * j : 2 * j + 2].reshape(HW, TOK))
        hid[row] = acc
        return carry

    lax.fori_loop(0, 4, proj, 0)

    def norm_stats(ref):
        v = ref[...]
        mean = jnp.sum(v, axis=0, keepdims=True) * (1.0 / D)
        square = jnp.sum(v * v, axis=0, keepdims=True) * (1.0 / D)
        return mean, lax.rsqrt(square - mean * mean + EPS)

    mean1, inv1 = norm_stats(hid)

    def norm1(i, carry):
        row = rows(i, C)
        n = (hid[row] - mean1) * inv1
        nrm[row] = n
        h = n * vcol[row, 1:2] + vcol[row, 2:3]
        hid[row] = h + vcol[row, 3:4]
        astore[0, row] = h.astype(bf16)
        return carry

    lax.fori_loop(0, 4, norm1, 0)
    outt[...] = transposed(astore[0])
    wb_zg.wait()
    for k in (1, 2, 3):
        wb_s.append(to_sibling(wb.at[d, :, :, cols(lax.rem(c + k, 4), FB)]))

    wait_all(wa_s)

    def w_chunk(ref, i):
        return ref[:, :, cols(i, FA)].reshape(D, FA)

    def up_of(ref, bias, first):
        def up_chunk(i, carry):
            at = cols(first + i, FA)
            pre = mm(outt[...], w_chunk(ref, i)) + bias(i)
            half = 0.5 * (1.0 + lax.erf(pre * ROOT_HALF))
            bstore[1, :, at] = (pre * half).astype(bf16)
            slope[:, at] = (half + pre * jnp.exp(-0.5 * pre * pre) * INV_ROOT_TAU).astype(bf16)
            return carry

        return up_chunk

    def bias_b(i):
        return jnp.concatenate([ub[2 * i, 0:1, FA:], ub[2 * i + 1, 0:1, FA:]], axis=1)

    lax.fori_loop(0, 4, up_of(wa.at[0], lambda i: ub[i, 0:1, 0:FA], 0), 0)
    wait_all(wb_s)
    lax.fori_loop(0, 2, up_of(wb.at[0], bias_b, 4), 0)

    def down_of(ref, first):
        def down_chunk(i, carry):
            hid[...] = hid[...] + mt(w_chunk(ref, i), bstore[1, :, cols(first + i, FA)])
            return carry

        return down_chunk

    lax.fori_loop(0, 4, down_of(wa.at[1], 0), 0)
    lax.fori_loop(0, 2, down_of(wb.at[1], 4), 0)

    mean2, inv2 = norm_stats(hid)
    wait_all(tt)
    valid = lane_iota + c * TOK < length
    gcol[...] = jnp.zeros(gcol.shape, f32)
    sv[...] = jnp.zeros(sv.shape, f32)

    def norm2(i, carry):
        total, crossed, loss = carry
        row = rows(i, C)
        n = (hid[row] - mean2) * inv2
        hid[row] = n
        final = n * vcol[row, 4:5] + vcol[row, 5:6]
        delta[row] = final.astype(bf16)
        g = jnp.where(valid, final - tf[i].astype(f32), 0.0)
        gcol[row, 4:5] = jnp.sum(g * n, axis=1, keepdims=True)
        gcol[row, 5:6] = jnp.sum(g, axis=1, keepdims=True)
        s = g * vcol[row, 4:5]
        sg[row] = s
        return (
            total + jnp.sum(s, axis=0, keepdims=True),
            crossed + jnp.sum(s * n, axis=0, keepdims=True),
            loss + jnp.sum(g * g, axis=0, keepdims=True),
        )

    zero = jnp.zeros((1, TOK), f32)
    total2, crossed2, loss_row = lax.fori_loop(0, 4, norm2, (zero, zero, zero))
    fo = []
    out_o_own = local(delta.at[xrows], out_o.at[:, tcols])
    for k in (1, 3, 2):
        there = rows(lax.rem(c + k, 4), C)
        fo.append(links.send(delta.at[there], out_o.at[:, tcols], zdev(k)))

    def norm2_back(i, carry):
        row = rows(i, C)
        s = inv2 * (sg[row] - total2 * (1.0 / D) - hid[row] * (crossed2 * (1.0 / D)))
        sg[row] = s
        low = s.astype(bf16)
        astore[1, row] = low
        gcol[row, 3:4] = jnp.sum(low.astype(f32), axis=1, keepdims=True)
        return carry

    lax.fori_loop(0, 4, norm2_back, 0)
    outt[...] = transposed(astore[1])

    def act_of(ref, first):
        def act_chunk(i, carry):
            at = cols(first + i, FA)
            g = mm(outt[...], w_chunk(ref, i)) * slope[:, at].astype(f32)
            low = g.astype(bf16)
            bstore[0, :, at] = low
            sv[pl.ds(8 + first + i, 1), 0:FA] = jnp.sum(low.astype(f32), axis=0, keepdims=True)
            return carry

        return act_chunk

    lax.fori_loop(0, 2, act_of(wb.at[1], 4), 0)
    lax.fori_loop(0, 4, act_of(wa.at[1], 0), 0)
    ex = [
        links.send(astore.at[e], arecv, sib),
        links.send(bstore.at[e], brecv, sib),
    ]

    def back_of(ref, first):
        def back_chunk(i, carry):
            sg[...] = sg[...] + mt(w_chunk(ref, i), bstore[0, :, cols(first + i, FA)])
            return carry

        return back_chunk

    lax.fori_loop(0, 2, back_of(wb.at[0], 4), 0)
    lax.fori_loop(0, 4, back_of(wa.at[0], 0), 0)

    def hidden_back(i, carry):
        total, crossed = carry
        row = rows(i, C)
        g = sg[row]
        n = nrm[row]
        gcol[row, 1:2] = jnp.sum(g * n, axis=1, keepdims=True)
        gcol[row, 2:3] = jnp.sum(g, axis=1, keepdims=True)
        s = g * vcol[row, 1:2]
        sg[row] = s
        return (
            total + jnp.sum(s, axis=0, keepdims=True),
            crossed + jnp.sum(s * n, axis=0, keepdims=True),
        )

    total1, crossed1 = lax.fori_loop(0, 4, hidden_back, (zero, zero))

    def norm1_back(i, carry):
        row = rows(i, C)
        s = inv1 * (sg[row] - total1 * (1.0 / D) - nrm[row] * (crossed1 * (1.0 / D)))
        sg[row] = s
        low = s.astype(bf16)
        delta[row] = low
        gcol[row, 0:1] = jnp.sum(low.astype(f32), axis=1, keepdims=True)
        return carry

    for copy in fo:
        copy.wait_send()
    out_o_own.wait()
    lax.fori_loop(0, 4, norm1_back, 0)
    outt[...] = transposed(delta[...])

    dc = []
    for i in range(2):
        part = transposed(mm(outt[...], wo2[i].reshape(D, HW)).astype(bf16))
        dct[2 * i : 2 * i + 2] = part.reshape(2, C, TOK)
    dctx[:, tcols] = dct[c]
    for h in range(HEADS):
        hrow = pl.ds(h * HD, HD)
        dc.append(
            [
                links.send(dct.at[lax.rem(c + k, 4), hrow], dctx.at[hrow, tcols], zdev(k))
                for k in (1, 3, 2)
            ]
        )

    sv[0:8] = transposed(gcol[...])[0:8]
    sv[6:7] = jnp.broadcast_to(jnp.sum(loss_row, axis=1, keepdims=True), (1, D))
    sv[7:8] = jnp.broadcast_to(length.astype(f32), (1, D))
    n_sv = [1]
    v_sent = [links.send(sv, rsv.at[0], sib)]

    def sv_add():
        for copy in v_sent:
            copy.wait()
        lo = n_sv[0] - len(v_sent)
        total = sv[...]
        for i in range(len(v_sent)):
            total = total + rsv[lo + i]
        sv[...] = total
        v_sent.clear()

    def sv_send(dev):
        for k in (1, 3, 2):
            v_sent.append(links.send(sv, rsv.at[n_sv[0]], dev(k)))
            n_sv[0] += 1

    wait_all(ex)

    def grad_of(ref, first):
        def grad_chunk(i, carry):
            at = cols(first + i, FA)
            g = mm(astore[d], bstore[d, :, at]) + mm(arecv[...], brecv[:, at])
            ref[:, :, cols(i, FA)] = g.astype(bf16).reshape(16, RB, FA)
            return carry

        return grad_chunk

    lax.fori_loop(0, 2, grad_of(gb, 4), 0)
    HALVES = ((0,), (1,))

    def zb_own(at, half):
        return gb.at[pl.ds(half * 8, 8), :, cols(c_at[at], FB)]

    zb_sum = RingSum(links, zb_own, zi, zr, zdev(1), zdev(3), *HALVES)
    lax.fori_loop(0, 4, grad_of(ga, 0), 0)
    sv_add()
    sv_send(bdev)

    def sum_b(own, mid, recv):
        return RingSum(
            links, lambda at, j: own(ridx(j, b_at[at])), mid, recv, bdev(1), bdev(3), (0, 1), (2, 3)
        )

    def end_b(ring, summed, peer_recv):
        for j in range(4):
            summed[j] = ring.total(j).astype(bf16)
        return [
            links.send(summed.at[lax.rem(a_me + k, 4)], peer_recv.at[k - 1], adev(k))
            for k in (1, 3, 2)
        ]

    def end_a(sends, summed, recv):
        wait_all(sends)
        total = summed[a_me].astype(f32)
        for k in range(3):
            total = total + recv[k].astype(f32)
        return total

    def add_sibling(ref, other):
        def add(i, carry):
            ref[d, i] = (ref[d, i].astype(f32) + other[i].astype(f32)).astype(bf16)
            return carry

        lax.fori_loop(0, 16, add, 0)

    wa_sum = sum_b(lambda i: ga.at[i], im, rm)
    wa_sum.first()
    zb_sum.first()
    g = mt(delta[...], ctxa[...].reshape(D, TOK)).astype(bf16)
    for i in range(2):
        gao[i] = g[:, i * HW : (i + 1) * HW].reshape(16, RB, HW)
    go_x = links.send(gao.at[e], gor, sib)

    def bwd_head(h):
        hrow = pl.ds(h * HD, HD)
        krow = pl.ds(C + h * HD, HD)
        vrow = pl.ds(2 * C + h * HD, HD)

        def bwd_tile(n, acc):
            dk, dv = acc
            at = cols(n, TOK)
            inv = linv[h, 0:1, at]
            dc = dctx[hrow, at].astype(f32)
            inner = jnp.sum(dc * ctxt[hrow, at].astype(f32), axis=0, keepdims=True) * inv
            dcs = (dc * inv).astype(bf16)
            probs = pst[h, :, at]
            dp = mm(vtm[h, :, 0:HD], dcs) - inner
            ds = (probs.astype(f32) * dp).astype(bf16)
            dqkvt[hrow, at] = (mm(qkvt[krow, :], ds) * (HD**-0.5)).astype(bf16)
            dk = dk + mt(qkvt[hrow, at], ds)
            dv = dv + mt(dcs, probs)
            return dk, dv

        dk, dv = lax.fori_loop(
            0, 4, bwd_tile, (jnp.zeros((HD, LEN), f32), jnp.zeros((HD, LEN), f32))
        )
        dqkvt[krow] = dk.astype(bf16)
        dqkvt[vrow] = dv.astype(bf16)

    wait_all(dc[0])
    bwd_head(0)
    wa_sum.direct()
    zb_sum.direct()
    sv_add()
    sv_send(adev)
    go_x.wait_recv()
    add_sibling(gao, gor)
    o_sum = sum_b(lambda i: gao.at[d, i], io, ro)
    o_sum.first()
    wait_all(dc[1])
    bwd_head(1)
    wa_sum.middle()
    zb_sum.middle()
    o_sum.direct()
    wait_all(dc[2])
    bwd_head(2)

    def dx_part(i):
        row = rows(i, C)
        gi_o[...] = mm(wqkv[row], dqkvt[...])
        gi_o[:, tcols] = gi_o[:, tcols] + sg[row]

    SLOT = {"far": 0, "right": 1, "left": 2}

    def dx_own(at, half):
        return dxp.at[SLOT[at], pl.ds(half * (C // 2), C // 2)]

    dx_sum = RingSum(links, dx_own, rxi, rx, zdev(1), zdev(3), *HALVES)
    dx_part(c_at["far"])
    dxp[0] = gi_o[...].astype(bf16)
    dx_sum.first()

    bias_sum = mt(jnp.ones((8, LEN), bf16), dqkvt[...])[0:1]
    spare = HW - QH
    row_iota = lax.broadcasted_iota(jnp.int32, (RB, spare), 0)
    bias_rows = []
    for i in range(2):
        part_rows = jnp.zeros((RB, spare), f32)
        for j in range(3):
            at = i * QH + j * spare
            part = jnp.broadcast_to(bias_sum[:, at : at + spare], (RB, spare))
            part_rows = jnp.where(row_iota == j, part, part_rows)
        bias_rows.append(jnp.broadcast_to(part_rows.astype(bf16)[None], (4, RB, spare)))

    def dqkv_block(n, carry):
        row = rows(n, C)
        blocks = pl.ds(n * 4, 4)
        for i in range(2):
            g = mt(xf[row], dqkvt[i * QH : (i + 1) * QH])
            gaq[i, blocks, :, 0:QH] = g.astype(bf16).reshape(4, RB, QH)
            gaq[i, blocks, :, QH:] = bias_rows[i]
        return carry

    lax.fori_loop(0, 4, dqkv_block, 0)
    gx = links.send(gaq.at[e], gqr, sib)
    o_sum.middle()
    wa_sends = end_b(wa_sum, s1, r2)

    dx_part(c_at["right"])
    dxp[1] = gi_o[...].astype(bf16)
    dx_sum.direct(left=False)
    dx_part(c_at["left"])
    dxp[2] = gi_o[...].astype(bf16)
    dx_sum.direct(right=False)
    dx_part(c)

    gx.wait_recv()
    add_sibling(gaq, gqr)
    q_sum = sum_b(lambda i: gaq.at[d, i], iq, rq)
    q_sum.first()
    for half in range(2):
        sb0[half * 8 : half * 8 + 8] = zb_sum.total(half).astype(bf16)
    wb_sum = sum_b(lambda i: sb0.at[i], bi, br)
    wb_sum.first()
    dx_sum.middle()
    q_sum.direct()
    wb_sum.direct()
    o_sends = end_b(o_sum, so1, ro2)
    sv_add()
    sv_send(zdev)
    q_sum.middle()
    wb_sum.middle()
    s2[...] = end_a(wa_sends, s1, r2).astype(bf16)
    w3 = []
    for k in (1, 3, 2):
        w3.append(links.send(s2.at[:, cols(lax.rem(c + k, 4), FA)], r3.at[k - 1], zdev(k)))
    so2[0] = end_a(o_sends, so1, ro2).astype(bf16)
    o_x = links.send(so2.at[0], so2.at[1], sib)
    q_sends = end_b(q_sum, sq1, rq2)
    wb_sends = end_b(wb_sum, sb1, rb2)
    o_x.wait_recv()
    mine, other = so2[0], so2[1]
    low, high = jnp.where(d == 0, mine, other), jnp.where(d == 0, other, mine)
    so4[0], so4[1] = low[:, 0:C], low[:, C:]
    so4[2], so4[3] = high[:, 0:C], high[:, C:]
    o3 = [links.send(so4.at[lax.rem(c + k, 4)], ro3.at[k - 1], zdev(k)) for k in (1, 3, 2)]
    sv_add()
    sv_o[...] = sv[...]
    for half in range(2):
        dx_sum.got[0, half].wait_recv()
        dx_sum.got[1, half].wait_recv()
        row = pl.ds(half * (C // 2), C // 2)
        gi_o[row] = gi_o[row] + rx[0, half].astype(f32) + rx[1, half].astype(f32)
    dqkv = end_a(q_sends, sq1, rq2)
    xq1[0] = dqkv
    q3 = links.send(xq1.at[0], xq1.at[1], sib)
    xb1[0] = end_a(wb_sends, sb1, rb2)
    wb4 = links.send(xb1.at[0], xb1.at[1], sib)
    wait_all(w3)
    total = s2[:, cols(c, FA)].astype(f32)
    for k in range(3):
        total = total + r3[k].astype(f32)
    x1[0] = total
    w4 = links.send(x1.at[0], x1.at[1], sib)
    wait_all(o3)
    ototal = so4[c].astype(f32)
    for k in range(3):
        ototal = ototal + ro3[k].astype(f32)
    dwo_o[...] = ototal
    wb4.wait_recv()
    dwb_o[d] = xb1[0]
    dwb_o[e] = xb1[1]
    q3.wait_recv()
    dqkv_o[d] = dqkv
    dqkv_o[e] = xq1[1]
    w4.wait_recv()
    dwa_o[d] = total
    dwa_o[e] = x1[1]
    for copy in links.all:
        copy.wait()


def finish(
    out_i, gi_i, dwa_i, dwb_i, dwo_i, dqkv_i, sv_i,
    out, loss, gi, gwq, gbq, gwk, gwv, gbv, gwo, gob, gg1, gb1, gup, gub, gdn, gdb, gg2, gb2,
):
    c = lax.axis_index("col")
    out[...] = out_i[...]
    count = sv_i[7:8, 0:1] * 0.25
    factor = SLOTS / count
    loss[0] = jnp.sum(sv_i[6:7, 0:1] / (2.0 * D * count))
    gi[...] = gi_i[...] * factor
    low, high = dqkv_i[0] * factor, dqkv_i[1] * factor
    gwq[...] = low[:, 0:C]
    gwk[...] = jnp.concatenate([low[:, C:QH], high[:, 0 : QH - C]], axis=1)
    gwv[...] = high[:, QH - C : QH]
    gbq[...] = jnp.concatenate([low[0:1, QH:], low[1:2, QH:]], axis=1)
    gbv[...] = jnp.concatenate([high[1:2, QH:], high[2:3, QH:]], axis=1)
    gwo[...] = dwo_i[...] * factor
    for i, ref in enumerate((gup, gdn)):
        ref[:, 0:FA] = dwa_i[i] * factor
        ref[:, FA:] = dwb_i[i] * factor
    sums = sv_i[...] * factor
    for j in range(4):

        @pl.when(c == j)
        def _(j=j):
            for i in range(4):
                gub[i : i + 1] = sums[8 + j : 9 + j, i * 128 : (i + 1) * 128]
            for i in range(2):
                at = (j % 2) * FB + i * 128
                gub[4 + i : 5 + i] = sums[12 + j // 2 : 13 + j // 2, at : at + 128]
            for i, ref in enumerate((gob, gg1, gb1, gdb, gg2, gb2)):
                ref[...] = sums[i : i + 1, j * C : (j + 1) * C]


def local_step(
    inputs, teacher, lengths, query_weight, query_bias, key_weight, value_weight, value_bias,
    output_weight, output_bias, first_gain, first_shift, up_weight, up_bias, down_weight,
    down_bias, second_gain, second_shift,
):
    anyspec = pl.BlockSpec(memory_space=pl.ANY)
    vm = pl.BlockSpec(memory_space=pltpu.VMEM)
    sds = jax.ShapeDtypeStruct
    V = pltpu.VMEM
    vectors = [
        v.reshape(1, -1)
        for v in (
            output_bias, first_gain, first_shift, down_bias, second_gain, second_shift,
            query_bias, value_bias,
        )
    ]
    vectors.append(up_bias.reshape(6, 128))
    got = pl.pallas_call(
        layer,
        name="layer",
        out_shape=(
            sds((C, LEN), bf16),
            sds((C, LEN), f32),
            sds((2, RB, FA), f32),
            sds((2, RB, FB), f32),
            sds((RB, C), f32),
            sds((2, RB, HW), f32),
            sds((16, D), f32),
        ),
        in_specs=[anyspec, anyspec, pl.BlockSpec(memory_space=pltpu.SMEM)]
        + [vm] * 4
        + [anyspec] * 2
        + [vm] * 9,
        out_specs=(anyspec, vm, vm, vm, vm, vm, vm),
        scratch_shapes=[
            V((D, LEN), bf16),
            V((4, C, TOK), bf16),
            V((2, 16, RB, 4 * FA), bf16),
            V((2, 16, RB, 4 * FB), bf16),
            V((2, 16, RB, HW), bf16),
            V((2, 16, RB, HW), bf16),
            V((4, RB, C), bf16),
            V((D, 3 * C), bf16),
            V((4, 16, C), f32),
            V((4, 8, D), f32),
            V((D, 128), f32),
            V((2 * C, LEN), bf16),
            V((HEADS, LEN, 2 * HD), bf16),
            V((HEADS, 2 * HD, LEN), bf16),
            V((HEADS, HD + 16, LEN), bf16),
            V((HEADS, LEN, 2 * HD), bf16),
            V((HEADS, LEN, LEN), bf16),
            V((HEADS, 8, LEN), f32),
            V((C, LEN), bf16),
            V((4, C, TOK), bf16),
            V((D, TOK), f32),
            V((D, TOK), f32),
            V((D, TOK), f32),
            V((2, TOK, FF), bf16),
            V((2, D, TOK), bf16),
            V((TOK, FF), bf16),
            V((TOK, FF), bf16),
            V((D, TOK), bf16),
            V((16, RB, 4 * FA), bf16),
            V((16, RB, 4 * FB), bf16),
            V((2, 16, RB, HW), bf16),
            V((16, RB, HW), bf16),
            V((2, 16, RB, HW), bf16),
            V((16, RB, HW), bf16),
            V((C, LEN), bf16),
            V((4, C, TOK), bf16),
            V((TOK, D), bf16),
            V((D, TOK), bf16),
            V((3 * C, LEN), bf16),
            V((3, C, LEN), bf16),
            V((2, C // 2, LEN), bf16),
            V((2, 2, C // 2, LEN), bf16),
            V((4, RB, 4 * FA), bf16),
            V((2, 4, RB, 4 * FA), bf16),
            V((4, RB, 4 * FA), bf16),
            V((3, RB, 4 * FA), bf16),
            V((RB, 4 * FA), bf16),
            V((3, RB, FA), bf16),
            V((2, 8, RB, FB), bf16),
            V((2, 2, 8, RB, FB), bf16),
            V((16, RB, FB), bf16),
            V((4, RB, FB), bf16),
            V((2, 4, RB, FB), bf16),
            V((4, RB, FB), bf16),
            V((3, RB, FB), bf16),
            V((4, RB, HW), bf16),
            V((2, 4, RB, HW), bf16),
            V((4, RB, HW), bf16),
            V((3, RB, HW), bf16),
            V((4, RB, HW), bf16),
            V((2, 4, RB, HW), bf16),
            V((4, RB, HW), bf16),
            V((3, RB, HW), bf16),
            V((2, RB, HW), bf16),
            V((4, RB, C), bf16),
            V((3, RB, C), bf16),
            V((2, RB, FA), f32),
            V((2, RB, FB), f32),
            V((2, RB, HW), f32),
            V((D, 128), f32),
            V((16, D), f32),
            V((10, 16, D), f32),
            V((2, RB, D), bf16),
            pltpu.SemaphoreType.DMA((12,)),
            pltpu.SemaphoreType.DMA((N_SEM,)),
            pltpu.SemaphoreType.DMA((N_SEM,)),
        ],
        compiler_params=pltpu.CompilerParams(
            collective_id=0, has_side_effects=True, vmem_limit_bytes=62 * 2**20
        ),
    )(
        inputs, teacher, lengths, query_weight, key_weight, value_weight, output_weight.T,
        up_weight, down_weight, *vectors,
    )
    vector = sds((1, C), f32)
    weight = sds((RB, C), f32)
    wide = sds((RB, D), f32)
    done = pl.pallas_call(
        finish,
        name="finish",
        out_shape=(
            sds((C, LEN), bf16), sds((1,), f32), sds((C, LEN), f32),
            weight, vector, weight, weight, vector, weight,
            vector, vector, vector, wide, sds((6, 128), f32), wide, vector, vector, vector,
        ),
        in_specs=[vm] * 7,
        out_specs=(vm, pl.BlockSpec(memory_space=pltpu.SMEM)) + (vm,) * 16,
    )(*got)
    shapes = [
        (C, LEN), (), (C, LEN), (RB, C), (C,), (RB, C), (RB, C), (C,), (RB, C), (C,), (C,), (C,),
        (RB, D), (D,), (RB, D), (C,), (C,), (C,),
    ]
    done = [o.reshape(shape) for o, shape in zip(done, shapes)]
    done[8] = done[8].T
    return tuple(done)


def solution(mesh):
    split = Mesh(
        mesh.devices.reshape(mesh.shape["dp"], 4, 4, mesh.shape["col"]), AXES
    )
    tokens = P("col", DP_ROW)
    weight = P(ROW, "col")
    vector = P("col")
    return jax.shard_map(
        local_step,
        mesh=split,
        in_specs=(
            tokens, tokens, P(DP_ROW), weight, vector, weight, weight, vector,
            P("col", ROW), vector, vector, vector, weight, vector, weight,
            vector, vector, vector,
        ),
        out_specs=(
            tokens, P(), tokens, weight, vector, weight, weight, vector,
            P("col", ROW), vector, vector, vector, weight, vector, weight,
            vector, vector, vector,
        ),
        check_vma=False,
    )
```

```python
import jax
import jax.numpy as jnp
from jax import lax
from jax.experimental import pallas as pl
from jax.experimental.pallas import tpu as pltpu
from jax.sharding import Mesh
from jax.sharding import PartitionSpec as P

D = 768
FF = 3072
LEN = 1024
HD = 64
HEADS = 3
C = 192
TOK = 256
RB = 48
SLOTS = 32768
EPS = 1e-12
MASK = -1e30
ROOT_HALF = 0.7071067811865476
INV_ROOT_TAU = 0.3989422804014327
AXES = ("dp", "row_0", "row_1", "col")
ROW = ("row_0", "row_1")
DP_ROW = ("dp", "row_0", "row_1")
N_SEM = 96
HL = 128
QC = 96
FA = 512
FB = 256
WT = 512
WF = 1024
QH = 288
HW = 384
f32 = jnp.float32
bf16 = jnp.bfloat16


def mm(a, b):
    return lax.dot_general(a, b, (((1,), (0,)), ((), ())), preferred_element_type=f32)


def mt(a, b):
    return lax.dot_general(a, b, (((1,), (1,)), ((), ())), preferred_element_type=f32)


def transposed(a):
    return jnp.transpose(a, (1, 0))


class Sent:
    def __init__(self, copy):
        self.copy, self.open_send, self.open_recv = copy, True, True

    def wait_send(self):
        if self.open_send:
            self.copy.wait_send()
        self.open_send = False

    def wait_recv(self):
        if self.open_recv:
            self.copy.wait_recv()
        self.open_recv = False

    def wait(self):
        self.wait_send()
        self.wait_recv()


class Batch(Sent):
    def __init__(self, ssem, rsem, whole):
        self.ssem, self.rsem, self.whole, self.dev = ssem, rsem, whole, None
        super().__init__(None)

    def copy_of(self, src, dst):
        return pltpu.make_async_remote_copy(
            src_ref=src,
            dst_ref=dst,
            send_sem=self.ssem,
            recv_sem=self.rsem,
            device_id=self.dev,
            device_id_type=pl.DeviceIdType.MESH,
        )

    def send(self, src, dst, dev):
        self.dev = dev
        self.copy_of(src, dst).start()

    def wait_send(self):
        if self.open_send:
            self.copy = self.copy_of(self.whole, self.whole)
        super().wait_send()

    def wait_recv(self):
        if self.open_recv:
            self.copy = self.copy_of(self.whole, self.whole)
        super().wait_recv()


class Links:
    def __init__(self, ssem, rsem):
        self.ssem, self.rsem, self.n, self.all = ssem, rsem, 0, []

    def send(self, src, dst, dev):
        copy = pltpu.make_async_remote_copy(
            src_ref=src,
            dst_ref=dst,
            send_sem=self.ssem.at[self.n],
            recv_sem=self.rsem.at[self.n],
            device_id=dev,
            device_id_type=pl.DeviceIdType.MESH,
        )
        copy.start()
        self.n += 1
        self.all.append(Sent(copy))
        return self.all[-1]

    def batch(self, whole):
        self.all.append(Batch(self.ssem.at[self.n], self.rsem.at[self.n], whole))
        self.n += 1
        return self.all[-1]


class RingGather:
    def __init__(self, links, ref, whole, plus, minus, plus_parts, minus_parts):
        self.ref, self.plus, self.minus = ref, plus, minus
        self.plus_parts, self.minus_parts = plus_parts, minus_parts
        half = len(plus_parts)
        self.left_on, self.left_end = links.batch(whole(half)), links.batch(whole(half))
        self.right_on, self.right_end = links.batch(whole(half)), links.batch(whole(half))
        self.far = links.batch(whole(2 * half))

    def send_plus(self, part):
        own = self.ref("me", part)
        batch = self.left_on if part in self.plus_parts else self.left_end
        batch.send(own, own, self.plus)

    def send_minus(self, part):
        own = self.ref("me", part)
        batch = self.right_on if part in self.minus_parts else self.right_end
        batch.send(own, own, self.minus)

    def send(self, part):
        self.send_plus(part)
        self.send_minus(part)

    def first(self):
        for part in self.plus_parts:
            self.send_plus(part)
        for part in self.minus_parts:
            self.send_minus(part)

    def rest(self):
        for part in self.minus_parts:
            self.send_plus(part)
        for part in self.plus_parts:
            self.send_minus(part)

    def forward(self):
        self.left_on.wait_recv()
        for part in self.plus_parts:
            ref = self.ref("left", part)
            self.far.send(ref, ref, self.plus)
        self.right_on.wait_recv()
        for part in self.minus_parts:
            ref = self.ref("right", part)
            self.far.send(ref, ref, self.minus)

    def wait(self, at):
        batches = {
            "left": (self.left_on, self.left_end),
            "right": (self.right_on, self.right_end),
            "far": (self.far,),
        }
        for batch in batches[at]:
            batch.wait_recv()


class DirectGather:
    def __init__(self, links, ref, whole, devs):
        self.ref, self.devs, self.batch = ref, devs, links.batch(whole(12))

    def send(self, part):
        own = self.ref("me", part)
        for dev in self.devs:
            self.batch.send(own, own, dev)


class DirectSum:
    def __init__(self, links, own, recv, devs):
        self.own, self.recv, self.devs, self.batch = own, recv, devs, links.batch(recv)

    def start(self):
        for i, at in enumerate(("right", "left", "far")):
            for p in range(4):
                self.batch.send(self.own(at, p), self.recv.at[i, p], self.devs[i])

    def total(self, p):
        self.batch.wait_recv()
        total = self.own("me", p)[...].astype(f32)
        for i in range(3):
            total = total + self.recv[i, p].astype(f32)
        return total


class RingSum:
    def __init__(self, links, own, mid, recv, plus, minus, parts):
        self.own, self.mid, self.recv, self.plus, self.minus = own, mid, recv, plus, minus
        half = parts // 2
        self.low, self.high = range(half), range(half, parts)
        self.mid_left = links.batch(mid.at[pl.ds(0, half)])
        self.mid_right = links.batch(mid.at[pl.ds(half, half)])
        self.left, self.right = links.batch(recv.at[0]), links.batch(recv.at[1])

    def first(self):
        for p in self.low:
            self.mid_left.send(self.own("far", p), self.mid.at[p], self.plus)
        for p in self.high:
            self.mid_right.send(self.own("far", p), self.mid.at[p], self.minus)

    def direct_right(self):
        for p in self.high:
            self.left.send(self.own("right", p), self.recv.at[0, p], self.plus)

    def direct_left(self):
        for p in self.low:
            self.right.send(self.own("left", p), self.recv.at[1, p], self.minus)

    def direct(self):
        self.direct_right()
        self.direct_left()

    def middle(self):
        self.mid_left.wait_recv()
        for p in self.low:
            self.mid[p] = self.plus_f32(self.own("right", p)[...], self.mid[p])
            self.left.send(self.mid.at[p], self.recv.at[0, p], self.plus)
        self.mid_right.wait_recv()
        for p in self.high:
            self.mid[p] = self.plus_f32(self.own("left", p)[...], self.mid[p])
            self.right.send(self.mid.at[p], self.recv.at[1, p], self.minus)

    @staticmethod
    def plus_f32(a, b):
        return (a.astype(f32) + b.astype(f32)).astype(bf16)

    def wait(self):
        self.left.wait_recv()
        self.right.wait_recv()

    def total(self, p):
        self.wait()
        total = self.own("me", p)[...].astype(f32)
        return total + self.recv[0, p].astype(f32) + self.recv[1, p].astype(f32)


def layer(
    x_in, t_in, len_in, wq_in, wk_in, wv_in, wo_in, up_in, down_in,
    ob_in, g1_in, b1_in, db_in, g2_in, b2_in, qb_in, vb_in, ub_in,
    out_o, gi_o, dwa_o, dwb_o, dwo_o, dqkv_o, sv_o,
    xf, tf, wa, wb, wq2, wo2, wo4, wqkv, vec, ub, vcol, qkvt, ktm, qaug, vaug, vtm, pst, linv,
    ctxt, ctxa, hid, nrm, sg, bstore, astore, slope, brecv, arecv,
    ga, gb, gqa, gqb, gra, grb, gao, gor, dctx, dct, outt, delta,
    dqkvt, dxp, rxi, rx, im, rm, s1, r2, s2, r3, zi, zr, sb0, br, sb1, rb2,
    rqa, rqb, sqa, sqb, ra2, rb3, ro, so1, ro2, so2, so4, ro3,
    x1, xb1, xq1, gcol, sv, rsv, wown,
    lsem, ssem, rsem,
):
    d = lax.axis_index("dp")
    y = lax.axis_index("row_0")
    x = lax.axis_index("row_1")
    c = lax.axis_index("col")
    e = 1 - d
    r = 4 * y + x
    a_me = x * e + y * d
    b_me = y * e + x * d

    def around(me):
        return {
            "me": me,
            "left": lax.rem(me + 3, 4),
            "right": lax.rem(me + 1, 4),
            "far": lax.rem(me + 2, 4),
        }

    b_at, c_at = around(b_me), around(c)

    def ridx(a, b):
        return (4 * b + a) * e + (4 * a + b) * d

    def zdev(k):
        return {"col": lax.rem(c + k, 4)}

    def adev(k):
        return {"row_0": lax.rem(y + k * d, 4), "row_1": lax.rem(x + k * e, 4)}

    def bdev(k):
        return {"row_0": lax.rem(y + k * e, 4), "row_1": lax.rem(x + k * d, 4)}

    sib = {"dp": e}
    links = Links(ssem, rsem)

    def wait_all(copies):
        for copy in copies:
            copy.wait_recv()

    def triple(whole, src, dst, dev):
        batch = links.batch(whole)
        for k in (1, 3, 2):
            batch.send(src(k), dst(k), dev(k))
        return batch

    def unrolled(n, body, carry):
        for i in range(n):
            carry = body(i, carry)
        return carry

    def cols(i, width):
        if isinstance(i, int):
            return pl.ds(i * width, width)
        return pl.ds(pl.multiple_of(i * width, 128), width)

    def rows(i, height):
        if isinstance(i, int):
            return pl.ds(i * height, height)
        return pl.ds(pl.multiple_of(i * height, 16), height)

    n_local = [0]

    def local(src, dst):
        copy = pltpu.make_async_copy(src, dst, lsem.at[n_local[0]])
        copy.start()
        n_local[0] += 1
        return copy

    xrows = rows(c, C)
    tcols = cols(c, TOK)
    bar = pltpu.get_barrier_semaphore()
    for k in (1, 2, 3):
        for dev in (zdev(k), adev(k), bdev(k)):
            pl.semaphore_signal(bar, inc=1, device_id=dev, device_id_type=pl.DeviceIdType.MESH)
    pl.semaphore_signal(bar, inc=1, device_id=sib, device_id_type=pl.DeviceIdType.MESH)
    cup = local(up_in, wown.at[0])
    cdn = local(down_in, wown.at[1])
    cx = local(x_in, xf.at[xrows])
    ct = local(t_in.at[:, tcols], tf.at[c])
    wo4[c] = wo_in[...]
    for i, ref in enumerate((ob_in, g1_in, b1_in, db_in, g2_in, b2_in, qb_in, vb_in)):
        vec[c, i : i + 1, :] = ref[...].reshape(1, C)
    ub[c, 0:1, :] = jnp.concatenate([ub_in[i : i + 1] for i in range(6)], axis=1)
    own_qkv = [w[...] for w in (wq_in, wk_in, wv_in)]
    own_qkv = jnp.concatenate(
        [w[:, h * HD : (h + 1) * HD] for h in range(HEADS) for w in own_qkv], axis=1
    )
    own_qkv = jnp.where(d == 0, own_qkv[:, 0:QH], own_qkv[:, QH:])
    wq2[d, r] = jnp.concatenate([own_qkv, jnp.zeros((RB, HW - QH), bf16)], axis=1)
    pl.semaphore_wait(bar, 10)

    def along_a(ref, whole):
        return triple(whole, lambda k: ref, lambda k: ref, adev)

    def of_b(ref):
        return lambda at, k: ref(ridx(lax.rem(a_me + 4 - k, 4), b_at[at]))

    def direct_b(ref, whole):
        return DirectGather(links, of_b(ref), whole, (bdev(1), bdev(3), bdev(2)))

    def wq_ref(i):
        return wq2.at[d, i]

    def wo_ref(i):
        return wo2.at[d, i]

    def wa_ref(i):
        return wa.at[d, i]

    def wb_ref(i):
        return wb.at[d, i, :, cols(c, FB)]

    def some(buf):
        return lambda n: buf.at[d, pl.ds(0, n)]

    def some_b(n):
        return wb.at[d, pl.ds(0, n), :, cols(c, FB)]

    class ToSibling:
        def __init__(self, whole):
            self.batch = links.batch(whole)

        def send(self, ref):
            self.batch.send(ref, ref, sib)

        def wait(self):
            self.batch.wait_recv()

    wq_a = along_a(wq_ref(r), some(wq2)(3))
    wq_b = direct_b(wq_ref, some(wq2))
    wq_b.send(0)
    cup.wait()
    cdn.wait()
    wz = triple(
        wa.at[d, 0, :, pl.ds(0, 3 * FA)],
        lambda k: wown.at[d, :, pl.ds(0, FA)],
        lambda k: wa.at[d, r, :, cols(c, FA)],
        zdev,
    )
    cx.wait()
    x_z = RingGather(
        links,
        lambda at, half: xf.at[rows(2 * c_at[at] + half, C // 2)],
        lambda n: xf.at[pl.ds(0, n * C // 2)],
        zdev(1), zdev(3), (0,), (1,),
    )
    x_z.first()
    oz = triple(wo4.at[pl.ds(0, 3)], lambda k: wo4.at[c], lambda k: wo4.at[c], zdev)
    vz = triple(vec.at[pl.ds(0, 3)], lambda k: vec.at[c], lambda k: vec.at[c], zdev)
    uz = triple(
        ub.at[pl.ds(0, 3), 0:1], lambda k: ub.at[c, 0:1], lambda k: ub.at[c, 0:1], zdev
    )
    wa[d, r, :, cols(c, FA)] = wown[d, :, 0:FA]
    wb[d, r, :, cols(c, FB)] = wown[d, :, FA:]
    wb_a = along_a(wb_ref(r), some_b(3))
    wb_b = direct_b(wb_ref, some_b)
    wb_b.send(0)

    wq_a.wait_recv()
    for k in (1, 3, 2):
        wq_b.send(k)
    wq_s = ToSibling(wq2.at[d])
    for j in range(4):
        wq_s.send(wq_ref(ridx(j, b_me)))
    wb_a.wait_recv()
    for k in (1, 3, 2):
        wb_b.send(k)
    x_z.rest()
    wz.wait_recv()
    wa_a = [links.batch(wa_ref(0)) for _ in range(3)]
    for i, k in enumerate((1, 3, 2)):
        wa_a[i].send(wa_ref(r), wa_ref(r), adev(k))
    wa_b = RingGather(links, of_b(wa_ref), some(wa), bdev(1), bdev(3), (0, 2), (1, 3))
    wa_b.send(0)
    oz.wait_recv()
    own_wo = jnp.concatenate([wo4[j] for j in range(4)], axis=1)
    wo2[d, r] = jnp.where(d == 0, own_wo[:, 0:HW], own_wo[:, HW:])
    wo_a = along_a(wo_ref(r), some(wo2)(3))
    wo_b = direct_b(wo_ref, some(wo2))
    wo_b.send(0)
    wq_b.batch.wait_recv()
    for at in ("left", "right", "far"):
        for k in range(4):
            wq_s.send(wq_b.ref(at, k))
    x_z.forward()
    wo_s = ToSibling(wo2.at[d])
    wo_s.send(wo_ref(r))
    wa_s = ToSibling(wa.at[d])
    wa_s.send(wa_ref(r))
    for i, k in enumerate((1, 3, 2)):
        wa_a[i].wait_recv()
        wa_b.send(k)
        wa_s.send(wa_b.ref("me", k))
    wo_a.wait_recv()
    for k in (1, 3, 2):
        wo_b.send(k)
        wo_s.send(wo_b.ref("me", k))
    vown = transposed(vec[c])
    length = len_in[0]

    for at in ("left", "right", "far"):
        x_z.wait(at)
    wb_b.batch.wait_recv()

    def wb_z(at, half):
        return wb.at[d, pl.ds(half * 8, 8), :, cols(c_at[at], FB)]

    def some_z(n):
        return wb.at[d, pl.ds(0, 8), :, pl.ds(0, n * FB)]

    wb_zg = RingGather(links, wb_z, some_z, zdev(1), zdev(3), (0,), (1,))
    wb_zg.first()
    wb_s = ToSibling(wb.at[d])
    wb_s.send(wb.at[d, :, :, cols(c, FB)])
    wq_s.wait()
    w_low = transposed(wq2[0].reshape(D, HW))[0:QH]
    w_high = transposed(wq2[1].reshape(D, HW))[0:QH]
    dxp[0, :, 0:D] = w_low[0:C]
    dxp[1, 0 : QH - C, 0:D] = w_low[C:]
    dxp[1, QH - C :, 0:D] = w_high[0 : QH - C]
    dxp[2, :, 0:D] = w_high[QH - C :]
    q_bias = vown[:, 6:7]
    v_bias = vown[:, 7:8]
    lane_iota = lax.broadcasted_iota(jnp.int32, (1, TOK), 1)
    first_row = lax.broadcasted_iota(jnp.int32, (HD, TOK), 0) == 0

    def qkv_chunk(i, carry):
        at = cols(i, TOK)
        tok = xf[:, at]
        qkv = mm(dxp[:, :, 0:D].reshape(3 * C, D), tok)
        bias = jnp.where(lane_iota + i * TOK < length, 0.0, MASK)
        bias = jnp.where(first_row, jnp.broadcast_to(bias, (HD, TOK)), 0.0).astype(bf16)
        ones = jnp.where(first_row, 1.0, 0.0).astype(bf16)
        for h in range(HEADS):
            hs = slice(h * HD, (h + 1) * HD)
            of = h * C
            q = (qkv[of : of + HD] + q_bias[hs]).astype(bf16)
            q = (q.astype(f32) * (HD**-0.5)).astype(bf16)
            k = qkv[of + HD : of + 2 * HD].astype(bf16)
            v = (qkv[of + 2 * HD : of + 3 * HD] + v_bias[hs]).astype(bf16)
            qkvt[h * HD : (h + 1) * HD, at] = q
            qkvt[C + h * HD : C + (h + 1) * HD, at] = k
            qaug[h, 0:HD, at] = q
            qaug[h, HD : 2 * HD, at] = ones
            vaug[h, 0:HD, at] = v
            vaug[h, HD : HD + 16, at] = ones[0:16]
            ktm[h, at, :] = transposed(jnp.concatenate([k, bias], axis=0))
            vtm[h, at, :] = transposed(jnp.concatenate([v, ones], axis=0))
        return carry

    unrolled(4, qkv_chunk, 0)
    wb_zg.rest()

    def fwd_head(h):
        score = mm(ktm[h], qaug[h, :, 0:WT])
        for n in range(LEN // WT):
            at = cols(n, WT)
            later = mm(ktm[h], qaug[h, :, cols(n + 1, WT)]) if (n + 1) * WT < LEN else None
            top = jnp.max(score, axis=0, keepdims=True)
            probs = jnp.exp(score - top).astype(bf16)
            pst[h, :, at] = probs
            both = mm(vaug[h], probs)
            inv = 1.0 / both[HD : HD + 1]
            linv[h, 0:1, at] = inv
            ctxt[h * HD : (h + 1) * HD, at] = (both[0:HD] * inv).astype(bf16)
            score = later

    cc = links.batch(ctxa.at[pl.ds(0, 3)])

    def context_out(h):
        hrow = pl.ds(h * HD, HD)
        ctxa[c, hrow] = ctxt[hrow, tcols]
        for k in (1, 3, 2):
            there = cols(lax.rem(c + k, 4), TOK)
            cc.send(ctxt.at[hrow, there], ctxa.at[c, hrow], zdev(k))

    def pass_on(ring, sent, at):
        ring.wait(at)
        for k in range(4):
            sent.send(ring.ref(at, k))

    fwd_head(0)
    context_out(0)
    wa_b.forward()
    pass_on(wa_b, wa_s, "left")
    pass_on(wa_b, wa_s, "right")
    fwd_head(1)
    context_out(1)
    wo_b.batch.wait_recv()
    for at in ("left", "right", "far"):
        for k in range(4):
            wo_s.send(wo_b.ref(at, k))
    wait_all((vz, uz))
    for i in range(4):
        vcol[i * C : (i + 1) * C, 0:16] = transposed(vec[i])
    fwd_head(2)
    context_out(2)
    wb_zg.forward()
    pass_on(wa_b, wa_s, "far")
    for i in range(2):
        wqkv[:, i * QH : (i + 1) * QH] = wq2[i].reshape(D, HW)[:, 0:QH]
    wo_s.wait()
    cc.wait_recv()
    ct.wait()
    tt = triple(
        tf.at[pl.ds(0, 3)],
        lambda k: t_in.at[:, cols(lax.rem(c + k, 4), TOK)],
        lambda k: tf.at[c],
        zdev,
    )

    acc = xf[:, tcols].astype(f32) + vcol[:, 0:1]
    for j in range(2):
        w = wo2[j].reshape(D, HW)
        acc = acc + mm(w, ctxa[2 * j : 2 * j + 2].reshape(HW, TOK))
    hid[...] = acc

    def norm_stats(ref):
        v = ref[...]
        mean = jnp.sum(v, axis=0, keepdims=True) * (1.0 / D)
        square = jnp.sum(v * v, axis=0, keepdims=True) * (1.0 / D)
        return mean, lax.rsqrt(square - mean * mean + EPS)

    mean1, inv1 = norm_stats(hid)

    def norm1(i, carry):
        row = rows(i, C)
        n = (hid[row] - mean1) * inv1
        nrm[row] = n
        h = n * vcol[row, 1:2] + vcol[row, 2:3]
        hid[row] = h + vcol[row, 3:4]
        astore[0, row] = h.astype(bf16)
        return carry

    unrolled(4, norm1, 0)
    outt[...] = transposed(astore[0])
    for at in ("left", "right"):
        wb_zg.wait(at)
        wb_s.send(wb.at[d, :, :, cols(c_at[at], FB)])

    wa_s.wait()

    def w_chunk(ref, i):
        return ref[:, :, cols(i, WF)].reshape(D, WF)

    def store_halves(w, chunk, v):
        if isinstance(chunk, int) and chunk == 2:
            for j in range(4):
                for half in range(2):
                    at = j * FB + half * FB // 2
                    to = 4 * FA // 2 + j * FB // 2
                    bstore[w, half, :, to : to + FB // 2] = v[:, at : at + FB // 2]
        else:
            for j in range(2):
                for half in range(2):
                    at = j * FA + half * FA // 2
                    bstore[w, half, :, cols(2 * chunk + j, FA // 2)] = v[:, at : at + FA // 2]

    def load_halves(w, chunk):
        if isinstance(chunk, int) and chunk == 2:
            return jnp.concatenate(
                [
                    bstore[w, half, :, 2 * FA + j * FB // 2 : 2 * FA + (j + 1) * FB // 2]
                    for j in range(4)
                    for half in range(2)
                ],
                axis=1,
            )
        return jnp.concatenate(
            [bstore[w, half, :, cols(2 * chunk + j, FA // 2)] for j in range(2) for half in range(2)],
            axis=1,
        )

    def up_of(ref, bias, first):
        def up_chunk(i, carry):
            at = cols(first + i, WF)
            pre = mm(outt[...], w_chunk(ref, i)) + bias(i)
            half = 0.5 * (1.0 + lax.erf(pre * ROOT_HALF))
            store_halves(1, first + i, (pre * half).astype(bf16))
            slope[:, at] = (half + pre * jnp.exp(-0.5 * pre * pre) * INV_ROOT_TAU).astype(bf16)
            return carry

        return up_chunk

    def bias_a(i):
        return jnp.concatenate([ub[2 * i, 0:1, 0:FA], ub[2 * i + 1, 0:1, 0:FA]], axis=1)

    def bias_b(i):
        return jnp.concatenate([ub[j, 0:1, FA:] for j in range(4)], axis=1)

    lax.fori_loop(0, 2, up_of(wa.at[0], bias_a, 0), 0)
    wb_zg.wait("far")
    wb_s.send(wb.at[d, :, :, cols(c_at["far"], FB)])

    def down_of(ref, first):
        def down_chunk(i, carry):
            hid[...] = hid[...] + mt(w_chunk(ref, i), load_halves(1, first + i))
            return carry

        return down_chunk

    lax.fori_loop(0, 2, down_of(wa.at[1], 0), 0)
    wb_s.wait()
    unrolled(1, up_of(wb.at[0], bias_b, 2), 0)
    unrolled(1, down_of(wb.at[1], 2), 0)

    mean2, inv2 = norm_stats(hid)
    tt.wait_recv()
    valid = lane_iota + c * TOK < length
    gcol[...] = jnp.zeros(gcol.shape, f32)
    sv[...] = jnp.zeros(sv.shape, f32)

    def norm2(i, carry):
        total, crossed, loss = carry
        row = rows(i, C)
        n = (hid[row] - mean2) * inv2
        hid[row] = n
        final = n * vcol[row, 4:5] + vcol[row, 5:6]
        delta[row] = final.astype(bf16)
        g = jnp.where(valid, final - tf[i].astype(f32), 0.0)
        gcol[row, 4:5] = jnp.sum(g * n, axis=1, keepdims=True)
        gcol[row, 5:6] = jnp.sum(g, axis=1, keepdims=True)
        s = g * vcol[row, 4:5]
        sg[row] = s
        return (
            total + jnp.sum(s, axis=0, keepdims=True),
            crossed + jnp.sum(s * n, axis=0, keepdims=True),
            loss + jnp.sum(g * g, axis=0, keepdims=True),
        )

    zero = jnp.zeros((1, TOK), f32)
    total2, crossed2, loss_row = unrolled(4, norm2, (zero, zero, zero))
    out_o_own = local(delta.at[xrows], out_o.at[:, tcols])
    fo = triple(
        delta.at[pl.ds(0, 3 * C)],
        lambda k: delta.at[rows(lax.rem(c + k, 4), C)],
        lambda k: out_o.at[:, tcols],
        zdev,
    )

    def norm2_back(i, carry):
        row = rows(i, C)
        s = inv2 * (sg[row] - total2 * (1.0 / D) - hid[row] * (crossed2 * (1.0 / D)))
        sg[row] = s
        low = s.astype(bf16)
        astore[1, row] = low
        gcol[row, 3:4] = jnp.sum(low.astype(f32), axis=1, keepdims=True)
        return carry

    unrolled(4, norm2_back, 0)

    def exchange(w):
        return [
            links.send(astore.at[w], arecv.at[w], sib),
            links.send(bstore.at[w, e], brecv.at[w], sib),
        ]

    ex_down = exchange(1)
    outt[...] = transposed(astore[1])

    def act_of(ref, first):
        def act_chunk(i, carry):
            at = cols(first + i, WF)
            g = mm(outt[...], w_chunk(ref, i)) * slope[:, at].astype(f32)
            low = g.astype(bf16)
            store_halves(0, first + i, low)
            total = jnp.sum(low.astype(f32), axis=0, keepdims=True)
            sv[pl.ds(8 + 2 * (first + i), 1), 0:FA] = total[:, 0:FA]
            sv[pl.ds(9 + 2 * (first + i), 1), 0:FA] = total[:, FA:]
            return carry

        return act_chunk

    unrolled(1, act_of(wb.at[1], 2), 0)
    lax.fori_loop(0, 2, act_of(wa.at[1], 0), 0)
    ex_up = exchange(0)

    def back_of(ref, first):
        def back_chunk(i, carry):
            sg[...] = sg[...] + mt(w_chunk(ref, i), load_halves(0, first + i))
            return carry

        return back_chunk

    def sum_b(own, mid, recv):
        return RingSum(
            links, lambda at, j: own(ridx(j, b_at[at])), mid, recv, bdev(1), bdev(3), 4
        )

    def direct_sum(own, recv):
        return DirectSum(
            links, lambda at, j: own(ridx(j, b_at[at])), recv, (bdev(1), bdev(3), bdev(2))
        )

    def end_b(ring, summed, peer_recv):
        for j in range(4):
            summed[j] = ring.total(j).astype(bf16)
        return triple(
            peer_recv,
            lambda k: summed.at[lax.rem(a_me + k, 4)],
            lambda k: peer_recv.at[k - 1],
            adev,
        )

    def end_a(sends, summed, recv):
        sends.wait_recv()
        total = summed[a_me].astype(f32)
        for k in range(3):
            total = total + recv[k].astype(f32)
        return total

    def add_sibling(ref, other):
        def add(i, carry):
            ref[d, i] = (ref[d, i].astype(f32) + other[i].astype(f32)).astype(bf16)
            return carry

        unrolled(16, add, 0)

    def weight_grad(w):
        for at, ref in ((0, ga), (2 * FA, gb)):
            for lo in range(0, ref.shape[3], FA):
                cut = pl.ds(at + lo, FA)
                g = mm(astore[w], bstore[w, d, :, cut]) + mm(arecv[w], brecv[w, :, cut])
                ref[w, :, :, lo : lo + FA] = g.astype(bf16).reshape(16, RB, FA)

        def z_own(at, half):
            return gb.at[w, pl.ds(half * 8, 8), :, cols(c_at[at], FB // 2)]

        a_ring = sum_b(lambda i: ga.at[w, i], im.at[w], rm.at[w])
        b_ring = RingSum(links, z_own, zi.at[w], zr.at[w], zdev(1), zdev(3), 2)
        a_ring.first()
        b_ring.first()
        return a_ring, b_ring

    unrolled(1, back_of(wb.at[0], 2), 0)
    wait_all(ex_down)
    wd_a, wd_b = weight_grad(1)
    lax.fori_loop(0, 2, back_of(wa.at[0], 0), 0)

    def hidden_back(i, carry):
        total, crossed = carry
        row = rows(i, C)
        g = sg[row]
        n = nrm[row]
        gcol[row, 1:2] = jnp.sum(g * n, axis=1, keepdims=True)
        gcol[row, 2:3] = jnp.sum(g, axis=1, keepdims=True)
        s = g * vcol[row, 1:2]
        sg[row] = s
        return (
            total + jnp.sum(s, axis=0, keepdims=True),
            crossed + jnp.sum(s * n, axis=0, keepdims=True),
        )

    total1, crossed1 = unrolled(4, hidden_back, (zero, zero))

    def norm1_back(i, carry):
        row = rows(i, C)
        s = inv1 * (sg[row] - total1 * (1.0 / D) - nrm[row] * (crossed1 * (1.0 / D)))
        sg[row] = s
        low = s.astype(bf16)
        delta[row] = low
        gcol[row, 0:1] = jnp.sum(low.astype(f32), axis=1, keepdims=True)
        return carry

    fo.wait_send()
    out_o_own.wait()
    unrolled(4, norm1_back, 0)
    outt[...] = transposed(delta[...])
    wd_a.direct()

    dc = []
    for i in range(2):
        part = transposed(mm(outt[...], wo2[i].reshape(D, HW)).astype(bf16))
        dct[2 * i : 2 * i + 2] = part.reshape(2, C, TOK)
    dctx[:, tcols] = dct[c]
    for h in range(HEADS):
        hrow = pl.ds(h * HD, HD)
        dc.append(
            triple(
                dct.at[0],
                lambda k: dct.at[lax.rem(c + k, 4), hrow],
                lambda k: dctx.at[hrow, tcols],
                zdev,
            )
        )

    sv[0:8] = transposed(gcol[...])[0:8]
    sv[6:7] = jnp.broadcast_to(jnp.sum(loss_row, axis=1, keepdims=True), (1, D))
    sv[7:8] = jnp.broadcast_to(length.astype(f32), (1, D))
    v_sent = [links.send(sv, rsv.at[0], sib)]
    v_from = [(0, 1)]

    def sv_add():
        v_sent.pop().wait()
        lo, n = v_from[-1]
        total = sv[...]
        for i in range(n):
            total = total + rsv[lo + i]
        sv[...] = total

    def sv_send(dev):
        lo = sum(v_from[-1])
        v_from.append((lo, 3))
        v_sent.append(
            triple(
                rsv.at[pl.ds(lo, 3)], lambda k: sv, lambda k: rsv.at[lo + k - 1], dev
            )
        )

    wait_all(ex_up)
    wd_b.direct()
    wu_a, wu_b = weight_grad(0)
    sv_add()
    sv_send(bdev)
    g = mt(delta[...], ctxa[...].reshape(D, TOK)).astype(bf16)
    for i in range(2):
        gao[i] = g[:, i * HW : (i + 1) * HW].reshape(16, RB, HW)
    go_x = links.send(gao.at[e], gor, sib)
    wd_a.middle()
    wd_b.middle()

    def bwd_head(h, meanwhile=None):
        hrow = pl.ds(h * HD, HD)
        krow = pl.ds(C + h * HD, HD)
        of = h * C

        dk = dv = jnp.zeros((HD, LEN), f32)
        for n in range(LEN // WT):
            at = cols(n, WT)
            inv = linv[h, 0:1, at]
            dc = dctx[hrow, at].astype(f32)
            inner = jnp.sum(dc * ctxt[hrow, at].astype(f32), axis=0, keepdims=True) * inv
            dcs = (dc * inv).astype(bf16)
            probs = pst[h, :, at]
            dv = dv + mt(dcs, probs)
            dp = mm(vtm[h, :, 0:HD], dcs) - inner
            ds = (probs.astype(f32) * dp).astype(bf16)
            dk = dk + mt(qkvt[hrow, at], ds)
            dqkvt[of : of + HD, at] = (mm(qkvt[krow, :], ds) * (HD**-0.5)).astype(bf16)
            if n == 0 and meanwhile is not None:
                meanwhile()
        dqkvt[of + HD : of + 2 * HD] = dk.astype(bf16)
        dqkvt[of + 2 * HD : of + 3 * HD] = dv.astype(bf16)

    spare = HL - QC
    row_iota = lax.broadcasted_iota(jnp.int32, (RB, spare), 0)

    def qkv_grad(h, ref, at):
        of = dqkvt[h * C : (h + 1) * C]
        g = mt(xf[...], of).astype(bf16)
        sums = mt(jnp.ones((8, LEN), bf16), of)[0:1]
        for half in range(2):
            lo = half * QC
            part_rows = jnp.zeros((RB, spare), f32)
            for j in range(3):
                part = sums[:, lo + j * spare : lo + (j + 1) * spare]
                part_rows = jnp.where(row_iota == j, jnp.broadcast_to(part, (RB, spare)), part_rows)
            ref[half, :, :, at : at + QC] = g[:, lo : lo + QC].reshape(16, RB, QC)
            ref[half, :, :, at + QC : at + HL] = jnp.broadcast_to(
                part_rows.astype(bf16)[None], (16, RB, spare)
            )

    dc[0].wait_recv()
    bwd_head(0)
    wu_a.direct()
    wu_b.direct()
    go_x.wait_recv()
    add_sibling(gao, gor)
    o_sum = direct_sum(lambda i: gao.at[d, i], ro)
    o_sum.start()
    dc[1].wait_recv()
    bwd_head(1, lambda: qkv_grad(0, gqa, 0))
    wd_sends = end_b(wd_a, s1.at[1], r2.at[1])
    wu_a.middle()
    wu_b.middle()

    def total_z(w, ring):
        for half in range(2):
            sb0[w, half * 8 : half * 8 + 8] = ring.total(half).astype(bf16)
        ring_b = direct_sum(lambda i: sb0.at[w, i], br.at[w])
        ring_b.start()
        return ring_b

    sv_add()
    sv_send(adev)
    dc[2].wait_recv()
    bwd_head(2, lambda: qkv_grad(1, gqa, HL))

    def dx_part(i):
        row = rows(i, C)
        gi_o[...] = mm(wqkv[row], dqkvt[...])
        gi_o[:, tcols] = gi_o[:, tcols] + sg[row]

    SLOT = {"far": 0, "right": 1, "left": 2}

    def dx_own(at, half):
        return dxp.at[SLOT[at], pl.ds(half * (C // 2), C // 2)]

    dx_sum = RingSum(links, dx_own, rxi, rx, zdev(1), zdev(3), 2)
    dx_part(c_at["far"])
    dxp[0] = gi_o[...].astype(bf16)
    dx_sum.first()
    xa = links.send(gqa.at[e], gra, sib)
    qkv_grad(2, gqb, 0)
    xb = links.send(gqb.at[e], grb, sib)

    dx_part(c_at["right"])
    dxp[1] = gi_o[...].astype(bf16)
    dx_sum.direct_right()
    dx_part(c_at["left"])
    dxp[2] = gi_o[...].astype(bf16)
    dx_sum.direct_left()
    xa.wait_recv()
    add_sibling(gqa, gra)
    qa_sum = direct_sum(lambda i: gqa.at[d, i], rqa)
    qa_sum.start()
    xb.wait_recv()
    add_sibling(gqb, grb)
    qb_sum = direct_sum(lambda i: gqb.at[d, i], rqb)
    qb_sum.start()
    bd_sum = total_z(1, wd_b)
    dx_part(c)
    o_sends = end_b(o_sum, so1, ro2)

    def along_z(w, sends):
        s2[w] = end_a(sends, s1.at[w], r2.at[w]).astype(bf16)
        return triple(
            r3.at[w],
            lambda k: s2.at[w, :, cols(lax.rem(c + k, 4), FA // 2)],
            lambda k: r3.at[w, k - 1],
            zdev,
        )

    w3 = {1: along_z(1, wd_sends)}
    wu_sends = end_b(wu_a, s1.at[0], r2.at[0])
    dx_sum.middle()
    bu_sum = total_z(0, wu_b)
    sv_add()
    sv_send(zdev)
    bd_sends = end_b(bd_sum, sb1.at[1], rb2.at[1])
    qa_sends = end_b(qa_sum, sqa, ra2)
    qb_sends = end_b(qb_sum, sqb, rb3)
    so2[0] = end_a(o_sends, so1, ro2).astype(bf16)
    o_x = links.send(so2.at[0], so2.at[1], sib)
    w3[0] = along_z(0, wu_sends)
    bu_sends = end_b(bu_sum, sb1.at[0], rb2.at[0])
    o_x.wait_recv()
    mine, other = so2[0], so2[1]
    low, high = jnp.where(d == 0, mine, other), jnp.where(d == 0, other, mine)
    so4[0], so4[1] = low[:, 0:C], low[:, C:]
    so4[2], so4[3] = high[:, 0:C], high[:, C:]
    o3 = triple(
        ro3, lambda k: so4.at[lax.rem(c + k, 4)], lambda k: ro3.at[k - 1], zdev
    )
    xb1[0, 1] = end_a(bd_sends, sb1.at[1], rb2.at[1])
    xq1[0, :, 0 : 2 * HL] = end_a(qa_sends, sqa, ra2)
    xq1[0, :, 2 * HL :] = end_a(qb_sends, sqb, rb3)
    q3 = links.send(xq1.at[0], xq1.at[1], sib)
    xb1[0, 0] = end_a(bu_sends, sb1.at[0], rb2.at[0])
    wb4 = links.send(xb1.at[0], xb1.at[1], sib)
    wait_all((w3[1], w3[0]))
    x1[0] = s2[:, :, cols(c, FA // 2)].astype(f32)
    for w in range(2):
        for k in range(3):
            x1[0, w] = x1[0, w] + r3[w, k].astype(f32)
    w4 = links.send(x1.at[0], x1.at[1], sib)
    o3.wait_recv()
    ototal = so4[c].astype(f32)
    for k in range(3):
        ototal = ototal + ro3[k].astype(f32)
    dwo_o[...] = ototal
    sv_add()
    sv_o[...] = sv[...]
    w4.wait_recv()
    dwa_o[d] = x1[0]
    dwa_o[e] = x1[1]
    q3.wait_recv()
    dqkv_o[d] = xq1[0]
    dqkv_o[e] = xq1[1]
    wb4.wait_recv()
    dwb_o[d] = xb1[0]
    dwb_o[e] = xb1[1]
    dx_sum.wait()
    for half in range(2):
        row = pl.ds(half * (C // 2), C // 2)
        gi_o[row] = gi_o[row] + rx[0, half].astype(f32) + rx[1, half].astype(f32)
    for copy in links.all:
        copy.wait()


def finish(
    out_i, gi_i, dwa_i, dwb_i, dwo_i, dqkv_i, sv_i,
    out, loss, gi, gwq, gbq, gwk, gwv, gbv, gwo, gob, gg1, gb1, gup, gub, gdn, gdb, gg2, gb2,
):
    c = lax.axis_index("col")
    out[...] = out_i[...]
    count = sv_i[7:8, 0:1] * 0.25
    factor = SLOTS / count
    loss[0] = jnp.sum(sv_i[6:7, 0:1] / (2.0 * D * count))
    gi[...] = gi_i[...] * factor
    low, high = dqkv_i[0] * factor, dqkv_i[1] * factor
    at = [h * HL for h in range(HEADS)]
    gwq[...] = jnp.concatenate([low[:, i : i + HD] for i in at], axis=1)
    parts = []
    for i in at:
        parts += [low[:, i + HD : i + QC], high[:, i : i + QC - HD]]
    gwk[...] = jnp.concatenate(parts, axis=1)
    gwv[...] = jnp.concatenate([high[:, i + QC - HD : i + QC] for i in at], axis=1)
    gbq[...] = jnp.concatenate([low[j : j + 1, i + QC : i + HL] for i in at for j in (0, 1)], axis=1)
    gbv[...] = jnp.concatenate([high[j : j + 1, i + QC : i + HL] for i in at for j in (1, 2)], axis=1)
    gwo[...] = dwo_i[...] * factor
    for i, ref in enumerate((gup, gdn)):
        for half in range(2):
            ref[:, half * FA // 2 : (half + 1) * FA // 2] = dwa_i[half, i] * factor
            at = FA + half * FB // 2
            ref[:, at : at + FB // 2] = dwb_i[half, i] * factor
    sums = sv_i[...] * factor
    for j in range(4):

        @pl.when(c == j)
        def _(j=j):
            for i in range(4):
                gub[i : i + 1] = sums[8 + j : 9 + j, i * 128 : (i + 1) * 128]
            for i in range(2):
                at = (j % 2) * FB + i * 128
                gub[4 + i : 5 + i] = sums[12 + j // 2 : 13 + j // 2, at : at + 128]
            for i, ref in enumerate((gob, gg1, gb1, gdb, gg2, gb2)):
                ref[...] = sums[i : i + 1, j * C : (j + 1) * C]


def local_step(
    inputs, teacher, lengths, query_weight, query_bias, key_weight, value_weight, value_bias,
    output_weight, output_bias, first_gain, first_shift, up_weight, up_bias, down_weight,
    down_bias, second_gain, second_shift,
):
    anyspec = pl.BlockSpec(memory_space=pl.ANY)
    vm = pl.BlockSpec(memory_space=pltpu.VMEM)
    sds = jax.ShapeDtypeStruct
    V = pltpu.VMEM
    vectors = [
        v.reshape(1, -1)
        for v in (
            output_bias, first_gain, first_shift, down_bias, second_gain, second_shift,
            query_bias, value_bias,
        )
    ]
    vectors.append(up_bias.reshape(6, 128))
    got = pl.pallas_call(
        layer,
        name="layer",
        out_shape=(
            sds((C, LEN), bf16),
            sds((C, LEN), f32),
            sds((2, 2, RB, FA // 2), f32),
            sds((2, 2, RB, FB // 2), f32),
            sds((RB, C), f32),
            sds((2, RB, HW), f32),
            sds((16, D), f32),
        ),
        in_specs=[anyspec, anyspec, pl.BlockSpec(memory_space=pltpu.SMEM)]
        + [vm] * 4
        + [anyspec] * 2
        + [vm] * 9,
        out_specs=(anyspec, vm, vm, vm, vm, vm, vm),
        scratch_shapes=[
            V((D, LEN), bf16),
            V((4, C, TOK), bf16),
            V((2, 16, RB, 4 * FA), bf16),
            V((2, 16, RB, 4 * FB), bf16),
            V((2, 16, RB, HW), bf16),
            V((2, 16, RB, HW), bf16),
            V((4, RB, C), bf16),
            V((D, 3 * C), bf16),
            V((4, 16, C), f32),
            V((4, 8, D), f32),
            V((D, 128), f32),
            V((2 * C, LEN), bf16),
            V((HEADS, LEN, 2 * HD), bf16),
            V((HEADS, 2 * HD, LEN), bf16),
            V((HEADS, HD + 16, LEN), bf16),
            V((HEADS, LEN, 2 * HD), bf16),
            V((HEADS, LEN, LEN), bf16),
            V((HEADS, 8, LEN), f32),
            V((C, LEN), bf16),
            V((4, C, TOK), bf16),
            V((D, TOK), f32),
            V((D, TOK), f32),
            V((D, TOK), f32),
            V((2, 2, TOK, FF // 2), bf16),
            V((2, D, TOK), bf16),
            V((TOK, FF), bf16),
            V((2, TOK, FF // 2), bf16),
            V((2, D, TOK), bf16),
            V((2, 16, RB, 2 * FA), bf16),
            V((2, 16, RB, 2 * FB), bf16),
            V((2, 16, RB, 2 * HL), bf16),
            V((2, 16, RB, HL), bf16),
            V((16, RB, 2 * HL), bf16),
            V((16, RB, HL), bf16),
            V((2, 16, RB, HW), bf16),
            V((16, RB, HW), bf16),
            V((C, LEN), bf16),
            V((4, C, TOK), bf16),
            V((TOK, D), bf16),
            V((D, TOK), bf16),
            V((3 * C, LEN), bf16),
            V((3, C, LEN), bf16),
            V((2, C // 2, LEN), bf16),
            V((2, 2, C // 2, LEN), bf16),
            V((2, 4, RB, 2 * FA), bf16),
            V((2, 2, 4, RB, 2 * FA), bf16),
            V((2, 4, RB, 2 * FA), bf16),
            V((2, 3, RB, 2 * FA), bf16),
            V((2, RB, 2 * FA), bf16),
            V((2, 3, RB, FA // 2), bf16),
            V((2, 2, 8, RB, FB // 2), bf16),
            V((2, 2, 2, 8, RB, FB // 2), bf16),
            V((2, 16, RB, FB // 2), bf16),
            V((2, 3, 4, RB, FB // 2), bf16),
            V((2, 4, RB, FB // 2), bf16),
            V((2, 3, RB, FB // 2), bf16),
            V((3, 4, RB, 2 * HL), bf16),
            V((3, 4, RB, HL), bf16),
            V((4, RB, 2 * HL), bf16),
            V((4, RB, HL), bf16),
            V((3, RB, 2 * HL), bf16),
            V((3, RB, HL), bf16),
            V((3, 4, RB, HW), bf16),
            V((4, RB, HW), bf16),
            V((3, RB, HW), bf16),
            V((2, RB, HW), bf16),
            V((4, RB, C), bf16),
            V((3, RB, C), bf16),
            V((2, 2, RB, FA // 2), f32),
            V((2, 2, RB, FB // 2), f32),
            V((2, RB, HW), f32),
            V((D, 128), f32),
            V((16, D), f32),
            V((10, 16, D), f32),
            V((2, RB, D), bf16),
            pltpu.SemaphoreType.DMA((12,)),
            pltpu.SemaphoreType.DMA((N_SEM,)),
            pltpu.SemaphoreType.DMA((N_SEM,)),
        ],
        compiler_params=pltpu.CompilerParams(
            collective_id=0, has_side_effects=True, vmem_limit_bytes=62 * 2**20
        ),
    )(
        inputs, teacher, lengths, query_weight, key_weight, value_weight, output_weight.T,
        up_weight, down_weight, *vectors,
    )
    vector = sds((1, C), f32)
    weight = sds((RB, C), f32)
    wide = sds((RB, D), f32)
    done = pl.pallas_call(
        finish,
        name="finish",
        out_shape=(
            sds((C, LEN), bf16), sds((1,), f32), sds((C, LEN), f32),
            weight, vector, weight, weight, vector, weight,
            vector, vector, vector, wide, sds((6, 128), f32), wide, vector, vector, vector,
        ),
        in_specs=[vm] * 7,
        out_specs=(vm, pl.BlockSpec(memory_space=pltpu.SMEM)) + (vm,) * 16,
    )(*got)
    shapes = [
        (C, LEN), (), (C, LEN), (RB, C), (C,), (RB, C), (RB, C), (C,), (RB, C), (C,), (C,), (C,),
        (RB, D), (D,), (RB, D), (C,), (C,), (C,),
    ]
    done = [o.reshape(shape) for o, shape in zip(done, shapes)]
    done[8] = done[8].T
    return tuple(done)


def solution(mesh):
    split = Mesh(
        mesh.devices.reshape(mesh.shape["dp"], 4, 4, mesh.shape["col"]), AXES
    )
    tokens = P("col", DP_ROW)
    weight = P(ROW, "col")
    vector = P("col")
    return jax.shard_map(
        local_step,
        mesh=split,
        in_specs=(
            tokens, tokens, P(DP_ROW), weight, vector, weight, weight, vector,
            P("col", ROW), vector, vector, vector, weight, vector, weight,
            vector, vector, vector,
        ),
        out_specs=(
            tokens, P(), tokens, weight, vector, weight, weight, vector,
            P("col", ROW), vector, vector, vector, weight, vector, weight,
            vector, vector, vector,
        ),
        check_vma=False,
    )
```

```python
import jax
import jax.numpy as jnp
from jax import lax
from jax.experimental import pallas as pl
from jax.experimental.pallas import tpu as pltpu
from jax.sharding import Mesh
from jax.sharding import PartitionSpec as P

D = 768
FF = 3072
LEN = 1024
HD = 64
HEADS = 3
C = 192
TOK = 256
RB = 48
SLOTS = 32768
EPS = 1e-12
MASK = -1e30
ROOT_HALF = 0.7071067811865476
INV_ROOT_TAU = 0.3989422804014327
AXES = ("dp", "row_0", "row_1", "col")
ROW = ("row_0", "row_1")
DP_ROW = ("dp", "row_0", "row_1")
N_SEM = 96
HL = 128
QC = 96
FA = 512
FB = 256
WT = 512
QH = 288
HW = 384
f32 = jnp.float32
bf16 = jnp.bfloat16


def mm(a, b):
    return lax.dot_general(a, b, (((1,), (0,)), ((), ())), preferred_element_type=f32)


def mt(a, b):
    return lax.dot_general(a, b, (((1,), (1,)), ((), ())), preferred_element_type=f32)


def transposed(a):
    return jnp.transpose(a, (1, 0))


class Sent:
    def __init__(self, copy):
        self.copy, self.open_send, self.open_recv = copy, True, True

    def wait_send(self):
        if self.open_send:
            self.copy.wait_send()
        self.open_send = False

    def wait_recv(self):
        if self.open_recv:
            self.copy.wait_recv()
        self.open_recv = False

    def wait(self):
        self.wait_send()
        self.wait_recv()


class Batch(Sent):
    def __init__(self, ssem, rsem, whole):
        self.ssem, self.rsem, self.whole, self.dev = ssem, rsem, whole, None
        super().__init__(None)

    def copy_of(self, src, dst):
        return pltpu.make_async_remote_copy(
            src_ref=src,
            dst_ref=dst,
            send_sem=self.ssem,
            recv_sem=self.rsem,
            device_id=self.dev,
            device_id_type=pl.DeviceIdType.MESH,
        )

    def send(self, src, dst, dev):
        self.dev = dev
        self.copy_of(src, dst).start()

    def wait_send(self):
        if self.open_send:
            self.copy = self.copy_of(self.whole, self.whole)
        super().wait_send()

    def wait_recv(self):
        if self.open_recv:
            self.copy = self.copy_of(self.whole, self.whole)
        super().wait_recv()


class Links:
    def __init__(self, ssem, rsem):
        self.ssem, self.rsem, self.n, self.all = ssem, rsem, 0, []

    def send(self, src, dst, dev):
        copy = pltpu.make_async_remote_copy(
            src_ref=src,
            dst_ref=dst,
            send_sem=self.ssem.at[self.n],
            recv_sem=self.rsem.at[self.n],
            device_id=dev,
            device_id_type=pl.DeviceIdType.MESH,
        )
        copy.start()
        self.n += 1
        self.all.append(Sent(copy))
        return self.all[-1]

    def batch(self, whole):
        self.all.append(Batch(self.ssem.at[self.n], self.rsem.at[self.n], whole))
        self.n += 1
        return self.all[-1]


class RingGather:
    def __init__(self, links, ref, whole, plus, minus, plus_parts, minus_parts):
        self.ref, self.plus, self.minus = ref, plus, minus
        self.plus_parts, self.minus_parts = plus_parts, minus_parts
        half = len(plus_parts)
        self.left_on, self.left_end = links.batch(whole(half)), links.batch(whole(half))
        self.right_on, self.right_end = links.batch(whole(half)), links.batch(whole(half))
        self.far = links.batch(whole(2 * half))

    def send_plus(self, part):
        own = self.ref("me", part)
        batch = self.left_on if part in self.plus_parts else self.left_end
        batch.send(own, own, self.plus)

    def send_minus(self, part):
        own = self.ref("me", part)
        batch = self.right_on if part in self.minus_parts else self.right_end
        batch.send(own, own, self.minus)

    def send(self, part):
        self.send_plus(part)
        self.send_minus(part)

    def first(self):
        for part in self.plus_parts:
            self.send_plus(part)
        for part in self.minus_parts:
            self.send_minus(part)

    def rest(self):
        for part in self.minus_parts:
            self.send_plus(part)
        for part in self.plus_parts:
            self.send_minus(part)

    def forward(self):
        self.left_on.wait_recv()
        for part in self.plus_parts:
            ref = self.ref("left", part)
            self.far.send(ref, ref, self.plus)
        self.right_on.wait_recv()
        for part in self.minus_parts:
            ref = self.ref("right", part)
            self.far.send(ref, ref, self.minus)

    def wait(self, at):
        batches = {
            "left": (self.left_on, self.left_end),
            "right": (self.right_on, self.right_end),
            "far": (self.far,),
        }
        for batch in batches[at]:
            batch.wait_recv()


class DirectGather:
    def __init__(self, links, ref, whole, devs):
        self.ref, self.devs, self.batch = ref, devs, links.batch(whole(12))

    def send(self, part):
        own = self.ref("me", part)
        for dev in self.devs:
            self.batch.send(own, own, dev)


class DirectSum:
    def __init__(self, links, own, recv, devs):
        self.own, self.recv, self.devs, self.batch = own, recv, devs, links.batch(recv)

    def start(self):
        for i, at in enumerate(("right", "left", "far")):
            for p in range(4):
                self.batch.send(self.own(at, p), self.recv.at[i, p], self.devs[i])

    def total(self, p):
        self.batch.wait_recv()
        total = self.own("me", p)[...].astype(f32)
        for i in range(3):
            total = total + self.recv[i, p].astype(f32)
        return total


class RingSum:
    def __init__(self, links, own, mid, recv, plus, minus, parts):
        self.own, self.mid, self.recv, self.plus, self.minus = own, mid, recv, plus, minus
        half = parts // 2
        self.low, self.high = range(half), range(half, parts)
        self.mid_left = links.batch(mid.at[pl.ds(0, half)])
        self.mid_right = links.batch(mid.at[pl.ds(half, half)])
        self.left, self.right = links.batch(recv.at[0]), links.batch(recv.at[1])

    def first(self):
        for p in self.low:
            self.mid_left.send(self.own("far", p), self.mid.at[p], self.plus)
        for p in self.high:
            self.mid_right.send(self.own("far", p), self.mid.at[p], self.minus)

    def direct_right(self):
        for p in self.high:
            self.left.send(self.own("right", p), self.recv.at[0, p], self.plus)

    def direct_left(self):
        for p in self.low:
            self.right.send(self.own("left", p), self.recv.at[1, p], self.minus)

    def direct(self):
        self.direct_right()
        self.direct_left()

    def middle(self):
        self.mid_left.wait_recv()
        for p in self.low:
            self.mid[p] = self.plus_f32(self.own("right", p)[...], self.mid[p])
            self.left.send(self.mid.at[p], self.recv.at[0, p], self.plus)
        self.mid_right.wait_recv()
        for p in self.high:
            self.mid[p] = self.plus_f32(self.own("left", p)[...], self.mid[p])
            self.right.send(self.mid.at[p], self.recv.at[1, p], self.minus)

    @staticmethod
    def plus_f32(a, b):
        return (a.astype(f32) + b.astype(f32)).astype(bf16)

    def wait(self):
        self.left.wait_recv()
        self.right.wait_recv()

    def total(self, p):
        self.wait()
        total = self.own("me", p)[...].astype(f32)
        return total + self.recv[0, p].astype(f32) + self.recv[1, p].astype(f32)


def layer(
    x_in, t_in, len_in, wq_in, wk_in, wv_in, wo_in, up_in, down_in,
    ob_in, g1_in, b1_in, db_in, g2_in, b2_in, qb_in, vb_in, ub_in,
    out_o, gi_o, dwa_o, dwb_o, dwo_o, dqkv_o, sv_o,
    xf, tf, wa, wb, wq2, wo2, wo4, wqkv, vec, ub, vcol, qkvt, ktm, qaug, vaug, vtm, pst, linv,
    ctxt, ctxa, hid, nrm, sg, bstore, astore, slope, brecv, arecv,
    ga, gb, gqa, gqb, gra, grb, gao, gor, dctx, dct, outt, delta,
    dqkvt, dxp, rxi, rx, im, rm, s1, r2, s2, r3, zi, zr, sb0, br, sb1, rb2,
    rqa, rqb, sqa, sqb, ra2, rb3, ro, so1, ro2, so2, so4, ro3,
    x1, xb1, xq1, stat, gcol, sv, rsv, wown, wqs, vrow, ubs,
    lsem, ssem, rsem,
):
    d = lax.axis_index("dp")
    y = lax.axis_index("row_0")
    x = lax.axis_index("row_1")
    c = lax.axis_index("col")
    e = 1 - d
    r = 4 * y + x
    a_me = x * e + y * d
    b_me = y * e + x * d

    def around(me):
        return {
            "me": me,
            "left": lax.rem(me + 3, 4),
            "right": lax.rem(me + 1, 4),
            "far": lax.rem(me + 2, 4),
        }

    b_at, c_at = around(b_me), around(c)

    def ridx(a, b):
        return (4 * b + a) * e + (4 * a + b) * d

    def zdev(k):
        return {"col": lax.rem(c + k, 4)}

    def adev(k):
        return {"row_0": lax.rem(y + k * d, 4), "row_1": lax.rem(x + k * e, 4)}

    def bdev(k):
        return {"row_0": lax.rem(y + k * e, 4), "row_1": lax.rem(x + k * d, 4)}

    sib = {"dp": e}
    links = Links(ssem, rsem)

    def wait_all(copies):
        for copy in copies:
            copy.wait_recv()

    def triple(whole, src, dst, dev):
        batch = links.batch(whole)
        for k in (1, 3, 2):
            batch.send(src(k), dst(k), dev(k))
        return batch

    def region(body):
        @pl.when(e + d == 1 + d * e)
        def _():
            body()

    def unrolled(n, body, carry):
        for i in range(n):
            carry = body(i, carry)
        return carry

    def cols(i, width):
        if isinstance(i, int):
            return pl.ds(i * width, width)
        return pl.ds(pl.multiple_of(i * width, 128), width)

    def rows(i, height):
        if isinstance(i, int):
            return pl.ds(i * height, height)
        return pl.ds(pl.multiple_of(i * height, 16), height)

    n_local = [0]

    def local(src, dst):
        copy = pltpu.make_async_copy(src, dst, lsem.at[n_local[0]])
        copy.start()
        n_local[0] += 1
        return copy

    xrows = rows(c, C)
    tcols = cols(c, TOK)
    bar = pltpu.get_barrier_semaphore()
    for k in (1, 2, 3):
        for dev in (zdev(k), adev(k), bdev(k)):
            pl.semaphore_signal(bar, inc=1, device_id=dev, device_id_type=pl.DeviceIdType.MESH)
    pl.semaphore_signal(bar, inc=1, device_id=sib, device_id_type=pl.DeviceIdType.MESH)
    cw = [local(ref, wqs.at[i]) for i, ref in enumerate((wq_in, wk_in, wv_in))]
    cup = local(up_in, wown.at[0])
    cdn = local(down_in, wown.at[1])
    cx = local(x_in, xf.at[xrows])
    ct = local(t_in.at[:, tcols], tf.at[c])
    cwo = local(wo_in, wo4.at[c])
    cv = [
        local(ref, vrow.at[i])
        for i, ref in enumerate((ob_in, g1_in, b1_in, db_in, g2_in, b2_in, qb_in, vb_in))
    ]
    cub = local(ub_in, ubs)
    for copy in cw:
        copy.wait()
    own_qkv = [wqs[i] for i in range(3)]
    own_qkv = jnp.concatenate(
        [w[:, h * HD : (h + 1) * HD] for h in range(HEADS) for w in own_qkv], axis=1
    )
    own_qkv = jnp.where(d == 0, own_qkv[:, 0:QH], own_qkv[:, QH:])
    wq2[d, r] = jnp.concatenate([own_qkv, jnp.zeros((RB, HW - QH), bf16)], axis=1)
    pl.semaphore_wait(bar, 10)

    def along_a(ref, whole):
        return triple(whole, lambda k: ref, lambda k: ref, adev)

    def of_b(ref):
        return lambda at, k: ref(ridx(lax.rem(a_me + 4 - k, 4), b_at[at]))

    def direct_b(ref, whole):
        return DirectGather(links, of_b(ref), whole, (bdev(1), bdev(3), bdev(2)))

    def wq_ref(i):
        return wq2.at[d, i]

    def wo_ref(i):
        return wo2.at[d, i]

    def wa_ref(i):
        return wa.at[d, i]

    def wb_ref(i):
        return wb.at[d, i, :, cols(c, FB)]

    def some(buf):
        return lambda n: buf.at[d, pl.ds(0, n)]

    def some_b(n):
        return wb.at[d, pl.ds(0, n), :, cols(c, FB)]

    class ToSibling:
        def __init__(self, whole):
            self.batch = links.batch(whole)

        def send(self, ref):
            self.batch.send(ref, ref, sib)

        def wait(self):
            self.batch.wait_recv()

    wq_a = along_a(wq_ref(r), some(wq2)(3))
    wq_b = direct_b(wq_ref, some(wq2))
    wq_b.send(0)
    cup.wait()
    cdn.wait()
    wz = triple(
        wa.at[d, 0, :, pl.ds(0, 3 * FA)],
        lambda k: wown.at[d, :, pl.ds(0, FA)],
        lambda k: wa.at[d, r, :, cols(c, FA)],
        zdev,
    )
    cx.wait()
    x_z = RingGather(
        links,
        lambda at, half: xf.at[rows(2 * c_at[at] + half, C // 2)],
        lambda n: xf.at[pl.ds(0, n * C // 2)],
        zdev(1), zdev(3), (0,), (1,),
    )
    x_z.first()
    cwo.wait()
    for i, copy in enumerate(cv):
        copy.wait()
        vec[c, i : i + 1, :] = vrow[i]
    cub.wait()
    ub[c, 0:1, :] = jnp.concatenate([ubs[i : i + 1] for i in range(6)], axis=1)
    oz = triple(wo4.at[pl.ds(0, 3)], lambda k: wo4.at[c], lambda k: wo4.at[c], zdev)
    vz = triple(vec.at[pl.ds(0, 3)], lambda k: vec.at[c], lambda k: vec.at[c], zdev)
    uz = triple(
        ub.at[pl.ds(0, 3), 0:1], lambda k: ub.at[c, 0:1], lambda k: ub.at[c, 0:1], zdev
    )
    wa[d, r, :, cols(c, FA)] = wown[d, :, 0:FA]
    wb[d, r, :, cols(c, FB)] = wown[d, :, FA:]
    wb_a = along_a(wb_ref(r), some_b(3))
    wb_b = direct_b(wb_ref, some_b)
    wb_b.send(0)

    wq_a.wait_recv()
    for k in (1, 3, 2):
        wq_b.send(k)
    wq_s = ToSibling(wq2.at[d])
    for j in range(4):
        wq_s.send(wq_ref(ridx(j, b_me)))
    wb_a.wait_recv()
    for k in (1, 3, 2):
        wb_b.send(k)
    x_z.rest()
    wz.wait_recv()
    wa_a = [links.batch(wa_ref(0)) for _ in range(3)]
    for i, k in enumerate((1, 3, 2)):
        wa_a[i].send(wa_ref(r), wa_ref(r), adev(k))
    wa_b = RingGather(links, of_b(wa_ref), some(wa), bdev(1), bdev(3), (0, 2), (1, 3))
    wa_b.send(0)
    oz.wait_recv()
    own_wo = jnp.concatenate([wo4[j] for j in range(4)], axis=1)
    wo2[d, r] = jnp.where(d == 0, own_wo[:, 0:HW], own_wo[:, HW:])
    wo_a = along_a(wo_ref(r), some(wo2)(3))
    wo_b = direct_b(wo_ref, some(wo2))
    wo_b.send(0)
    wq_b.batch.wait_recv()
    for at in ("left", "right", "far"):
        for k in range(4):
            wq_s.send(wq_b.ref(at, k))
    x_z.forward()
    wo_s = ToSibling(wo2.at[d])
    wo_s.send(wo_ref(r))
    wa_s = ToSibling(wa.at[d])
    wa_s.send(wa_ref(r))
    for i, k in enumerate((1, 3, 2)):
        wa_a[i].wait_recv()
        wa_b.send(k)
        wa_s.send(wa_b.ref("me", k))
    wo_a.wait_recv()
    for k in (1, 3, 2):
        wo_b.send(k)
        wo_s.send(wo_b.ref("me", k))
    vown = transposed(vec[c])
    length = len_in[0]

    for at in ("left", "right", "far"):
        x_z.wait(at)
    wb_b.batch.wait_recv()

    def wb_z(at, half):
        return wb.at[d, pl.ds(half * 8, 8), :, cols(c_at[at], FB)]

    def some_z(n):
        return wb.at[d, pl.ds(0, 8), :, pl.ds(0, n * FB)]

    wb_zg = RingGather(links, wb_z, some_z, zdev(1), zdev(3), (0,), (1,))
    wb_zg.first()
    wb_s = ToSibling(wb.at[d])
    wb_s.send(wb.at[d, :, :, cols(c, FB)])
    wq_s.wait()
    q_bias = vown[:, 6:7]
    v_bias = vown[:, 7:8]
    lane_iota = lax.broadcasted_iota(jnp.int32, (1, TOK), 1)
    first_row = lax.broadcasted_iota(jnp.int32, (HD, TOK), 0) == 0

    def qkv_chunk(i, carry):
        at = cols(i, TOK)
        tok = xf[:, at]
        qkv = mm(dxp[:, :, 0:D].reshape(3 * C, D), tok)
        bias = jnp.where(lane_iota + i * TOK < length, 0.0, MASK)
        bias = jnp.where(first_row, jnp.broadcast_to(bias, (HD, TOK)), 0.0).astype(bf16)
        ones = jnp.where(first_row, 1.0, 0.0).astype(bf16)
        for h in range(HEADS):
            hs = slice(h * HD, (h + 1) * HD)
            of = h * C
            q = (qkv[of : of + HD] + q_bias[hs]).astype(bf16)
            q = (q.astype(f32) * (HD**-0.5)).astype(bf16)
            k = qkv[of + HD : of + 2 * HD].astype(bf16)
            v = (qkv[of + 2 * HD : of + 3 * HD] + v_bias[hs]).astype(bf16)
            qkvt[h * HD : (h + 1) * HD, at] = q
            qkvt[C + h * HD : C + (h + 1) * HD, at] = k
            qaug[h, 0:HD, at] = q
            qaug[h, HD : 2 * HD, at] = ones
            vaug[h, 0:HD, at] = v
            vaug[h, HD : HD + 16, at] = ones[0:16]
            ktm[h, at, :] = transposed(jnp.concatenate([k, bias], axis=0))
            vtm[h, at, :] = transposed(jnp.concatenate([v, ones], axis=0))
        return carry

    w_low = transposed(wq2[0].reshape(D, HW))[0:QH]
    w_high = transposed(wq2[1].reshape(D, HW))[0:QH]
    dxp[0, :, 0:D] = w_low[0:C]
    dxp[1, 0 : QH - C, 0:D] = w_low[C:]
    dxp[1, QH - C :, 0:D] = w_high[0 : QH - C]
    dxp[2, :, 0:D] = w_high[QH - C :]
    unrolled(4, qkv_chunk, 0)

    wb_zg.rest()

    def fwd_head(h):
        score = mm(ktm[h], qaug[h, :, 0:WT])
        for n in range(LEN // WT):
            at = cols(n, WT)
            later = mm(ktm[h], qaug[h, :, cols(n + 1, WT)]) if (n + 1) * WT < LEN else None
            top = jnp.max(score, axis=0, keepdims=True)
            probs = jnp.exp(score - top).astype(bf16)
            pst[h, :, at] = probs
            both = mm(vaug[h], probs)
            inv = 1.0 / both[HD : HD + 1]
            linv[h, 0:1, at] = inv
            ctxt[h * HD : (h + 1) * HD, at] = (both[0:HD] * inv).astype(bf16)
            score = later

    cc = links.batch(ctxa.at[pl.ds(0, 3)])

    def context_out(h):
        hrow = pl.ds(h * HD, HD)
        ctxa[c, hrow] = ctxt[hrow, tcols]
        for k in (1, 3, 2):
            there = cols(lax.rem(c + k, 4), TOK)
            cc.send(ctxt.at[hrow, there], ctxa.at[c, hrow], zdev(k))

    def pass_on(ring, sent, at):
        ring.wait(at)
        for k in range(4):
            sent.send(ring.ref(at, k))

    fwd_head(0)
    context_out(0)
    wa_b.forward()
    pass_on(wa_b, wa_s, "left")
    pass_on(wa_b, wa_s, "right")
    fwd_head(1)
    context_out(1)
    wo_b.batch.wait_recv()
    for at in ("left", "right", "far"):
        for k in range(4):
            wo_s.send(wo_b.ref(at, k))
    wait_all((vz, uz))
    for i in range(4):
        vcol[i * C : (i + 1) * C, 0:16] = transposed(vec[i])
    fwd_head(2)
    context_out(2)
    wb_zg.forward()
    pass_on(wa_b, wa_s, "far")
    for i in range(2):
        wqkv[:, i * QH : (i + 1) * QH] = wq2[i].reshape(D, HW)[:, 0:QH]
    wo_s.wait()
    cc.wait_recv()
    ct.wait()
    tt = triple(
        tf.at[pl.ds(0, 3)],
        lambda k: t_in.at[:, cols(lax.rem(c + k, 4), TOK)],
        lambda k: tf.at[c],
        zdev,
    )

    def norm_stats(ref):
        v = ref[...]
        mean = jnp.sum(v, axis=0, keepdims=True) * (1.0 / D)
        square = jnp.sum(v * v, axis=0, keepdims=True) * (1.0 / D)
        return mean, lax.rsqrt(square - mean * mean + EPS)


    @region
    def _():
        acc = xf[:, tcols].astype(f32) + vcol[:, 0:1]
        for j in range(2):
            w = wo2[j].reshape(D, HW)
            acc = acc + mm(w, ctxa[2 * j : 2 * j + 2].reshape(HW, TOK))
        hid[...] = acc
        mean1, inv1 = norm_stats(hid)
        stat[0:1] = inv1

        def norm1(i, carry):
            row = rows(i, C)
            n = (hid[row] - mean1) * inv1
            nrm[row] = n
            h = n * vcol[row, 1:2] + vcol[row, 2:3]
            hid[row] = h + vcol[row, 3:4]
            astore[0, row] = h.astype(bf16)
            return carry

        unrolled(4, norm1, 0)
        outt[...] = transposed(astore[0])

    for at in ("left", "right"):
        wb_zg.wait(at)
        wb_s.send(wb.at[d, :, :, cols(c_at[at], FB)])

    wa_s.wait()

    def w_chunk(ref, i):
        return ref[:, :, cols(i, FA)].reshape(D, FA)

    def halves(chunk):
        if chunk < 4:
            return [(half, chunk * FA // 2, FA // 2) for half in range(2)]
        pairs = [(half, j) for j in (2 * chunk - 8, 2 * chunk - 7) for half in range(2)]
        return [(half, 2 * FA + j * FB // 2, FB // 2) for half, j in pairs]

    def store_halves(w, chunk, v):
        at = 0
        for half, to, width in halves(chunk):
            bstore[w, half, :, to : to + width] = v[:, at : at + width]
            at += width

    def load_halves(w, chunk):
        return jnp.concatenate(
            [bstore[w, half, :, to : to + width] for half, to, width in halves(chunk)], axis=1
        )

    def up_of(ref, bias, first):
        def up_chunk(i, carry):
            at = cols(first + i, FA)
            pre = mm(outt[...], w_chunk(ref, i)) + bias(i)
            half = 0.5 * (1.0 + lax.erf(pre * ROOT_HALF))
            store_halves(1, first + i, (pre * half).astype(bf16))
            slope[:, at] = (half + pre * jnp.exp(-0.5 * pre * pre) * INV_ROOT_TAU).astype(bf16)
            return carry

        return up_chunk

    def bias_a(i):
        return ub[i, 0:1, 0:FA]

    def bias_b(i):
        return jnp.concatenate([ub[2 * i, 0:1, FA:], ub[2 * i + 1, 0:1, FA:]], axis=1)

    region(lambda: unrolled(4, up_of(wa.at[0], bias_a, 0), 0))

    def down_of(ref, first):
        def down_chunk(i, carry):
            hid[...] = hid[...] + mt(w_chunk(ref, i), load_halves(1, first + i))
            return carry

        return down_chunk

    region(lambda: unrolled(4, down_of(wa.at[1], 0), 0))
    wb_zg.wait("far")
    wb_s.send(wb.at[d, :, :, cols(c_at["far"], FB)])
    wb_s.wait()

    @region
    def _():
        unrolled(2, up_of(wb.at[0], bias_b, 4), 0)
        unrolled(2, down_of(wb.at[1], 4), 0)

    ex_down = [links.send(bstore.at[1, e], brecv.at[1], sib)]

    tt.wait_recv()
    valid = lane_iota + c * TOK < length

    zero = jnp.zeros((1, TOK), f32)

    @region
    def _():
        mean2, inv2 = norm_stats(hid)
        gcol[...] = jnp.zeros(gcol.shape, f32)
        sv[...] = jnp.zeros(sv.shape, f32)

        def norm2(i, carry):
            total, crossed, loss = carry
            row = rows(i, C)
            n = (hid[row] - mean2) * inv2
            hid[row] = n
            final = n * vcol[row, 4:5] + vcol[row, 5:6]
            delta[row] = final.astype(bf16)
            g = jnp.where(valid, final - tf[i].astype(f32), 0.0)
            gcol[row, 4:5] = jnp.sum(g * n, axis=1, keepdims=True)
            gcol[row, 5:6] = jnp.sum(g, axis=1, keepdims=True)
            s = g * vcol[row, 4:5]
            sg[row] = s
            return (
                total + jnp.sum(s, axis=0, keepdims=True),
                crossed + jnp.sum(s * n, axis=0, keepdims=True),
                loss + jnp.sum(g * g, axis=0, keepdims=True),
            )

        total2, crossed2, loss_row = unrolled(4, norm2, (zero, zero, zero))
        for i, row in enumerate((inv2, total2, crossed2, loss_row)):
            stat[1 + i : 2 + i] = row

    out_o_own = local(delta.at[xrows], out_o.at[:, tcols])
    fo = triple(
        delta.at[pl.ds(0, 3 * C)],
        lambda k: delta.at[rows(lax.rem(c + k, 4), C)],
        lambda k: out_o.at[:, tcols],
        zdev,
    )

    def norm2_back(i, carry):
        row = rows(i, C)
        s = stat[1:2] * (sg[row] - stat[2:3] * (1.0 / D) - hid[row] * (stat[3:4] * (1.0 / D)))
        sg[row] = s
        low = s.astype(bf16)
        astore[1, row] = low
        gcol[row, 3:4] = jnp.sum(low.astype(f32), axis=1, keepdims=True)
        return carry

    @region
    def _():
        unrolled(4, norm2_back, 0)
        outt[...] = transposed(astore[1])


    ex_down.append(links.send(astore.at[1], arecv.at[1], sib))

    def act_of(ref, first):
        def act_chunk(i, carry):
            at = cols(first + i, FA)
            g = mm(outt[...], w_chunk(ref, i)) * slope[:, at].astype(f32)
            low = g.astype(bf16)
            store_halves(0, first + i, low)
            total = jnp.sum(low.astype(f32), axis=0, keepdims=True)
            sv[8 + first + i : 9 + first + i, 0:FA] = total
            return carry

        return act_chunk

    @region
    def _():
        unrolled(2, act_of(wb.at[1], 4), 0)
        unrolled(4, act_of(wa.at[1], 0), 0)

    ex_up = [
        links.send(astore.at[0], arecv.at[0], sib),
        links.send(bstore.at[0, e], brecv.at[0], sib),
    ]

    def back_of(ref, first):
        def back_chunk(i, carry):
            sg[...] = sg[...] + mt(w_chunk(ref, i), load_halves(0, first + i))
            return carry

        return back_chunk

    def sum_b(own, mid, recv):
        return RingSum(
            links, lambda at, j: own(ridx(j, b_at[at])), mid, recv, bdev(1), bdev(3), 4
        )

    def direct_sum(own, recv):
        return DirectSum(
            links, lambda at, j: own(ridx(j, b_at[at])), recv, (bdev(1), bdev(3), bdev(2))
        )

    def end_b(ring, summed, peer_recv):
        for j in range(4):
            summed[j] = ring.total(j).astype(bf16)
        return triple(
            peer_recv,
            lambda k: summed.at[lax.rem(a_me + k, 4)],
            lambda k: peer_recv.at[k - 1],
            adev,
        )

    def end_a(sends, summed, recv):
        sends.wait_recv()
        total = summed[a_me].astype(f32)
        for k in range(3):
            total = total + recv[k].astype(f32)
        return total

    def add_sibling(ref, other):
        def add(i, carry):
            ref[d, i] = (ref[d, i].astype(f32) + other[i].astype(f32)).astype(bf16)
            return carry

        unrolled(16, add, 0)

    def weight_grad(w):
        @region
        def _():
            for at, ref in ((0, ga), (2 * FA, gb)):
                for lo in range(0, ref.shape[3], FA):
                    cut = pl.ds(at + lo, FA)
                    g = mm(astore[w], bstore[w, d, :, cut]) + mm(arecv[w], brecv[w, :, cut])
                    ref[w, :, :, lo : lo + FA] = g.astype(bf16).reshape(16, RB, FA)

        def z_own(at, half):
            return gb.at[w, pl.ds(half * 8, 8), :, cols(c_at[at], FB // 2)]

        a_ring = sum_b(lambda i: ga.at[w, i], im.at[w], rm.at[w])
        b_ring = RingSum(links, z_own, zi.at[w], zr.at[w], zdev(1), zdev(3), 2)
        a_ring.first()
        b_ring.first()
        return a_ring, b_ring

    region(lambda: unrolled(2, back_of(wb.at[0], 4), 0))
    wait_all(ex_down)
    wd_a, wd_b = weight_grad(1)
    region(lambda: unrolled(4, back_of(wa.at[0], 0), 0))

    def hidden_back(i, carry):
        total, crossed = carry
        row = rows(i, C)
        g = sg[row]
        n = nrm[row]
        gcol[row, 1:2] = jnp.sum(g * n, axis=1, keepdims=True)
        gcol[row, 2:3] = jnp.sum(g, axis=1, keepdims=True)
        s = g * vcol[row, 1:2]
        sg[row] = s
        return (
            total + jnp.sum(s, axis=0, keepdims=True),
            crossed + jnp.sum(s * n, axis=0, keepdims=True),
        )


    fo.wait_send()
    out_o_own.wait()
    wd_a.direct()

    @region
    def _():
        total1, crossed1 = unrolled(4, hidden_back, (zero, zero))

        def norm1_back(i, carry):
            row = rows(i, C)
            s = stat[0:1] * (sg[row] - total1 * (1.0 / D) - nrm[row] * (crossed1 * (1.0 / D)))
            sg[row] = s
            low = s.astype(bf16)
            delta[row] = low
            gcol[row, 0:1] = jnp.sum(low.astype(f32), axis=1, keepdims=True)
            return carry

        unrolled(4, norm1_back, 0)
        outt[...] = transposed(delta[...])
        for i in range(2):
            part = transposed(mm(outt[...], wo2[i].reshape(D, HW)).astype(bf16))
            dct[2 * i : 2 * i + 2] = part.reshape(2, C, TOK)
        dctx[:, tcols] = dct[c]


    dc = []
    for h in range(HEADS):
        hrow = pl.ds(h * HD, HD)
        dc.append(
            triple(
                dct.at[0],
                lambda k: dct.at[lax.rem(c + k, 4), hrow],
                lambda k: dctx.at[hrow, tcols],
                zdev,
            )
        )

    sv[0:8] = transposed(gcol[...])[0:8]
    sv[6:7] = jnp.broadcast_to(jnp.sum(stat[4:5], axis=1, keepdims=True), (1, D))
    sv[7:8] = jnp.broadcast_to(length.astype(f32), (1, D))
    v_sent = [links.send(sv, rsv.at[0], sib)]
    v_from = [(0, 1)]

    def sv_add():
        v_sent.pop().wait()
        lo, n = v_from[-1]
        total = sv[...]
        for i in range(n):
            total = total + rsv[lo + i]
        sv[...] = total

    def sv_send(dev):
        lo = sum(v_from[-1])
        v_from.append((lo, 3))
        v_sent.append(
            triple(
                rsv.at[pl.ds(lo, 3)], lambda k: sv, lambda k: rsv.at[lo + k - 1], dev
            )
        )

    wait_all(ex_up)
    wd_b.direct()
    wu_a, wu_b = weight_grad(0)
    sv_add()
    sv_send(bdev)

    @region
    def _():
        g = mt(delta[...], ctxa[...].reshape(D, TOK)).astype(bf16)
        for i in range(2):
            gao[i] = g[:, i * HW : (i + 1) * HW].reshape(16, RB, HW)

    go_x = links.send(gao.at[e], gor, sib)
    wd_a.middle()
    wd_b.middle()

    def bwd_head(h, meanwhile=None):
        hrow = pl.ds(h * HD, HD)
        krow = pl.ds(C + h * HD, HD)
        of = h * C

        dk = dv = jnp.zeros((HD, LEN), f32)
        for n in range(LEN // WT):
            at = cols(n, WT)
            inv = linv[h, 0:1, at]
            dc = dctx[hrow, at].astype(f32)
            inner = jnp.sum(dc * ctxt[hrow, at].astype(f32), axis=0, keepdims=True) * inv
            dcs = (dc * inv).astype(bf16)
            probs = pst[h, :, at]
            dv = dv + mt(dcs, probs)
            dp = mm(vtm[h, :, 0:HD], dcs) - inner
            ds = (probs.astype(f32) * dp).astype(bf16)
            dk = dk + mt(qkvt[hrow, at], ds)
            dqkvt[of : of + HD, at] = (mm(qkvt[krow, :], ds) * (HD**-0.5)).astype(bf16)
            if n == 0 and meanwhile is not None:
                meanwhile()
        dqkvt[of + HD : of + 2 * HD] = dk.astype(bf16)
        dqkvt[of + 2 * HD : of + 3 * HD] = dv.astype(bf16)

    spare = HL - QC
    row_iota = lax.broadcasted_iota(jnp.int32, (RB, spare), 0)

    def qkv_grad(h, ref, at):
        of = dqkvt[h * C : (h + 1) * C]
        g = mt(xf[...], of).astype(bf16)
        sums = mt(jnp.ones((8, LEN), bf16), of)[0:1]
        for half in range(2):
            lo = half * QC
            part_rows = jnp.zeros((RB, spare), f32)
            for j in range(3):
                part = sums[:, lo + j * spare : lo + (j + 1) * spare]
                part_rows = jnp.where(row_iota == j, jnp.broadcast_to(part, (RB, spare)), part_rows)
            ref[half, :, :, at : at + QC] = g[:, lo : lo + QC].reshape(16, RB, QC)
            ref[half, :, :, at + QC : at + HL] = jnp.broadcast_to(
                part_rows.astype(bf16)[None], (16, RB, spare)
            )

    dc[0].wait_recv()
    bwd_head(0)
    wu_a.direct()
    wu_b.direct()
    go_x.wait_recv()
    add_sibling(gao, gor)
    o_sum = direct_sum(lambda i: gao.at[d, i], ro)
    o_sum.start()
    dc[1].wait_recv()
    bwd_head(1, lambda: qkv_grad(0, gqa, 0))
    wd_sends = end_b(wd_a, s1.at[1], r2.at[1])
    def total_z(w, ring):
        for half in range(2):
            sb0[w, half * 8 : half * 8 + 8] = ring.total(half).astype(bf16)
        ring_b = direct_sum(lambda i: sb0.at[w, i], br.at[w])
        ring_b.start()
        return ring_b

    wu_a.middle()
    wu_b.middle()


    sv_add()
    sv_send(adev)
    dc[2].wait_recv()
    bwd_head(2, lambda: qkv_grad(1, gqa, HL))

    def dx_part(i, slot=None):
        @region
        def _():
            row = rows(i, C)
            gi_o[...] = mm(wqkv[row], dqkvt[...])
            gi_o[:, tcols] = gi_o[:, tcols] + sg[row]
            if slot is not None:
                dxp[slot] = gi_o[...].astype(bf16)

    SLOT = {"far": 0, "right": 1, "left": 2}

    def dx_own(at, half):
        return dxp.at[SLOT[at], pl.ds(half * (C // 2), C // 2)]

    dx_sum = RingSum(links, dx_own, rxi, rx, zdev(1), zdev(3), 2)
    dx_part(c_at["far"], 0)
    dx_sum.first()
    bd_sum = total_z(1, wd_b)
    xa = links.send(gqa.at[e], gra, sib)
    region(lambda: qkv_grad(2, gqb, 0))
    xb = links.send(gqb.at[e], grb, sib)

    dx_part(c_at["right"], 1)
    dx_sum.direct_right()
    dx_part(c_at["left"], 2)
    dx_sum.direct_left()
    xa.wait_recv()
    add_sibling(gqa, gra)
    qa_sum = direct_sum(lambda i: gqa.at[d, i], rqa)
    qa_sum.start()
    xb.wait_recv()
    add_sibling(gqb, grb)
    qb_sum = direct_sum(lambda i: gqb.at[d, i], rqb)
    qb_sum.start()
    dx_part(c)
    o_sends = end_b(o_sum, so1, ro2)

    def along_z(w, sends):
        s2[w] = end_a(sends, s1.at[w], r2.at[w]).astype(bf16)
        return triple(
            r3.at[w],
            lambda k: s2.at[w, :, cols(lax.rem(c + k, 4), FA // 2)],
            lambda k: r3.at[w, k - 1],
            zdev,
        )

    w3 = {1: along_z(1, wd_sends)}
    wu_sends = end_b(wu_a, s1.at[0], r2.at[0])
    dx_sum.middle()
    bu_sum = total_z(0, wu_b)
    sv_add()
    sv_send(zdev)
    qa_sends = end_b(qa_sum, sqa, ra2)
    qb_sends = end_b(qb_sum, sqb, rb3)
    bd_sends = end_b(bd_sum, sb1.at[1], rb2.at[1])
    so2[0] = end_a(o_sends, so1, ro2).astype(bf16)
    o_x = links.send(so2.at[0], so2.at[1], sib)
    w3[0] = along_z(0, wu_sends)
    bu_sends = end_b(bu_sum, sb1.at[0], rb2.at[0])
    o_x.wait_recv()
    mine, other = so2[0], so2[1]
    low, high = jnp.where(d == 0, mine, other), jnp.where(d == 0, other, mine)
    so4[0], so4[1] = low[:, 0:C], low[:, C:]
    so4[2], so4[3] = high[:, 0:C], high[:, C:]
    o3 = triple(
        ro3, lambda k: so4.at[lax.rem(c + k, 4)], lambda k: ro3.at[k - 1], zdev
    )
    xq1[0, :, 0 : 2 * HL] = end_a(qa_sends, sqa, ra2)
    xq1[0, :, 2 * HL :] = end_a(qb_sends, sqb, rb3)
    q3 = links.send(xq1.at[0], xq1.at[1], sib)
    wait_all((w3[1], w3[0]))
    x1[0] = s2[:, :, cols(c, FA // 2)].astype(f32)
    for w in range(2):
        for k in range(3):
            x1[0, w] = x1[0, w] + r3[w, k].astype(f32)
    w4 = links.send(x1.at[0], x1.at[1], sib)
    xb1[0, 1] = end_a(bd_sends, sb1.at[1], rb2.at[1])
    xb1[0, 0] = end_a(bu_sends, sb1.at[0], rb2.at[0])
    wb4 = links.send(xb1.at[0], xb1.at[1], sib)
    o3.wait_recv()
    ototal = so4[c].astype(f32)
    for k in range(3):
        ototal = ototal + ro3[k].astype(f32)
    dwo_o[...] = ototal
    sv_add()
    sv_o[...] = sv[...]
    w4.wait_recv()
    dwa_o[d] = x1[0]
    dwa_o[e] = x1[1]
    q3.wait_recv()
    dqkv_o[d] = xq1[0]
    dqkv_o[e] = xq1[1]
    wb4.wait_recv()
    dwb_o[d] = xb1[0]
    dwb_o[e] = xb1[1]
    dx_sum.wait()
    for half in range(2):
        row = pl.ds(half * (C // 2), C // 2)
        gi_o[row] = gi_o[row] + rx[0, half].astype(f32) + rx[1, half].astype(f32)
    for copy in links.all:
        copy.wait()


def finish(
    out_i, gi_i, dwa_i, dwb_i, dwo_i, dqkv_i, sv_i,
    out, loss, gi, gwq, gbq, gwk, gwv, gbv, gwo, gob, gg1, gb1, gup, gub, gdn, gdb, gg2, gb2,
):
    c = lax.axis_index("col")
    out[...] = out_i[...]
    count = sv_i[7:8, 0:1] * 0.25
    factor = SLOTS / count
    loss[0] = jnp.sum(sv_i[6:7, 0:1] / (2.0 * D * count))
    gi[...] = gi_i[...] * factor
    low, high = dqkv_i[0] * factor, dqkv_i[1] * factor
    at = [h * HL for h in range(HEADS)]
    gwq[...] = jnp.concatenate([low[:, i : i + HD] for i in at], axis=1)
    parts = []
    for i in at:
        parts += [low[:, i + HD : i + QC], high[:, i : i + QC - HD]]
    gwk[...] = jnp.concatenate(parts, axis=1)
    gwv[...] = jnp.concatenate([high[:, i + QC - HD : i + QC] for i in at], axis=1)
    gbq[...] = jnp.concatenate([low[j : j + 1, i + QC : i + HL] for i in at for j in (0, 1)], axis=1)
    gbv[...] = jnp.concatenate([high[j : j + 1, i + QC : i + HL] for i in at for j in (1, 2)], axis=1)
    gwo[...] = dwo_i[...] * factor
    for i, ref in enumerate((gup, gdn)):
        for half in range(2):
            ref[:, half * FA // 2 : (half + 1) * FA // 2] = dwa_i[half, i] * factor
            at = FA + half * FB // 2
            ref[:, at : at + FB // 2] = dwb_i[half, i] * factor
    sums = sv_i[...] * factor
    for j in range(4):

        @pl.when(c == j)
        def _(j=j):
            for i in range(4):
                gub[i : i + 1] = sums[8 + j : 9 + j, i * 128 : (i + 1) * 128]
            for i in range(2):
                at = (j % 2) * FB + i * 128
                gub[4 + i : 5 + i] = sums[12 + j // 2 : 13 + j // 2, at : at + 128]
            for i, ref in enumerate((gob, gg1, gb1, gdb, gg2, gb2)):
                ref[...] = sums[i : i + 1, j * C : (j + 1) * C]


def local_step(
    inputs, teacher, lengths, query_weight, query_bias, key_weight, value_weight, value_bias,
    output_weight, output_bias, first_gain, first_shift, up_weight, up_bias, down_weight,
    down_bias, second_gain, second_shift,
):
    anyspec = pl.BlockSpec(memory_space=pl.ANY)
    vm = pl.BlockSpec(memory_space=pltpu.VMEM)
    sds = jax.ShapeDtypeStruct
    V = pltpu.VMEM
    vectors = [
        v.reshape(1, -1)
        for v in (
            output_bias, first_gain, first_shift, down_bias, second_gain, second_shift,
            query_bias, value_bias,
        )
    ]
    vectors.append(up_bias.reshape(6, 128))
    got = pl.pallas_call(
        layer,
        name="layer",
        out_shape=(
            sds((C, LEN), bf16),
            sds((C, LEN), f32),
            sds((2, 2, RB, FA // 2), f32),
            sds((2, 2, RB, FB // 2), f32),
            sds((RB, C), f32),
            sds((2, RB, HW), f32),
            sds((16, D), f32),
        ),
        in_specs=[anyspec, anyspec, pl.BlockSpec(memory_space=pltpu.SMEM)] + [anyspec] * 15,
        out_specs=(anyspec, vm, vm, vm, vm, vm, vm),
        scratch_shapes=[
            V((D, LEN), bf16),
            V((4, C, TOK), bf16),
            V((2, 16, RB, 4 * FA), bf16),
            V((2, 16, RB, 4 * FB), bf16),
            V((2, 16, RB, HW), bf16),
            V((2, 16, RB, HW), bf16),
            V((4, RB, C), bf16),
            V((D, 3 * C), bf16),
            V((4, 16, C), f32),
            V((4, 8, D), f32),
            V((D, 128), f32),
            V((2 * C, LEN), bf16),
            V((HEADS, LEN, 2 * HD), bf16),
            V((HEADS, 2 * HD, LEN), bf16),
            V((HEADS, HD + 16, LEN), bf16),
            V((HEADS, LEN, 2 * HD), bf16),
            V((HEADS, LEN, LEN), bf16),
            V((HEADS, 8, LEN), f32),
            V((C, LEN), bf16),
            V((4, C, TOK), bf16),
            V((D, TOK), f32),
            V((D, TOK), f32),
            V((D, TOK), f32),
            V((2, 2, TOK, FF // 2), bf16),
            V((2, D, TOK), bf16),
            V((TOK, FF), bf16),
            V((2, TOK, FF // 2), bf16),
            V((2, D, TOK), bf16),
            V((2, 16, RB, 2 * FA), bf16),
            V((2, 16, RB, 2 * FB), bf16),
            V((2, 16, RB, 2 * HL), bf16),
            V((2, 16, RB, HL), bf16),
            V((16, RB, 2 * HL), bf16),
            V((16, RB, HL), bf16),
            V((2, 16, RB, HW), bf16),
            V((16, RB, HW), bf16),
            V((C, LEN), bf16),
            V((4, C, TOK), bf16),
            V((TOK, D), bf16),
            V((D, TOK), bf16),
            V((3 * C, LEN), bf16),
            V((3, C, LEN), bf16),
            V((2, C // 2, LEN), bf16),
            V((2, 2, C // 2, LEN), bf16),
            V((2, 4, RB, 2 * FA), bf16),
            V((2, 2, 4, RB, 2 * FA), bf16),
            V((2, 4, RB, 2 * FA), bf16),
            V((2, 3, RB, 2 * FA), bf16),
            V((2, RB, 2 * FA), bf16),
            V((2, 3, RB, FA // 2), bf16),
            V((2, 2, 8, RB, FB // 2), bf16),
            V((2, 2, 2, 8, RB, FB // 2), bf16),
            V((2, 16, RB, FB // 2), bf16),
            V((2, 3, 4, RB, FB // 2), bf16),
            V((2, 4, RB, FB // 2), bf16),
            V((2, 3, RB, FB // 2), bf16),
            V((3, 4, RB, 2 * HL), bf16),
            V((3, 4, RB, HL), bf16),
            V((4, RB, 2 * HL), bf16),
            V((4, RB, HL), bf16),
            V((3, RB, 2 * HL), bf16),
            V((3, RB, HL), bf16),
            V((3, 4, RB, HW), bf16),
            V((4, RB, HW), bf16),
            V((3, RB, HW), bf16),
            V((2, RB, HW), bf16),
            V((4, RB, C), bf16),
            V((3, RB, C), bf16),
            V((2, 2, RB, FA // 2), f32),
            V((2, 2, RB, FB // 2), f32),
            V((2, RB, HW), f32),
            V((8, TOK), f32),
            V((D, 128), f32),
            V((16, D), f32),
            V((10, 16, D), f32),
            V((2, RB, D), bf16),
            V((3, RB, C), bf16),
            V((8, 1, C), f32),
            V((6, 128), f32),
            pltpu.SemaphoreType.DMA((20,)),
            pltpu.SemaphoreType.DMA((N_SEM,)),
            pltpu.SemaphoreType.DMA((N_SEM,)),
        ],
        compiler_params=pltpu.CompilerParams(
            collective_id=0, has_side_effects=True, vmem_limit_bytes=62 * 2**20
        ),
    )(
        inputs, teacher, lengths, query_weight, key_weight, value_weight, output_weight.T,
        up_weight, down_weight, *vectors,
    )
    vector = sds((1, C), f32)
    weight = sds((RB, C), f32)
    wide = sds((RB, D), f32)
    done = pl.pallas_call(
        finish,
        name="finish",
        out_shape=(
            sds((C, LEN), bf16), sds((1,), f32), sds((C, LEN), f32),
            weight, vector, weight, weight, vector, weight,
            vector, vector, vector, wide, sds((6, 128), f32), wide, vector, vector, vector,
        ),
        in_specs=[vm] * 7,
        out_specs=(vm, pl.BlockSpec(memory_space=pltpu.SMEM)) + (vm,) * 16,
    )(*got)
    shapes = [
        (C, LEN), (), (C, LEN), (RB, C), (C,), (RB, C), (RB, C), (C,), (RB, C), (C,), (C,), (C,),
        (RB, D), (D,), (RB, D), (C,), (C,), (C,),
    ]
    done = [o.reshape(shape) for o, shape in zip(done, shapes)]
    done[8] = done[8].T
    return tuple(done)


def solution(mesh):
    split = Mesh(
        mesh.devices.reshape(mesh.shape["dp"], 4, 4, mesh.shape["col"]), AXES
    )
    tokens = P("col", DP_ROW)
    weight = P(ROW, "col")
    vector = P("col")
    return jax.shard_map(
        local_step,
        mesh=split,
        in_specs=(
            tokens, tokens, P(DP_ROW), weight, vector, weight, weight, vector,
            P("col", ROW), vector, vector, vector, weight, vector, weight,
            vector, vector, vector,
        ),
        out_specs=(
            tokens, P(), tokens, weight, vector, weight, weight, vector,
            P("col", ROW), vector, vector, vector, weight, vector, weight,
            vector, vector, vector,
        ),
        check_vma=False,
    )
```

```python
import jax
import jax.numpy as jnp
from jax import lax
from jax.experimental import pallas as pl
from jax.experimental.pallas import tpu as pltpu
from jax.sharding import Mesh
from jax.sharding import PartitionSpec as P

D = 768
FF = 3072
LEN = 1024
HD = 64
HEADS = 3
C = 192
TOK = 256
RB = 48
SLOTS = 32768
EPS = 1e-12
MASK = -1e30
ROOT_HALF = 0.7071067811865476
INV_ROOT_TAU = 0.3989422804014327
AXES = ("dp", "row_0", "row_1", "col")
ROW = ("row_0", "row_1")
DP_ROW = ("dp", "row_0", "row_1")
N_SEM = 90
HL = 128
QC = 96
FA = 512
FB = 256
WT = 512
QH = 288
HW = 384
f32 = jnp.float32
bf16 = jnp.bfloat16


def mm(a, b):
    return lax.dot_general(a, b, (((1,), (0,)), ((), ())), preferred_element_type=f32)


def mt(a, b):
    return lax.dot_general(a, b, (((1,), (1,)), ((), ())), preferred_element_type=f32)


def transposed(a):
    return jnp.transpose(a, (1, 0))


class Sent:
    def __init__(self, copy):
        self.copy, self.open_send, self.open_recv = copy, True, True

    def wait_send(self):
        if self.open_send:
            self.copy.wait_send()
        self.open_send = False

    def wait_recv(self):
        if self.open_recv:
            self.copy.wait_recv()
        self.open_recv = False

    def wait(self):
        self.wait_send()
        self.wait_recv()


class Batch(Sent):
    def __init__(self, ssem, rsem, whole):
        self.ssem, self.rsem, self.whole, self.dev = ssem, rsem, whole, None
        super().__init__(None)

    def copy_of(self, src, dst):
        return pltpu.make_async_remote_copy(
            src_ref=src,
            dst_ref=dst,
            send_sem=self.ssem,
            recv_sem=self.rsem,
            device_id=self.dev,
            device_id_type=pl.DeviceIdType.MESH,
        )

    def send(self, src, dst, dev):
        self.dev = dev
        self.copy_of(src, dst).start()

    def wait_send(self):
        if self.open_send:
            self.copy = self.copy_of(self.whole, self.whole)
        super().wait_send()

    def wait_recv(self):
        if self.open_recv:
            self.copy = self.copy_of(self.whole, self.whole)
        super().wait_recv()


class Links:
    def __init__(self, ssem, rsem):
        self.ssem, self.rsem, self.n, self.all = ssem, rsem, 0, []

    def send(self, src, dst, dev):
        copy = pltpu.make_async_remote_copy(
            src_ref=src,
            dst_ref=dst,
            send_sem=self.ssem.at[self.n],
            recv_sem=self.rsem.at[self.n],
            device_id=dev,
            device_id_type=pl.DeviceIdType.MESH,
        )
        copy.start()
        self.n += 1
        self.all.append(Sent(copy))
        return self.all[-1]

    def batch(self, whole):
        self.all.append(Batch(self.ssem.at[self.n], self.rsem.at[self.n], whole))
        self.n += 1
        return self.all[-1]


class RingGather:
    def __init__(self, links, ref, whole, plus, minus, plus_parts, minus_parts):
        self.ref, self.plus, self.minus = ref, plus, minus
        self.plus_parts, self.minus_parts = plus_parts, minus_parts
        half = len(plus_parts)
        self.left_on, self.left_end = links.batch(whole(half)), links.batch(whole(half))
        self.right_on, self.right_end = links.batch(whole(half)), links.batch(whole(half))
        self.far = links.batch(whole(2 * half))

    def send_plus(self, part):
        own = self.ref("me", part)
        batch = self.left_on if part in self.plus_parts else self.left_end
        batch.send(own, own, self.plus)

    def send_minus(self, part):
        own = self.ref("me", part)
        batch = self.right_on if part in self.minus_parts else self.right_end
        batch.send(own, own, self.minus)

    def send(self, part):
        self.send_plus(part)
        self.send_minus(part)

    def first(self):
        for part in self.plus_parts:
            self.send_plus(part)
        for part in self.minus_parts:
            self.send_minus(part)

    def rest(self):
        for part in self.minus_parts:
            self.send_plus(part)
        for part in self.plus_parts:
            self.send_minus(part)

    def forward(self):
        self.left_on.wait_recv()
        for part in self.plus_parts:
            ref = self.ref("left", part)
            self.far.send(ref, ref, self.plus)
        self.right_on.wait_recv()
        for part in self.minus_parts:
            ref = self.ref("right", part)
            self.far.send(ref, ref, self.minus)

    def wait(self, at):
        batches = {
            "left": (self.left_on, self.left_end),
            "right": (self.right_on, self.right_end),
            "far": (self.far,),
        }
        for batch in batches[at]:
            batch.wait_recv()


class DirectGather:
    def __init__(self, links, ref, whole, devs):
        self.ref, self.devs, self.batch = ref, devs, links.batch(whole(12))

    def send(self, part):
        own = self.ref("me", part)
        for dev in self.devs:
            self.batch.send(own, own, dev)


class DirectSum:
    def __init__(self, links, own, recv, devs):
        self.own, self.recv, self.devs, self.batch = own, recv, devs, links.batch(recv)

    def start(self):
        for i, at in enumerate(("right", "left", "far")):
            for p in range(4):
                self.batch.send(self.own(at, p), self.recv.at[i, p], self.devs[i])

    def total(self, p):
        self.batch.wait_recv()
        total = self.own("me", p)[...].astype(f32)
        for i in range(3):
            total = total + self.recv[i, p].astype(f32)
        return total


class RingSum:
    def __init__(self, links, own, mid, recv, plus, minus, parts):
        self.own, self.mid, self.recv, self.plus, self.minus = own, mid, recv, plus, minus
        half = parts // 2
        self.low, self.high = range(half), range(half, parts)
        self.mid_left = links.batch(mid.at[pl.ds(0, half)])
        self.mid_right = links.batch(mid.at[pl.ds(half, half)])
        self.left, self.right = links.batch(recv.at[0]), links.batch(recv.at[1])

    def first(self):
        for p in self.low:
            self.mid_left.send(self.own("far", p), self.mid.at[p], self.plus)
        for p in self.high:
            self.mid_right.send(self.own("far", p), self.mid.at[p], self.minus)

    def direct_right(self):
        for p in self.high:
            self.left.send(self.own("right", p), self.recv.at[0, p], self.plus)

    def direct_left(self):
        for p in self.low:
            self.right.send(self.own("left", p), self.recv.at[1, p], self.minus)

    def direct(self):
        self.direct_right()
        self.direct_left()

    def middle(self):
        self.mid_left.wait_recv()
        for p in self.low:
            self.mid[p] = self.plus_f32(self.own("right", p)[...], self.mid[p])
            self.left.send(self.mid.at[p], self.recv.at[0, p], self.plus)
        self.mid_right.wait_recv()
        for p in self.high:
            self.mid[p] = self.plus_f32(self.own("left", p)[...], self.mid[p])
            self.right.send(self.mid.at[p], self.recv.at[1, p], self.minus)

    @staticmethod
    def plus_f32(a, b):
        return (a.astype(f32) + b.astype(f32)).astype(bf16)

    def wait(self):
        self.left.wait_recv()
        self.right.wait_recv()

    def total(self, p):
        self.wait()
        total = self.own("me", p)[...].astype(f32)
        return total + self.recv[0, p].astype(f32) + self.recv[1, p].astype(f32)


def layer(
    x_in, t_in, len_in, wq_in, wk_in, wv_in, wo_in, up_in, down_in,
    ob_in, g1_in, b1_in, db_in, g2_in, b2_in, qb_in, vb_in, ub_in,
    out_o, gi_o, dwa_o, dwb_o, dwo_o, dqkv_o, sv_o,
    xf, tf, wa, wb, wq2, wo2, wo4, wqkv, vec, ub, vcol, qkvt, ktm, qaug, vaug, vtm, pst, linv,
    ctxt, ctxa, hid, nrm, sg, bstore, astore, slope, brecv, arecv,
    ga, gb, gqa, gqb, gra, grb, gao, gor, dctx, dct, outt, delta,
    dqkvt, dxp, rxi, rx, im, rm, s1, r2, s2, r3, zi, zr, sb0, br, sb1, rb2,
    rqa, rqb, sqa, sqb, ra2, rb3, ro, so1, ro2, so2, so4, ro3,
    x1, xb1, xq1, stat, gcol, sv, rs0, rsv, wown, wqs, vrow, ubs,
    lsem, ssem, rsem,
):
    d = lax.axis_index("dp")
    y = lax.axis_index("row_0")
    x = lax.axis_index("row_1")
    c = lax.axis_index("col")
    e = 1 - d
    r = 4 * y + x
    a_me = x * e + y * d
    b_me = y * e + x * d

    def around(me):
        return {
            "me": me,
            "left": lax.rem(me + 3, 4),
            "right": lax.rem(me + 1, 4),
            "far": lax.rem(me + 2, 4),
        }

    b_at, c_at = around(b_me), around(c)

    def ridx(a, b):
        return (4 * b + a) * e + (4 * a + b) * d

    def zdev(k):
        return {"col": lax.rem(c + k, 4)}

    def adev(k):
        return {"row_0": lax.rem(y + k * d, 4), "row_1": lax.rem(x + k * e, 4)}

    def bdev(k):
        return {"row_0": lax.rem(y + k * e, 4), "row_1": lax.rem(x + k * d, 4)}

    sib = {"dp": e}
    links = Links(ssem, rsem)

    def wait_all(copies):
        for copy in copies:
            copy.wait_recv()

    def triple(whole, src, dst, dev):
        batch = links.batch(whole)
        for k in (1, 3, 2):
            batch.send(src(k), dst(k), dev(k))
        return batch

    def region(body):
        @pl.when(e + d == 1 + d * e)
        def _():
            body()

    def unrolled(n, body, carry):
        for i in range(n):
            carry = body(i, carry)
        return carry

    def cols(i, width):
        if isinstance(i, int):
            return pl.ds(i * width, width)
        return pl.ds(pl.multiple_of(i * width, 128), width)

    def rows(i, height):
        if isinstance(i, int):
            return pl.ds(i * height, height)
        return pl.ds(pl.multiple_of(i * height, 16), height)

    n_local = [0]

    def local(src, dst):
        copy = pltpu.make_async_copy(src, dst, lsem.at[n_local[0]])
        copy.start()
        n_local[0] += 1
        return copy

    xrows = rows(c, C)
    tcols = cols(c, TOK)
    bar = pltpu.get_barrier_semaphore()
    for k in (1, 2, 3):
        for dev in (zdev(k), adev(k), bdev(k)):
            pl.semaphore_signal(bar, inc=1, device_id=dev, device_id_type=pl.DeviceIdType.MESH)
    pl.semaphore_signal(bar, inc=1, device_id=sib, device_id_type=pl.DeviceIdType.MESH)
    cw = [local(ref, wqs.at[i]) for i, ref in enumerate((wq_in, wk_in, wv_in))]
    cup = local(up_in, wown.at[0])
    cdn = local(down_in, wown.at[1])
    cx = local(x_in, xf.at[xrows])
    ct = local(t_in.at[:, tcols], tf.at[c])
    cwo = local(wo_in, wo4.at[c])
    cv = [
        local(ref, vrow.at[i])
        for i, ref in enumerate((ob_in, g1_in, b1_in, db_in, g2_in, b2_in, qb_in, vb_in))
    ]
    cub = local(ub_in, ubs)
    for copy in cw:
        copy.wait()
    own_qkv = [wqs[i] for i in range(3)]
    own_qkv = jnp.concatenate(
        [w[:, h * HD : (h + 1) * HD] for h in range(HEADS) for w in own_qkv], axis=1
    )
    own_qkv = jnp.where(d == 0, own_qkv[:, 0:QH], own_qkv[:, QH:])
    wq2[d, r] = jnp.concatenate([own_qkv, jnp.zeros((RB, HW - QH), bf16)], axis=1)
    pl.semaphore_wait(bar, 10)

    def along_a(ref, whole):
        return triple(whole, lambda k: ref, lambda k: ref, adev)

    def of_b(ref):
        return lambda at, k: ref(ridx(lax.rem(a_me + 4 - k, 4), b_at[at]))

    def direct_b(ref, whole):
        return DirectGather(links, of_b(ref), whole, (bdev(1), bdev(3), bdev(2)))

    def wq_ref(i):
        return wq2.at[d, i]

    def wo_ref(i):
        return wo2.at[d, i]

    def wa_ref(i):
        return wa.at[d, i]

    def wb_ref(i):
        return wb.at[d, i, :, cols(c, FB)]

    def some(buf):
        return lambda n: buf.at[d, pl.ds(0, n)]

    def some_b(n):
        return wb.at[d, pl.ds(0, n), :, cols(c, FB)]

    class ToSibling:
        def __init__(self, whole):
            self.batch = links.batch(whole)

        def send(self, ref):
            self.batch.send(ref, ref, sib)

        def wait(self):
            self.batch.wait_recv()

    wq_a = along_a(wq_ref(r), some(wq2)(3))
    wq_b = direct_b(wq_ref, some(wq2))
    wq_b.send(0)
    cup.wait()
    cdn.wait()
    wz = triple(
        wa.at[d, 0, :, pl.ds(0, 3 * FA)],
        lambda k: wown.at[d, :, pl.ds(0, FA)],
        lambda k: wa.at[d, r, :, cols(c, FA)],
        zdev,
    )
    cx.wait()
    x_z = RingGather(
        links,
        lambda at, half: xf.at[rows(2 * c_at[at] + half, C // 2)],
        lambda n: xf.at[pl.ds(0, n * C // 2)],
        zdev(1), zdev(3), (0,), (1,),
    )
    x_z.first()
    cwo.wait()
    for i, copy in enumerate(cv):
        copy.wait()
        vec[c, i : i + 1, :] = vrow[i]
    cub.wait()
    ub[c, 0:1, :] = jnp.concatenate([ubs[i : i + 1] for i in range(6)], axis=1)
    oz = triple(wo4.at[pl.ds(0, 3)], lambda k: wo4.at[c], lambda k: wo4.at[c], zdev)
    vz = triple(vec.at[pl.ds(0, 3)], lambda k: vec.at[c], lambda k: vec.at[c], zdev)
    uz = triple(
        ub.at[pl.ds(0, 3), 0:1], lambda k: ub.at[c, 0:1], lambda k: ub.at[c, 0:1], zdev
    )
    wa[d, r, :, cols(c, FA)] = wown[d, :, 0:FA]
    wb[d, r, :, cols(c, FB)] = wown[d, :, FA:]
    wb_a = along_a(wb_ref(r), some_b(3))
    wb_b = direct_b(wb_ref, some_b)
    wb_b.send(0)

    wq_a.wait_recv()
    for k in (1, 3, 2):
        wq_b.send(k)
    wq_s = ToSibling(wq2.at[d])
    for j in range(4):
        wq_s.send(wq_ref(ridx(j, b_me)))
    wb_a.wait_recv()
    for k in (1, 3, 2):
        wb_b.send(k)
    x_z.rest()
    wz.wait_recv()
    wa_a = [links.batch(wa_ref(0)) for _ in range(3)]
    for i, k in enumerate((1, 3, 2)):
        wa_a[i].send(wa_ref(r), wa_ref(r), adev(k))
    wa_b = RingGather(links, of_b(wa_ref), some(wa), bdev(1), bdev(3), (0, 2), (1, 3))
    wa_b.send(0)
    oz.wait_recv()
    own_wo = jnp.concatenate([wo4[j] for j in range(4)], axis=1)
    wo2[d, r] = jnp.where(d == 0, own_wo[:, 0:HW], own_wo[:, HW:])
    wo_a = along_a(wo_ref(r), some(wo2)(3))
    wo_b = direct_b(wo_ref, some(wo2))
    wo_b.send(0)
    wq_b.batch.wait_recv()
    for at in ("left", "right", "far"):
        for k in range(4):
            wq_s.send(wq_b.ref(at, k))
    x_z.forward()
    wo_s = ToSibling(wo2.at[d])
    wo_s.send(wo_ref(r))
    wa_s = ToSibling(wa.at[d])
    wa_s.send(wa_ref(r))
    for i, k in enumerate((1, 3, 2)):
        wa_a[i].wait_recv()
        wa_b.send(k)
        wa_s.send(wa_b.ref("me", k))
    wo_a.wait_recv()
    for k in (1, 3, 2):
        wo_b.send(k)
        wo_s.send(wo_b.ref("me", k))
    vown = transposed(vec[c])
    length = len_in[0]

    for at in ("left", "right", "far"):
        x_z.wait(at)
    wb_b.batch.wait_recv()

    def wb_z(at, half):
        return wb.at[d, pl.ds(half * 8, 8), :, cols(c_at[at], FB)]

    def some_z(n):
        return wb.at[d, pl.ds(0, 8), :, pl.ds(0, n * FB)]

    wb_zg = RingGather(links, wb_z, some_z, zdev(1), zdev(3), (0,), (1,))
    wb_zg.first()
    wb_s = ToSibling(wb.at[d])
    wb_s.send(wb.at[d, :, :, cols(c, FB)])
    wq_s.wait()
    q_bias = vown[:, 6:7]
    v_bias = vown[:, 7:8]
    lane_iota = lax.broadcasted_iota(jnp.int32, (1, TOK), 1)
    first_row = lax.broadcasted_iota(jnp.int32, (HD, TOK), 0) == 0

    def qkv_chunk(i, carry):
        at = cols(i, TOK)
        tok = xf[:, at]
        qkv = mm(dxp[:, :, 0:D].reshape(3 * C, D), tok)
        bias = jnp.where(lane_iota + i * TOK < length, 0.0, MASK)
        bias = jnp.where(first_row, jnp.broadcast_to(bias, (HD, TOK)), 0.0).astype(bf16)
        ones = jnp.where(first_row, 1.0, 0.0).astype(bf16)
        for h in range(HEADS):
            hs = slice(h * HD, (h + 1) * HD)
            of = h * C
            q = (qkv[of : of + HD] + q_bias[hs]).astype(bf16)
            q = (q.astype(f32) * (HD**-0.5)).astype(bf16)
            k = qkv[of + HD : of + 2 * HD].astype(bf16)
            v = (qkv[of + 2 * HD : of + 3 * HD] + v_bias[hs]).astype(bf16)
            qkvt[h * HD : (h + 1) * HD, at] = q
            qkvt[C + h * HD : C + (h + 1) * HD, at] = k
            qaug[h, 0:HD, at] = q
            qaug[h, HD : 2 * HD, at] = ones
            vaug[h, 0:HD, at] = v
            vaug[h, HD : HD + 16, at] = ones[0:16]
            ktm[h, at, :] = transposed(jnp.concatenate([k, bias], axis=0))
            vtm[h, at, :] = transposed(jnp.concatenate([v, ones], axis=0))
        return carry

    w_low = transposed(wq2[0].reshape(D, HW))[0:QH]
    w_high = transposed(wq2[1].reshape(D, HW))[0:QH]
    dxp[0, :, 0:D] = w_low[0:C]
    dxp[1, 0 : QH - C, 0:D] = w_low[C:]
    dxp[1, QH - C :, 0:D] = w_high[0 : QH - C]
    dxp[2, :, 0:D] = w_high[QH - C :]
    unrolled(4, qkv_chunk, 0)

    wb_zg.rest()

    def fwd_head(h):
        score = mm(ktm[h], qaug[h, :, 0:WT])
        for n in range(LEN // WT):
            at = cols(n, WT)
            later = mm(ktm[h], qaug[h, :, cols(n + 1, WT)]) if (n + 1) * WT < LEN else None
            top = jnp.max(score, axis=0, keepdims=True)
            probs = jnp.exp(score - top).astype(bf16)
            pst[h, :, at] = probs
            both = mm(vaug[h], probs)
            inv = 1.0 / both[HD : HD + 1]
            linv[h, 0:1, at] = inv
            ctxt[h * HD : (h + 1) * HD, at] = (both[0:HD] * inv).astype(bf16)
            score = later

    cc = links.batch(ctxa.at[pl.ds(0, 3)])

    def context_out(h):
        hrow = pl.ds(h * HD, HD)
        ctxa[c, hrow] = ctxt[hrow, tcols]
        for k in (1, 3, 2):
            there = cols(lax.rem(c + k, 4), TOK)
            cc.send(ctxt.at[hrow, there], ctxa.at[c, hrow], zdev(k))

    def pass_on(ring, sent, at):
        ring.wait(at)
        for k in range(4):
            sent.send(ring.ref(at, k))

    fwd_head(0)
    context_out(0)
    wa_b.forward()
    pass_on(wa_b, wa_s, "left")
    pass_on(wa_b, wa_s, "right")
    fwd_head(1)
    context_out(1)
    wo_b.batch.wait_recv()
    for at in ("left", "right", "far"):
        for k in range(4):
            wo_s.send(wo_b.ref(at, k))
    wait_all((vz, uz))
    for i in range(4):
        vcol[i * C : (i + 1) * C, 0:16] = transposed(vec[i])
    fwd_head(2)
    context_out(2)
    wb_zg.forward()
    pass_on(wa_b, wa_s, "far")
    for i in range(2):
        wqkv[:, i * QH : (i + 1) * QH] = wq2[i].reshape(D, HW)[:, 0:QH]
    wo_s.wait()
    cc.wait_recv()
    ct.wait()
    tt = triple(
        tf.at[pl.ds(0, 3)],
        lambda k: t_in.at[:, cols(lax.rem(c + k, 4), TOK)],
        lambda k: tf.at[c],
        zdev,
    )

    def norm_stats(ref):
        v = ref[...]
        mean = jnp.sum(v, axis=0, keepdims=True) * (1.0 / D)
        square = jnp.sum(v * v, axis=0, keepdims=True) * (1.0 / D)
        return mean, lax.rsqrt(square - mean * mean + EPS)


    @region
    def _():
        acc = xf[:, tcols].astype(f32) + vcol[:, 0:1]
        for j in range(2):
            w = wo2[j].reshape(D, HW)
            acc = acc + mm(w, ctxa[2 * j : 2 * j + 2].reshape(HW, TOK))
        hid[...] = acc
        mean1, inv1 = norm_stats(hid)
        stat[0:1] = inv1

        def norm1(i, carry):
            row = rows(i, C)
            n = (hid[row] - mean1) * inv1
            nrm[row] = n
            h = n * vcol[row, 1:2] + vcol[row, 2:3]
            hid[row] = h + vcol[row, 3:4]
            astore[0, row] = h.astype(bf16)
            return carry

        unrolled(4, norm1, 0)
        outt[...] = transposed(astore[0])

    for at in ("left", "right"):
        wb_zg.wait(at)
        wb_s.send(wb.at[d, :, :, cols(c_at[at], FB)])

    wa_s.wait()

    def w_chunk(ref, i):
        return ref[:, :, cols(i, FA)].reshape(D, FA)

    def halves(chunk):
        if chunk < 4:
            return [(half, chunk * FA // 2, FA // 2) for half in range(2)]
        pairs = [(half, j) for j in (2 * chunk - 8, 2 * chunk - 7) for half in range(2)]
        return [(half, 2 * FA + j * FB // 2, FB // 2) for half, j in pairs]

    def store_halves(w, chunk, v):
        at = 0
        for half, to, width in halves(chunk):
            bstore[w, half, :, to : to + width] = v[:, at : at + width]
            at += width

    def load_halves(w, chunk):
        return jnp.concatenate(
            [bstore[w, half, :, to : to + width] for half, to, width in halves(chunk)], axis=1
        )

    def up_of(ref, bias, first):
        def up_chunk(i, carry):
            at = cols(first + i, FA)
            pre = mm(outt[...], w_chunk(ref, i)) + bias(i)
            half = 0.5 * (1.0 + lax.erf(pre * ROOT_HALF))
            store_halves(1, first + i, (pre * half).astype(bf16))
            slope[:, at] = (half + pre * jnp.exp(-0.5 * pre * pre) * INV_ROOT_TAU).astype(bf16)
            return carry

        return up_chunk

    def bias_a(i):
        return ub[i, 0:1, 0:FA]

    def bias_b(i):
        return jnp.concatenate([ub[2 * i, 0:1, FA:], ub[2 * i + 1, 0:1, FA:]], axis=1)

    region(lambda: unrolled(4, up_of(wa.at[0], bias_a, 0), 0))

    def down_of(ref, first):
        def down_chunk(i, carry):
            hid[...] = hid[...] + mt(w_chunk(ref, i), load_halves(1, first + i))
            return carry

        return down_chunk

    region(lambda: unrolled(4, down_of(wa.at[1], 0), 0))
    wb_zg.wait("far")
    wb_s.send(wb.at[d, :, :, cols(c_at["far"], FB)])
    wb_s.wait()

    @region
    def _():
        unrolled(2, up_of(wb.at[0], bias_b, 4), 0)
        unrolled(2, down_of(wb.at[1], 4), 0)

    ex_down = [links.send(bstore.at[1, e], brecv.at[1], sib)]

    tt.wait_recv()
    valid = lane_iota + c * TOK < length

    zero = jnp.zeros((1, TOK), f32)

    @region
    def _():
        mean2, inv2 = norm_stats(hid)
        gcol[...] = jnp.zeros(gcol.shape, f32)
        sv[...] = jnp.zeros(sv.shape, f32)

        def norm2(i, carry):
            total, crossed, loss = carry
            row = rows(i, C)
            n = (hid[row] - mean2) * inv2
            hid[row] = n
            final = n * vcol[row, 4:5] + vcol[row, 5:6]
            delta[row] = final.astype(bf16)
            g = jnp.where(valid, final - tf[i].astype(f32), 0.0)
            gcol[row, 4:5] = jnp.sum(g * n, axis=1, keepdims=True)
            gcol[row, 5:6] = jnp.sum(g, axis=1, keepdims=True)
            s = g * vcol[row, 4:5]
            sg[row] = s
            return (
                total + jnp.sum(s, axis=0, keepdims=True),
                crossed + jnp.sum(s * n, axis=0, keepdims=True),
                loss + jnp.sum(g * g, axis=0, keepdims=True),
            )

        total2, crossed2, loss_row = unrolled(4, norm2, (zero, zero, zero))
        for i, row in enumerate((inv2, total2, crossed2, loss_row)):
            stat[1 + i : 2 + i] = row

    out_o_own = local(delta.at[xrows], out_o.at[:, tcols])
    fo = triple(
        delta.at[pl.ds(0, 3 * C)],
        lambda k: delta.at[rows(lax.rem(c + k, 4), C)],
        lambda k: out_o.at[:, tcols],
        zdev,
    )

    def norm2_back(i, carry):
        row = rows(i, C)
        s = stat[1:2] * (sg[row] - stat[2:3] * (1.0 / D) - hid[row] * (stat[3:4] * (1.0 / D)))
        sg[row] = s
        low = s.astype(bf16)
        astore[1, row] = low
        gcol[row, 3:4] = jnp.sum(low.astype(f32), axis=1, keepdims=True)
        return carry

    @region
    def _():
        unrolled(4, norm2_back, 0)
        outt[...] = transposed(astore[1])


    ex_down.append(links.send(astore.at[1], arecv.at[1], sib))

    def act_of(ref, first):
        def act_chunk(i, carry):
            at = cols(first + i, FA)
            g = mm(outt[...], w_chunk(ref, i)) * slope[:, at].astype(f32)
            low = g.astype(bf16)
            store_halves(0, first + i, low)
            total = jnp.sum(low.astype(f32), axis=0, keepdims=True)
            sv[8 + first + i : 9 + first + i, 0:FA] = total
            return carry

        return act_chunk

    @region
    def _():
        unrolled(2, act_of(wb.at[1], 4), 0)
        unrolled(4, act_of(wa.at[1], 0), 0)

    ex_up = [
        links.send(astore.at[0], arecv.at[0], sib),
        links.send(bstore.at[0, e], brecv.at[0], sib),
    ]

    def back_of(ref, first):
        def back_chunk(i, carry):
            sg[...] = sg[...] + mt(w_chunk(ref, i), load_halves(0, first + i))
            return carry

        return back_chunk

    def sum_b(own, mid, recv):
        return RingSum(
            links, lambda at, j: own(ridx(j, b_at[at])), mid, recv, bdev(1), bdev(3), 4
        )

    def direct_sum(own, recv):
        return DirectSum(
            links, lambda at, j: own(ridx(j, b_at[at])), recv, (bdev(1), bdev(3), bdev(2))
        )

    def end_b(ring, summed, peer_recv):
        for j in range(4):
            summed[j] = ring.total(j).astype(bf16)
        return triple(
            peer_recv,
            lambda k: summed.at[lax.rem(a_me + k, 4)],
            lambda k: peer_recv.at[k - 1],
            adev,
        )

    def end_a(sends, summed, recv):
        sends.wait_recv()
        total = summed[a_me].astype(f32)
        for k in range(3):
            total = total + recv[k].astype(f32)
        return total

    def add_sibling(ref, other):
        def add(i, carry):
            ref[d, i] = (ref[d, i].astype(f32) + other[i].astype(f32)).astype(bf16)
            return carry

        unrolled(16, add, 0)

    def weight_grad(w):
        @region
        def _():
            for at, ref in ((0, ga), (2 * FA, gb)):
                for lo in range(0, ref.shape[3], FA):
                    cut = pl.ds(at + lo, FA)
                    g = mm(astore[w], bstore[w, d, :, cut]) + mm(arecv[w], brecv[w, :, cut])
                    ref[w, :, :, lo : lo + FA] = g.astype(bf16).reshape(16, RB, FA)

        def z_own(at, half):
            return gb.at[w, pl.ds(half * 8, 8), :, cols(c_at[at], FB // 2)]

        a_ring = sum_b(lambda i: ga.at[w, i], im.at[w], rm.at[w])
        b_ring = RingSum(links, z_own, zi.at[w], zr.at[w], zdev(1), zdev(3), 2)
        a_ring.first()
        b_ring.first()
        return a_ring, b_ring

    region(lambda: unrolled(2, back_of(wb.at[0], 4), 0))
    wait_all(ex_down)
    wd_a, wd_b = weight_grad(1)
    region(lambda: unrolled(4, back_of(wa.at[0], 0), 0))

    def hidden_back(i, carry):
        total, crossed = carry
        row = rows(i, C)
        g = sg[row]
        n = nrm[row]
        gcol[row, 1:2] = jnp.sum(g * n, axis=1, keepdims=True)
        gcol[row, 2:3] = jnp.sum(g, axis=1, keepdims=True)
        s = g * vcol[row, 1:2]
        sg[row] = s
        return (
            total + jnp.sum(s, axis=0, keepdims=True),
            crossed + jnp.sum(s * n, axis=0, keepdims=True),
        )


    fo.wait_send()
    out_o_own.wait()
    wd_a.direct()

    @region
    def _():
        total1, crossed1 = unrolled(4, hidden_back, (zero, zero))

        def norm1_back(i, carry):
            row = rows(i, C)
            s = stat[0:1] * (sg[row] - total1 * (1.0 / D) - nrm[row] * (crossed1 * (1.0 / D)))
            sg[row] = s
            low = s.astype(bf16)
            delta[row] = low
            gcol[row, 0:1] = jnp.sum(low.astype(f32), axis=1, keepdims=True)
            return carry

        unrolled(4, norm1_back, 0)
        outt[...] = transposed(delta[...])
        for i in range(2):
            part = transposed(mm(outt[...], wo2[i].reshape(D, HW)).astype(bf16))
            dct[2 * i : 2 * i + 2] = part.reshape(2, C, TOK)
        dctx[:, tcols] = dct[c]


    dc = []
    for h in range(HEADS):
        hrow = pl.ds(h * HD, HD)
        dc.append(
            triple(
                dct.at[0],
                lambda k: dct.at[lax.rem(c + k, 4), hrow],
                lambda k: dctx.at[hrow, tcols],
                zdev,
            )
        )

    sv[0:8] = transposed(gcol[...])[0:8]
    sv[6:7] = jnp.broadcast_to(jnp.sum(stat[4:5], axis=1, keepdims=True), (1, D))
    sv[7:8] = jnp.broadcast_to(length.astype(f32), (1, D))
    v_sent = [links.send(sv, rs0, sib)]
    v_from = [(0, 0)]
    half8 = pl.ds(pl.multiple_of(8 * d, 8), 8)
    other8 = pl.ds(pl.multiple_of(8 * e, 8), 8)

    def sv_add():
        v_sent.pop().wait()
        lo, n = v_from[-1]
        if n == 0:
            sv[...] = sv[...] + rs0[...]
        else:
            total = sv[half8]
            for i in range(n):
                total = total + rsv[lo + i]
            sv[half8] = total

    def sv_send(dev):
        lo = sum(v_from[-1])
        v_from.append((lo, 3))
        v_sent.append(
            triple(
                rsv.at[pl.ds(lo, 3)],
                lambda k: sv.at[half8],
                lambda k: rsv.at[lo + k - 1],
                dev,
            )
        )

    wait_all(ex_up)
    wd_b.direct()
    wu_a, wu_b = weight_grad(0)
    sv_add()
    sv_send(bdev)

    @region
    def _():
        g = mt(delta[...], ctxa[...].reshape(D, TOK)).astype(bf16)
        for i in range(2):
            gao[i] = g[:, i * HW : (i + 1) * HW].reshape(16, RB, HW)

    go_x = links.send(gao.at[e], gor, sib)
    wd_a.middle()
    wd_b.middle()

    def bwd_head(h, meanwhile=None):
        hrow = pl.ds(h * HD, HD)
        krow = pl.ds(C + h * HD, HD)
        of = h * C

        dk = dv = jnp.zeros((HD, LEN), f32)
        for n in range(LEN // WT):
            at = cols(n, WT)
            inv = linv[h, 0:1, at]
            dc = dctx[hrow, at].astype(f32)
            inner = jnp.sum(dc * ctxt[hrow, at].astype(f32), axis=0, keepdims=True) * inv
            dcs = (dc * inv).astype(bf16)
            probs = pst[h, :, at]
            dv = dv + mt(dcs, probs)
            dp = mm(vtm[h, :, 0:HD], dcs) - inner
            ds = (probs.astype(f32) * dp).astype(bf16)
            dk = dk + mt(qkvt[hrow, at], ds)
            dqkvt[of : of + HD, at] = (mm(qkvt[krow, :], ds) * (HD**-0.5)).astype(bf16)
            if n == 0 and meanwhile is not None:
                meanwhile()
        dqkvt[of + HD : of + 2 * HD] = dk.astype(bf16)
        dqkvt[of + 2 * HD : of + 3 * HD] = dv.astype(bf16)

    spare = HL - QC
    row_iota = lax.broadcasted_iota(jnp.int32, (RB, spare), 0)

    def qkv_grad(h, ref, at):
        of = dqkvt[h * C : (h + 1) * C]
        g = mt(xf[...], of).astype(bf16)
        sums = mt(jnp.ones((8, LEN), bf16), of)[0:1]
        for half in range(2):
            lo = half * QC
            part_rows = jnp.zeros((RB, spare), f32)
            for j in range(3):
                part = sums[:, lo + j * spare : lo + (j + 1) * spare]
                part_rows = jnp.where(row_iota == j, jnp.broadcast_to(part, (RB, spare)), part_rows)
            ref[half, :, :, at : at + QC] = g[:, lo : lo + QC].reshape(16, RB, QC)
            ref[half, :, :, at + QC : at + HL] = jnp.broadcast_to(
                part_rows.astype(bf16)[None], (16, RB, spare)
            )

    dc[0].wait_recv()
    bwd_head(0)
    wu_a.direct()
    wu_b.direct()
    go_x.wait_recv()
    add_sibling(gao, gor)
    o_sum = direct_sum(lambda i: gao.at[d, i], ro)
    o_sum.start()
    dc[1].wait_recv()
    bwd_head(1, lambda: qkv_grad(0, gqa, 0))
    wd_sends = end_b(wd_a, s1.at[1], r2.at[1])
    def total_z(w, ring):
        for half in range(2):
            sb0[w, half * 8 : half * 8 + 8] = ring.total(half).astype(bf16)
        ring_b = direct_sum(lambda i: sb0.at[w, i], br.at[w])
        ring_b.start()
        return ring_b

    wu_a.middle()
    wu_b.middle()


    sv_add()
    sv_send(adev)
    dc[2].wait_recv()
    bwd_head(2, lambda: qkv_grad(1, gqa, HL))

    def dx_part(i, slot=None):
        @region
        def _():
            row = rows(i, C)
            gi_o[...] = mm(wqkv[row], dqkvt[...])
            gi_o[:, tcols] = gi_o[:, tcols] + sg[row]
            if slot is not None:
                dxp[slot] = gi_o[...].astype(bf16)

    SLOT = {"far": 0, "right": 1, "left": 2}

    def dx_own(at, half):
        return dxp.at[SLOT[at], pl.ds(half * (C // 2), C // 2)]

    dx_sum = RingSum(links, dx_own, rxi, rx, zdev(1), zdev(3), 2)
    dx_part(c_at["far"], 0)
    dx_sum.first()
    bd_sum = total_z(1, wd_b)
    xa = links.send(gqa.at[e], gra, sib)
    region(lambda: qkv_grad(2, gqb, 0))
    xb = links.send(gqb.at[e], grb, sib)

    dx_part(c_at["right"], 1)
    dx_sum.direct_right()
    dx_part(c_at["left"], 2)
    dx_sum.direct_left()
    xa.wait_recv()
    add_sibling(gqa, gra)
    qa_sum = direct_sum(lambda i: gqa.at[d, i], rqa)
    qa_sum.start()
    xb.wait_recv()
    add_sibling(gqb, grb)
    qb_sum = direct_sum(lambda i: gqb.at[d, i], rqb)
    qb_sum.start()
    dx_part(c)
    o_sends = end_b(o_sum, so1, ro2)

    def along_z(w, sends):
        s2[w] = end_a(sends, s1.at[w], r2.at[w]).astype(bf16)
        return triple(
            r3.at[w],
            lambda k: s2.at[w, :, cols(lax.rem(c + k, 4), FA // 2)],
            lambda k: r3.at[w, k - 1],
            zdev,
        )

    w3 = {1: along_z(1, wd_sends)}
    wu_sends = end_b(wu_a, s1.at[0], r2.at[0])
    dx_sum.middle()
    bu_sum = total_z(0, wu_b)
    sv_add()
    sv_send(zdev)
    qa_sends = end_b(qa_sum, sqa, ra2)
    w3[0] = along_z(0, wu_sends)
    qb_sends = end_b(qb_sum, sqb, rb3)
    bd_sends = end_b(bd_sum, sb1.at[1], rb2.at[1])
    so2[0] = end_a(o_sends, so1, ro2).astype(bf16)
    o_x = links.send(so2.at[0], so2.at[1], sib)
    bu_sends = end_b(bu_sum, sb1.at[0], rb2.at[0])
    o_x.wait_recv()
    mine, other = so2[0], so2[1]
    low, high = jnp.where(d == 0, mine, other), jnp.where(d == 0, other, mine)
    so4[0], so4[1] = low[:, 0:C], low[:, C:]
    so4[2], so4[3] = high[:, 0:C], high[:, C:]
    o3 = triple(
        ro3, lambda k: so4.at[lax.rem(c + k, 4)], lambda k: ro3.at[k - 1], zdev
    )
    xq1[0, :, 0 : 2 * HL] = end_a(qa_sends, sqa, ra2)
    xq1[0, :, 2 * HL :] = end_a(qb_sends, sqb, rb3)
    q3 = links.send(xq1.at[0], xq1.at[1], sib)
    wait_all((w3[1], w3[0]))
    sv_add()
    v_other = links.send(sv.at[half8], rsv.at[9], sib)
    x1[0] = s2[:, :, cols(c, FA // 2)].astype(f32)
    for w in range(2):
        for k in range(3):
            x1[0, w] = x1[0, w] + r3[w, k].astype(f32)
    w4 = links.send(x1.at[0], x1.at[1], sib)
    xb1[0, 1] = end_a(bd_sends, sb1.at[1], rb2.at[1])
    xb1[0, 0] = end_a(bu_sends, sb1.at[0], rb2.at[0])
    wb4 = links.send(xb1.at[0], xb1.at[1], sib)
    o3.wait_recv()
    ototal = so4[c].astype(f32)
    for k in range(3):
        ototal = ototal + ro3[k].astype(f32)
    dwo_o[...] = ototal
    sv_o[half8] = sv[half8]
    v_other.wait_recv()
    sv_o[other8] = rsv[9]
    w4.wait_recv()
    dwa_o[d] = x1[0]
    dwa_o[e] = x1[1]
    q3.wait_recv()
    dqkv_o[d] = xq1[0]
    dqkv_o[e] = xq1[1]
    wb4.wait_recv()
    dwb_o[d] = xb1[0]
    dwb_o[e] = xb1[1]
    dx_sum.wait()
    for half in range(2):
        row = pl.ds(half * (C // 2), C // 2)
        gi_o[row] = gi_o[row] + rx[0, half].astype(f32) + rx[1, half].astype(f32)
    for copy in links.all:
        copy.wait()


def finish(
    out_i, gi_i, dwa_i, dwb_i, dwo_i, dqkv_i, sv_i,
    out, loss, gi, gwq, gbq, gwk, gwv, gbv, gwo, gob, gg1, gb1, gup, gub, gdn, gdb, gg2, gb2,
):
    c = lax.axis_index("col")
    out[...] = out_i[...]
    count = sv_i[7:8, 0:1] * 0.25
    factor = SLOTS / count
    loss[0] = jnp.sum(sv_i[6:7, 0:1] / (2.0 * D * count))
    gi[...] = gi_i[...] * factor
    low, high = dqkv_i[0] * factor, dqkv_i[1] * factor
    at = [h * HL for h in range(HEADS)]
    gwq[...] = jnp.concatenate([low[:, i : i + HD] for i in at], axis=1)
    parts = []
    for i in at:
        parts += [low[:, i + HD : i + QC], high[:, i : i + QC - HD]]
    gwk[...] = jnp.concatenate(parts, axis=1)
    gwv[...] = jnp.concatenate([high[:, i + QC - HD : i + QC] for i in at], axis=1)
    gbq[...] = jnp.concatenate([low[j : j + 1, i + QC : i + HL] for i in at for j in (0, 1)], axis=1)
    gbv[...] = jnp.concatenate([high[j : j + 1, i + QC : i + HL] for i in at for j in (1, 2)], axis=1)
    gwo[...] = dwo_i[...] * factor
    for i, ref in enumerate((gup, gdn)):
        for half in range(2):
            ref[:, half * FA // 2 : (half + 1) * FA // 2] = dwa_i[half, i] * factor
            at = FA + half * FB // 2
            ref[:, at : at + FB // 2] = dwb_i[half, i] * factor
    sums = sv_i[...] * factor
    for j in range(4):

        @pl.when(c == j)
        def _(j=j):
            for i in range(4):
                gub[i : i + 1] = sums[8 + j : 9 + j, i * 128 : (i + 1) * 128]
            for i in range(2):
                at = (j % 2) * FB + i * 128
                gub[4 + i : 5 + i] = sums[12 + j // 2 : 13 + j // 2, at : at + 128]
            for i, ref in enumerate((gob, gg1, gb1, gdb, gg2, gb2)):
                ref[...] = sums[i : i + 1, j * C : (j + 1) * C]


def local_step(
    inputs, teacher, lengths, query_weight, query_bias, key_weight, value_weight, value_bias,
    output_weight, output_bias, first_gain, first_shift, up_weight, up_bias, down_weight,
    down_bias, second_gain, second_shift,
):
    anyspec = pl.BlockSpec(memory_space=pl.ANY)
    vm = pl.BlockSpec(memory_space=pltpu.VMEM)
    sds = jax.ShapeDtypeStruct
    V = pltpu.VMEM
    vectors = [
        v.reshape(1, -1)
        for v in (
            output_bias, first_gain, first_shift, down_bias, second_gain, second_shift,
            query_bias, value_bias,
        )
    ]
    vectors.append(up_bias.reshape(6, 128))
    got = pl.pallas_call(
        layer,
        name="layer",
        out_shape=(
            sds((C, LEN), bf16),
            sds((C, LEN), f32),
            sds((2, 2, RB, FA // 2), f32),
            sds((2, 2, RB, FB // 2), f32),
            sds((RB, C), f32),
            sds((2, RB, HW), f32),
            sds((16, D), f32),
        ),
        in_specs=[anyspec, anyspec, pl.BlockSpec(memory_space=pltpu.SMEM)] + [anyspec] * 15,
        out_specs=(anyspec, vm, vm, vm, vm, vm, vm),
        scratch_shapes=[
            V((D, LEN), bf16),
            V((4, C, TOK), bf16),
            V((2, 16, RB, 4 * FA), bf16),
            V((2, 16, RB, 4 * FB), bf16),
            V((2, 16, RB, HW), bf16),
            V((2, 16, RB, HW), bf16),
            V((4, RB, C), bf16),
            V((D, 3 * C), bf16),
            V((4, 16, C), f32),
            V((4, 8, D), f32),
            V((D, 128), f32),
            V((2 * C, LEN), bf16),
            V((HEADS, LEN, 2 * HD), bf16),
            V((HEADS, 2 * HD, LEN), bf16),
            V((HEADS, HD + 16, LEN), bf16),
            V((HEADS, LEN, 2 * HD), bf16),
            V((HEADS, LEN, LEN), bf16),
            V((HEADS, 8, LEN), f32),
            V((C, LEN), bf16),
            V((4, C, TOK), bf16),
            V((D, TOK), f32),
            V((D, TOK), f32),
            V((D, TOK), f32),
            V((2, 2, TOK, FF // 2), bf16),
            V((2, D, TOK), bf16),
            V((TOK, FF), bf16),
            V((2, TOK, FF // 2), bf16),
            V((2, D, TOK), bf16),
            V((2, 16, RB, 2 * FA), bf16),
            V((2, 16, RB, 2 * FB), bf16),
            V((2, 16, RB, 2 * HL), bf16),
            V((2, 16, RB, HL), bf16),
            V((16, RB, 2 * HL), bf16),
            V((16, RB, HL), bf16),
            V((2, 16, RB, HW), bf16),
            V((16, RB, HW), bf16),
            V((C, LEN), bf16),
            V((4, C, TOK), bf16),
            V((TOK, D), bf16),
            V((D, TOK), bf16),
            V((3 * C, LEN), bf16),
            V((3, C, LEN), bf16),
            V((2, C // 2, LEN), bf16),
            V((2, 2, C // 2, LEN), bf16),
            V((2, 4, RB, 2 * FA), bf16),
            V((2, 2, 4, RB, 2 * FA), bf16),
            V((2, 4, RB, 2 * FA), bf16),
            V((2, 3, RB, 2 * FA), bf16),
            V((2, RB, 2 * FA), bf16),
            V((2, 3, RB, FA // 2), bf16),
            V((2, 2, 8, RB, FB // 2), bf16),
            V((2, 2, 2, 8, RB, FB // 2), bf16),
            V((2, 16, RB, FB // 2), bf16),
            V((2, 3, 4, RB, FB // 2), bf16),
            V((2, 4, RB, FB // 2), bf16),
            V((2, 3, RB, FB // 2), bf16),
            V((3, 4, RB, 2 * HL), bf16),
            V((3, 4, RB, HL), bf16),
            V((4, RB, 2 * HL), bf16),
            V((4, RB, HL), bf16),
            V((3, RB, 2 * HL), bf16),
            V((3, RB, HL), bf16),
            V((3, 4, RB, HW), bf16),
            V((4, RB, HW), bf16),
            V((3, RB, HW), bf16),
            V((2, RB, HW), bf16),
            V((4, RB, C), bf16),
            V((3, RB, C), bf16),
            V((2, 2, RB, FA // 2), f32),
            V((2, 2, RB, FB // 2), f32),
            V((2, RB, HW), f32),
            V((8, TOK), f32),
            V((D, 128), f32),
            V((16, D), f32),
            V((16, D), f32),
            V((10, 8, D), f32),
            V((2, RB, D), bf16),
            V((3, RB, C), bf16),
            V((8, 1, C), f32),
            V((6, 128), f32),
            pltpu.SemaphoreType.DMA((18,)),
            pltpu.SemaphoreType.DMA((N_SEM,)),
            pltpu.SemaphoreType.DMA((N_SEM,)),
        ],
        compiler_params=pltpu.CompilerParams(
            collective_id=0, has_side_effects=True, vmem_limit_bytes=62 * 2**20
        ),
    )(
        inputs, teacher, lengths, query_weight, key_weight, value_weight, output_weight.T,
        up_weight, down_weight, *vectors,
    )
    vector = sds((1, C), f32)
    weight = sds((RB, C), f32)
    wide = sds((RB, D), f32)
    done = pl.pallas_call(
        finish,
        name="finish",
        out_shape=(
            sds((C, LEN), bf16), sds((1,), f32), sds((C, LEN), f32),
            weight, vector, weight, weight, vector, weight,
            vector, vector, vector, wide, sds((6, 128), f32), wide, vector, vector, vector,
        ),
        in_specs=[vm] * 7,
        out_specs=(vm, pl.BlockSpec(memory_space=pltpu.SMEM)) + (vm,) * 16,
    )(*got)
    shapes = [
        (C, LEN), (), (C, LEN), (RB, C), (C,), (RB, C), (RB, C), (C,), (RB, C), (C,), (C,), (C,),
        (RB, D), (D,), (RB, D), (C,), (C,), (C,),
    ]
    done = [o.reshape(shape) for o, shape in zip(done, shapes)]
    done[8] = done[8].T
    return tuple(done)


def solution(mesh):
    split = Mesh(
        mesh.devices.reshape(mesh.shape["dp"], 4, 4, mesh.shape["col"]), AXES
    )
    tokens = P("col", DP_ROW)
    weight = P(ROW, "col")
    vector = P("col")
    return jax.shard_map(
        local_step,
        mesh=split,
        in_specs=(
            tokens, tokens, P(DP_ROW), weight, vector, weight, weight, vector,
            P("col", ROW), vector, vector, vector, weight, vector, weight,
            vector, vector, vector,
        ),
        out_specs=(
            tokens, P(), tokens, weight, vector, weight, weight, vector,
            P("col", ROW), vector, vector, vector, weight, vector, weight,
            vector, vector, vector,
        ),
        check_vma=False,
    )
```

```python
import jax
import jax.numpy as jnp
from jax import lax
from jax.experimental import pallas as pl
from jax.experimental.pallas import tpu as pltpu
from jax.sharding import Mesh
from jax.sharding import PartitionSpec as P

D = 768
FF = 3072
LEN = 1024
HD = 64
HEADS = 3
C = 192
TOK = 256
RB = 48
SLOTS = 32768
EPS = 1e-12
MASK = -1e30
ROOT_HALF = 0.7071067811865476
INV_ROOT_TAU = 0.3989422804014327
AXES = ("dp", "row_0", "row_1", "col")
ROW = ("row_0", "row_1")
DP_ROW = ("dp", "row_0", "row_1")
N_SEM = 90
HL = 128
QC = 96
FA = 512
FB = 256
WT = 512
QH = 288
HW = 384
f32 = jnp.float32
bf16 = jnp.bfloat16


def mm(a, b):
    return lax.dot_general(a, b, (((1,), (0,)), ((), ())), preferred_element_type=f32)


def mt(a, b):
    return lax.dot_general(a, b, (((1,), (1,)), ((), ())), preferred_element_type=f32)


def transposed(a):
    return jnp.transpose(a, (1, 0))


class Sent:
    def __init__(self, copy):
        self.copy, self.open_send, self.open_recv = copy, True, True

    def wait_send(self):
        if self.open_send:
            self.copy.wait_send()
        self.open_send = False

    def wait_recv(self):
        if self.open_recv:
            self.copy.wait_recv()
        self.open_recv = False

    def wait(self):
        self.wait_send()
        self.wait_recv()


class Batch(Sent):
    def __init__(self, ssem, rsem, whole):
        self.ssem, self.rsem, self.whole, self.dev = ssem, rsem, whole, None
        super().__init__(None)

    def copy_of(self, src, dst):
        return pltpu.make_async_remote_copy(
            src_ref=src,
            dst_ref=dst,
            send_sem=self.ssem,
            recv_sem=self.rsem,
            device_id=self.dev,
            device_id_type=pl.DeviceIdType.MESH,
        )

    def send(self, src, dst, dev):
        self.dev = dev
        self.copy_of(src, dst).start()

    def wait_send(self):
        if self.open_send:
            self.copy = self.copy_of(self.whole, self.whole)
        super().wait_send()

    def wait_recv(self):
        if self.open_recv:
            self.copy = self.copy_of(self.whole, self.whole)
        super().wait_recv()


class Links:
    def __init__(self, ssem, rsem):
        self.ssem, self.rsem, self.n, self.all = ssem, rsem, 0, []

    def send(self, src, dst, dev):
        copy = pltpu.make_async_remote_copy(
            src_ref=src,
            dst_ref=dst,
            send_sem=self.ssem.at[self.n],
            recv_sem=self.rsem.at[self.n],
            device_id=dev,
            device_id_type=pl.DeviceIdType.MESH,
        )
        copy.start()
        self.n += 1
        self.all.append(Sent(copy))
        return self.all[-1]

    def batch(self, whole):
        self.all.append(Batch(self.ssem.at[self.n], self.rsem.at[self.n], whole))
        self.n += 1
        return self.all[-1]


class RingGather:
    def __init__(self, links, ref, whole, plus, minus, plus_parts, minus_parts):
        self.ref, self.plus, self.minus = ref, plus, minus
        self.plus_parts, self.minus_parts = plus_parts, minus_parts
        half = len(plus_parts)
        self.left_on, self.left_end = links.batch(whole(half)), links.batch(whole(half))
        self.right_on, self.right_end = links.batch(whole(half)), links.batch(whole(half))
        self.far = links.batch(whole(2 * half))

    def send_plus(self, part):
        own = self.ref("me", part)
        batch = self.left_on if part in self.plus_parts else self.left_end
        batch.send(own, own, self.plus)

    def send_minus(self, part):
        own = self.ref("me", part)
        batch = self.right_on if part in self.minus_parts else self.right_end
        batch.send(own, own, self.minus)

    def send(self, part):
        self.send_plus(part)
        self.send_minus(part)

    def first(self):
        for part in self.plus_parts:
            self.send_plus(part)
        for part in self.minus_parts:
            self.send_minus(part)

    def rest(self):
        for part in self.minus_parts:
            self.send_plus(part)
        for part in self.plus_parts:
            self.send_minus(part)

    def forward(self):
        self.left_on.wait_recv()
        for part in self.plus_parts:
            ref = self.ref("left", part)
            self.far.send(ref, ref, self.plus)
        self.right_on.wait_recv()
        for part in self.minus_parts:
            ref = self.ref("right", part)
            self.far.send(ref, ref, self.minus)

    def wait(self, at):
        batches = {
            "left": (self.left_on, self.left_end),
            "right": (self.right_on, self.right_end),
            "far": (self.far,),
        }
        for batch in batches[at]:
            batch.wait_recv()


class DirectGather:
    def __init__(self, links, ref, whole, devs):
        self.ref, self.devs, self.batch = ref, devs, links.batch(whole(12))

    def send(self, part):
        own = self.ref("me", part)
        for dev in self.devs:
            self.batch.send(own, own, dev)


class DirectSum:
    def __init__(self, links, own, recv, devs):
        self.own, self.recv, self.devs, self.batch = own, recv, devs, links.batch(recv)

    def start(self):
        for i, at in enumerate(("right", "left", "far")):
            for p in range(4):
                self.batch.send(self.own(at, p), self.recv.at[i, p], self.devs[i])

    def total(self, p):
        self.batch.wait_recv()
        total = self.own("me", p)[...].astype(f32)
        for i in range(3):
            total = total + self.recv[i, p].astype(f32)
        return total


class RingSum:
    def __init__(self, links, own, mid, recv, plus, minus, parts):
        self.own, self.mid, self.recv, self.plus, self.minus = own, mid, recv, plus, minus
        half = parts // 2
        self.low, self.high = range(half), range(half, parts)
        self.mid_left = links.batch(mid.at[pl.ds(0, half)])
        self.mid_right = links.batch(mid.at[pl.ds(half, half)])
        self.left, self.right = links.batch(recv.at[0]), links.batch(recv.at[1])

    def first(self):
        for p in self.low:
            self.mid_left.send(self.own("far", p), self.mid.at[p], self.plus)
        for p in self.high:
            self.mid_right.send(self.own("far", p), self.mid.at[p], self.minus)

    def direct_right(self):
        for p in self.high:
            self.left.send(self.own("right", p), self.recv.at[0, p], self.plus)

    def direct_left(self):
        for p in self.low:
            self.right.send(self.own("left", p), self.recv.at[1, p], self.minus)

    def direct(self):
        self.direct_right()
        self.direct_left()

    def middle(self):
        self.mid_left.wait_recv()
        for p in self.low:
            self.mid[p] = self.plus_f32(self.own("right", p)[...], self.mid[p])
            self.left.send(self.mid.at[p], self.recv.at[0, p], self.plus)
        self.mid_right.wait_recv()
        for p in self.high:
            self.mid[p] = self.plus_f32(self.own("left", p)[...], self.mid[p])
            self.right.send(self.mid.at[p], self.recv.at[1, p], self.minus)

    @staticmethod
    def plus_f32(a, b):
        return (a.astype(f32) + b.astype(f32)).astype(bf16)

    def wait(self):
        self.left.wait_recv()
        self.right.wait_recv()

    def total(self, p):
        self.wait()
        total = self.own("me", p)[...].astype(f32)
        return total + self.recv[0, p].astype(f32) + self.recv[1, p].astype(f32)


def layer(
    x_in, t_in, len_in, wq_in, wk_in, wv_in, wo_in, up_in, down_in,
    ob_in, g1_in, b1_in, db_in, g2_in, b2_in, qb_in, vb_in, ub_in,
    out_o, gi_o, dwa_o, dwb_o, dwo_o, dqkv_o, sv_o,
    xf, tf, wa, wb, wq2, wo2, wo4, wqkv, vec, ub, vcol, qkvt, ktm, qaug, vaug, vtm, pst, linv,
    ctxt, ctxa, hid, nrm, sg, bstore, astore, slope, brecv, arecv,
    ga, gb, gqa, gqb, gra, grb, gao, gor, dctx, dct, outt, delta,
    dqkvt, dxp, rxi, rx, im, rm, s1, r2, s2, r3, zi, zr, sb0, br, sb1, rb2,
    rqa, rqb, sqa, sqb, ra2, rb3, ro, so1, ro2, so2, so4, ro3,
    x1, xb1, xq1, stat, gcol, sv, rs0, rsv, wown, wqs, vrow, ubs,
    lsem, ssem, rsem,
):
    d = lax.axis_index("dp")
    y = lax.axis_index("row_0")
    x = lax.axis_index("row_1")
    c = lax.axis_index("col")
    e = 1 - d
    r = 4 * y + x
    a_me = x * e + y * d
    b_me = y * e + x * d

    def around(me):
        return {
            "me": me,
            "left": lax.rem(me + 3, 4),
            "right": lax.rem(me + 1, 4),
            "far": lax.rem(me + 2, 4),
        }

    b_at, c_at = around(b_me), around(c)

    def ridx(a, b):
        return (4 * b + a) * e + (4 * a + b) * d

    def zdev(k):
        return {"col": lax.rem(c + k, 4)}

    def adev(k):
        return {"row_0": lax.rem(y + k * d, 4), "row_1": lax.rem(x + k * e, 4)}

    def bdev(k):
        return {"row_0": lax.rem(y + k * e, 4), "row_1": lax.rem(x + k * d, 4)}

    sib = {"dp": e}
    links = Links(ssem, rsem)

    def wait_all(copies):
        for copy in copies:
            copy.wait_recv()

    def triple(whole, src, dst, dev):
        batch = links.batch(whole)
        for k in (1, 3, 2):
            batch.send(src(k), dst(k), dev(k))
        return batch

    def region(body):
        @pl.when(e + d == 1 + d * e)
        def _():
            body()

    def unrolled(n, body, carry):
        for i in range(n):
            carry = body(i, carry)
        return carry

    def cols(i, width):
        if isinstance(i, int):
            return pl.ds(i * width, width)
        return pl.ds(pl.multiple_of(i * width, 128), width)

    def rows(i, height):
        if isinstance(i, int):
            return pl.ds(i * height, height)
        return pl.ds(pl.multiple_of(i * height, 16), height)

    n_local = [0]

    def local(src, dst):
        copy = pltpu.make_async_copy(src, dst, lsem.at[n_local[0]])
        copy.start()
        n_local[0] += 1
        return copy

    xrows = rows(c, C)
    tcols = cols(c, TOK)
    bar = pltpu.get_barrier_semaphore()
    for k in (1, 2, 3):
        for dev in (zdev(k), adev(k), bdev(k)):
            pl.semaphore_signal(bar, inc=1, device_id=dev, device_id_type=pl.DeviceIdType.MESH)
    pl.semaphore_signal(bar, inc=1, device_id=sib, device_id_type=pl.DeviceIdType.MESH)
    cw = [local(ref, wqs.at[i]) for i, ref in enumerate((wq_in, wk_in, wv_in))]
    cup = local(up_in, wown.at[0])
    cdn = local(down_in, wown.at[1])
    cx = local(x_in, xf.at[xrows])
    ct = local(t_in.at[:, tcols], tf.at[c])
    cwo = local(wo_in, wo4.at[c])
    cv = [
        local(ref, vrow.at[i])
        for i, ref in enumerate((ob_in, g1_in, b1_in, db_in, g2_in, b2_in, qb_in, vb_in))
    ]
    cub = local(ub_in, ubs)
    for copy in cw:
        copy.wait()
    own_qkv = [wqs[i] for i in range(3)]
    own_qkv = jnp.concatenate(
        [w[:, h * HD : (h + 1) * HD] for h in range(HEADS) for w in own_qkv], axis=1
    )
    own_qkv = jnp.where(d == 0, own_qkv[:, 0:QH], own_qkv[:, QH:])
    wq2[d, r] = jnp.concatenate([own_qkv, jnp.zeros((RB, HW - QH), bf16)], axis=1)
    pl.semaphore_wait(bar, 10)

    def along_a(ref, whole):
        return triple(whole, lambda k: ref, lambda k: ref, adev)

    def of_b(ref):
        return lambda at, k: ref(ridx(lax.rem(a_me + 4 - k, 4), b_at[at]))

    def direct_b(ref, whole):
        return DirectGather(links, of_b(ref), whole, (bdev(1), bdev(3), bdev(2)))

    def wq_ref(i):
        return wq2.at[d, i]

    def wo_ref(i):
        return wo2.at[d, i]

    def wa_ref(i):
        return wa.at[d, i]

    def wb_ref(i):
        return wb.at[d, i, :, cols(c, FB)]

    def some(buf):
        return lambda n: buf.at[d, pl.ds(0, n)]

    def some_b(n):
        return wb.at[d, pl.ds(0, n), :, cols(c, FB)]

    class ToSibling:
        def __init__(self, whole):
            self.batch = links.batch(whole)

        def send(self, ref):
            self.batch.send(ref, ref, sib)

        def wait(self):
            self.batch.wait_recv()

    wq_a = along_a(wq_ref(r), some(wq2)(3))
    wq_b = direct_b(wq_ref, some(wq2))
    wq_b.send(0)
    cup.wait()
    cdn.wait()
    wz = triple(
        wa.at[d, 0, :, pl.ds(0, 3 * FA)],
        lambda k: wown.at[d, :, pl.ds(0, FA)],
        lambda k: wa.at[d, r, :, cols(c, FA)],
        zdev,
    )
    cx.wait()
    x_z = RingGather(
        links,
        lambda at, half: xf.at[rows(2 * c_at[at] + half, C // 2)],
        lambda n: xf.at[pl.ds(0, n * C // 2)],
        zdev(1), zdev(3), (0,), (1,),
    )
    x_z.first()
    cwo.wait()
    for i, copy in enumerate(cv):
        copy.wait()
        vec[c, i : i + 1, :] = vrow[i]
    cub.wait()
    ub[c, 0:1, :] = jnp.concatenate([ubs[i : i + 1] for i in range(6)], axis=1)
    oz = triple(wo4.at[pl.ds(0, 3)], lambda k: wo4.at[c], lambda k: wo4.at[c], zdev)
    wa[d, r, :, cols(c, FA)] = wown[d, :, 0:FA]
    wb[d, r, :, cols(c, FB)] = wown[d, :, FA:]
    wb_a = along_a(wb_ref(r), some_b(3))
    wb_b = direct_b(wb_ref, some_b)
    wb_b.send(0)

    wq_a.wait_recv()
    for k in (1, 3, 2):
        wq_b.send(k)
    wq_s = ToSibling(wq2.at[d])
    for j in range(4):
        wq_s.send(wq_ref(ridx(j, b_me)))
    wb_a.wait_recv()
    for k in (1, 3, 2):
        wb_b.send(k)
    x_z.rest()
    wz.wait_recv()
    wa_a = [links.batch(wa_ref(0)) for _ in range(3)]
    for i, k in enumerate((1, 3, 2)):
        wa_a[i].send(wa_ref(r), wa_ref(r), adev(k))
    wa_b = RingGather(links, of_b(wa_ref), some(wa), bdev(1), bdev(3), (0, 2), (1, 3))
    wa_b.send(0)
    oz.wait_recv()
    own_wo = jnp.concatenate([wo4[j] for j in range(4)], axis=1)
    wo2[d, r] = jnp.where(d == 0, own_wo[:, 0:HW], own_wo[:, HW:])
    wo_a = along_a(wo_ref(r), some(wo2)(3))
    wo_b = direct_b(wo_ref, some(wo2))
    wo_b.send(0)
    wq_b.batch.wait_recv()
    for at in ("left", "right", "far"):
        for k in range(4):
            wq_s.send(wq_b.ref(at, k))
    x_z.forward()
    wo_s = ToSibling(wo2.at[d])
    wo_s.send(wo_ref(r))
    wa_s = ToSibling(wa.at[d])
    wa_s.send(wa_ref(r))
    for i, k in enumerate((1, 3, 2)):
        wa_a[i].wait_recv()
        wa_b.send(k)
        wa_s.send(wa_b.ref("me", k))
    wo_a.wait_recv()
    for k in (1, 3, 2):
        wo_b.send(k)
        wo_s.send(wo_b.ref("me", k))
    vown = transposed(vec[c])
    length = len_in[0]

    for at in ("left", "right", "far"):
        x_z.wait(at)
    wb_b.batch.wait_recv()

    def wb_z(at, half):
        return wb.at[d, pl.ds(half * 8, 8), :, cols(c_at[at], FB)]

    def some_z(n):
        return wb.at[d, pl.ds(0, 8), :, pl.ds(0, n * FB)]

    wb_zg = RingGather(links, wb_z, some_z, zdev(1), zdev(3), (0,), (1,))
    vz = triple(
        vec.at[pl.ds(0, 3), 0:8], lambda k: vec.at[c, 0:8], lambda k: vec.at[c, 0:8], zdev
    )
    uz = triple(
        ub.at[pl.ds(0, 3), 0:1], lambda k: ub.at[c, 0:1], lambda k: ub.at[c, 0:1], zdev
    )
    wb_zg.first()
    wb_s = ToSibling(wb.at[d])
    wb_s.send(wb.at[d, :, :, cols(c, FB)])
    wq_s.wait()
    q_bias = vown[:, 6:7]
    v_bias = vown[:, 7:8]
    lane_iota = lax.broadcasted_iota(jnp.int32, (1, TOK), 1)
    first_row = lax.broadcasted_iota(jnp.int32, (HD, TOK), 0) == 0

    def qkv_chunk(i, carry):
        at = cols(i, TOK)
        tok = xf[:, at]
        qkv = mm(dxp[:, :, 0:D].reshape(3 * C, D), tok)
        bias = jnp.where(lane_iota + i * TOK < length, 0.0, MASK)
        bias = jnp.where(first_row, jnp.broadcast_to(bias, (HD, TOK)), 0.0).astype(bf16)
        ones = jnp.where(first_row, 1.0, 0.0).astype(bf16)
        for h in range(HEADS):
            hs = slice(h * HD, (h + 1) * HD)
            of = h * C
            q = (qkv[of : of + HD] + q_bias[hs]).astype(bf16)
            q = (q.astype(f32) * (HD**-0.5)).astype(bf16)
            k = qkv[of + HD : of + 2 * HD].astype(bf16)
            v = (qkv[of + 2 * HD : of + 3 * HD] + v_bias[hs]).astype(bf16)
            qkvt[h * HD : (h + 1) * HD, at] = q
            qkvt[C + h * HD : C + (h + 1) * HD, at] = k
            qaug[h, 0:HD, at] = q
            qaug[h, HD : 2 * HD, at] = ones
            vaug[h, 0:HD, at] = v
            vaug[h, HD : HD + 16, at] = ones[0:16]
            ktm[h, at, :] = transposed(jnp.concatenate([k, bias], axis=0))
            vtm[h, at, :] = transposed(jnp.concatenate([v, ones], axis=0))
        return carry

    w_low = transposed(wq2[0].reshape(D, HW))[0:QH]
    w_high = transposed(wq2[1].reshape(D, HW))[0:QH]
    dxp[0, :, 0:D] = w_low[0:C]
    dxp[1, 0 : QH - C, 0:D] = w_low[C:]
    dxp[1, QH - C :, 0:D] = w_high[0 : QH - C]
    dxp[2, :, 0:D] = w_high[QH - C :]
    unrolled(4, qkv_chunk, 0)

    wb_zg.rest()

    def fwd_head(h):
        score = mm(ktm[h], qaug[h, :, 0:WT])
        for n in range(LEN // WT):
            at = cols(n, WT)
            later = mm(ktm[h], qaug[h, :, cols(n + 1, WT)]) if (n + 1) * WT < LEN else None
            top = jnp.max(score, axis=0, keepdims=True)
            probs = jnp.exp(score - top).astype(bf16)
            pst[h, :, at] = probs
            both = mm(vaug[h], probs)
            inv = 1.0 / both[HD : HD + 1]
            linv[h, 0:1, at] = inv
            ctxt[h * HD : (h + 1) * HD, at] = (both[0:HD] * inv).astype(bf16)
            score = later

    cc = links.batch(ctxa.at[pl.ds(0, 3)])

    def context_out(h):
        hrow = pl.ds(h * HD, HD)
        ctxa[c, hrow] = ctxt[hrow, tcols]
        for k in (1, 3, 2):
            there = cols(lax.rem(c + k, 4), TOK)
            cc.send(ctxt.at[hrow, there], ctxa.at[c, hrow], zdev(k))

    def pass_on(ring, sent, at):
        ring.wait(at)
        for k in range(4):
            sent.send(ring.ref(at, k))

    fwd_head(0)
    context_out(0)
    wa_b.forward()
    pass_on(wa_b, wa_s, "left")
    pass_on(wa_b, wa_s, "right")
    fwd_head(1)
    context_out(1)
    wo_b.batch.wait_recv()
    for at in ("left", "right", "far"):
        for k in range(4):
            wo_s.send(wo_b.ref(at, k))
    wait_all((vz, uz))
    for i in range(4):
        vcol[i * C : (i + 1) * C, 0:16] = transposed(vec[i])
    fwd_head(2)
    context_out(2)
    wb_zg.forward()
    pass_on(wa_b, wa_s, "far")
    for i in range(2):
        wqkv[:, i * QH : (i + 1) * QH] = wq2[i].reshape(D, HW)[:, 0:QH]
    wo_s.wait()
    cc.wait_recv()
    ct.wait()
    tt = triple(
        tf.at[pl.ds(0, 3)],
        lambda k: t_in.at[:, cols(lax.rem(c + k, 4), TOK)],
        lambda k: tf.at[c],
        zdev,
    )

    def norm_stats(ref):
        v = ref[...]
        mean = jnp.sum(v, axis=0, keepdims=True) * (1.0 / D)
        square = jnp.sum(v * v, axis=0, keepdims=True) * (1.0 / D)
        return mean, lax.rsqrt(square - mean * mean + EPS)


    @region
    def _():
        acc = xf[:, tcols].astype(f32) + vcol[:, 0:1]
        for j in range(2):
            w = wo2[j].reshape(D, HW)
            acc = acc + mm(w, ctxa[2 * j : 2 * j + 2].reshape(HW, TOK))
        hid[...] = acc
        mean1, inv1 = norm_stats(hid)
        stat[0:1] = inv1

        def norm1(i, carry):
            row = rows(i, C)
            n = (hid[row] - mean1) * inv1
            nrm[row] = n
            h = n * vcol[row, 1:2] + vcol[row, 2:3]
            hid[row] = h + vcol[row, 3:4]
            astore[0, row] = h.astype(bf16)
            return carry

        unrolled(4, norm1, 0)
        outt[...] = transposed(astore[0])

    for at in ("left", "right"):
        wb_zg.wait(at)
        wb_s.send(wb.at[d, :, :, cols(c_at[at], FB)])

    wa_s.wait()

    def w_chunk(ref, i):
        return ref[:, :, cols(i, FA)].reshape(D, FA)

    def halves(chunk):
        if chunk < 4:
            return [(half, chunk * FA // 2, FA // 2) for half in range(2)]
        pairs = [(half, j) for j in (2 * chunk - 8, 2 * chunk - 7) for half in range(2)]
        return [(half, 2 * FA + j * FB // 2, FB // 2) for half, j in pairs]

    def store_halves(w, chunk, v):
        at = 0
        for half, to, width in halves(chunk):
            bstore[w, half, :, to : to + width] = v[:, at : at + width]
            at += width

    def load_halves(w, chunk):
        return jnp.concatenate(
            [bstore[w, half, :, to : to + width] for half, to, width in halves(chunk)], axis=1
        )

    def up_of(ref, bias, first):
        def up_chunk(i, carry):
            at = cols(first + i, FA)
            pre = mm(outt[...], w_chunk(ref, i)) + bias(i)
            half = 0.5 * (1.0 + lax.erf(pre * ROOT_HALF))
            store_halves(1, first + i, (pre * half).astype(bf16))
            slope[:, at] = (half + pre * jnp.exp(-0.5 * pre * pre) * INV_ROOT_TAU).astype(bf16)
            return carry

        return up_chunk

    def bias_a(i):
        return ub[i, 0:1, 0:FA]

    def bias_b(i):
        return jnp.concatenate([ub[2 * i, 0:1, FA:], ub[2 * i + 1, 0:1, FA:]], axis=1)

    region(lambda: unrolled(4, up_of(wa.at[0], bias_a, 0), 0))

    def down_of(ref, first):
        def down_chunk(i, carry):
            hid[...] = hid[...] + mt(w_chunk(ref, i), load_halves(1, first + i))
            return carry

        return down_chunk

    region(lambda: unrolled(4, down_of(wa.at[1], 0), 0))
    wb_zg.wait("far")
    wb_s.send(wb.at[d, :, :, cols(c_at["far"], FB)])
    wb_s.wait()

    @region
    def _():
        unrolled(2, up_of(wb.at[0], bias_b, 4), 0)
        unrolled(2, down_of(wb.at[1], 4), 0)

    ex_down = [links.send(bstore.at[1, e], brecv.at[1], sib)]

    tt.wait_recv()
    valid = lane_iota + c * TOK < length

    zero = jnp.zeros((1, TOK), f32)

    @region
    def _():
        mean2, inv2 = norm_stats(hid)
        gcol[...] = jnp.zeros(gcol.shape, f32)
        sv[...] = jnp.zeros(sv.shape, f32)

        def norm2(i, carry):
            total, crossed, loss = carry
            row = rows(i, C)
            n = (hid[row] - mean2) * inv2
            hid[row] = n
            final = n * vcol[row, 4:5] + vcol[row, 5:6]
            delta[row] = final.astype(bf16)
            g = jnp.where(valid, final - tf[i].astype(f32), 0.0)
            gcol[row, 4:5] = jnp.sum(g * n, axis=1, keepdims=True)
            gcol[row, 5:6] = jnp.sum(g, axis=1, keepdims=True)
            s = g * vcol[row, 4:5]
            sg[row] = s
            return (
                total + jnp.sum(s, axis=0, keepdims=True),
                crossed + jnp.sum(s * n, axis=0, keepdims=True),
                loss + jnp.sum(g * g, axis=0, keepdims=True),
            )

        total2, crossed2, loss_row = unrolled(4, norm2, (zero, zero, zero))
        for i, row in enumerate((inv2, total2, crossed2, loss_row)):
            stat[1 + i : 2 + i] = row

    out_o_own = local(delta.at[xrows], out_o.at[:, tcols])
    fo = triple(
        delta.at[pl.ds(0, 3 * C)],
        lambda k: delta.at[rows(lax.rem(c + k, 4), C)],
        lambda k: out_o.at[:, tcols],
        zdev,
    )

    def norm2_back(i, carry):
        row = rows(i, C)
        s = stat[1:2] * (sg[row] - stat[2:3] * (1.0 / D) - hid[row] * (stat[3:4] * (1.0 / D)))
        sg[row] = s
        low = s.astype(bf16)
        astore[1, row] = low
        gcol[row, 3:4] = jnp.sum(low.astype(f32), axis=1, keepdims=True)
        return carry

    @region
    def _():
        unrolled(4, norm2_back, 0)
        outt[...] = transposed(astore[1])


    ex_down.append(links.send(astore.at[1], arecv.at[1], sib))

    def act_of(ref, first):
        def act_chunk(i, carry):
            at = cols(first + i, FA)
            g = mm(outt[...], w_chunk(ref, i)) * slope[:, at].astype(f32)
            low = g.astype(bf16)
            store_halves(0, first + i, low)
            total = jnp.sum(low.astype(f32), axis=0, keepdims=True)
            sv[8 + first + i : 9 + first + i, 0:FA] = total
            return carry

        return act_chunk

    @region
    def _():
        unrolled(2, act_of(wb.at[1], 4), 0)
        unrolled(4, act_of(wa.at[1], 0), 0)

    ex_up = [
        links.send(astore.at[0], arecv.at[0], sib),
        links.send(bstore.at[0, e], brecv.at[0], sib),
    ]

    def back_of(ref, first):
        def back_chunk(i, carry):
            sg[...] = sg[...] + mt(w_chunk(ref, i), load_halves(0, first + i))
            return carry

        return back_chunk

    def sum_b(own, mid, recv):
        return RingSum(
            links, lambda at, j: own(ridx(j, b_at[at])), mid, recv, bdev(1), bdev(3), 4
        )

    def direct_sum(own, recv):
        return DirectSum(
            links, lambda at, j: own(ridx(j, b_at[at])), recv, (bdev(1), bdev(3), bdev(2))
        )

    def end_b(ring, summed, peer_recv):
        for j in range(4):
            summed[j] = ring.total(j).astype(bf16)
        return triple(
            peer_recv,
            lambda k: summed.at[lax.rem(a_me + k, 4)],
            lambda k: peer_recv.at[k - 1],
            adev,
        )

    def end_a(sends, summed, recv):
        sends.wait_recv()
        total = summed[a_me].astype(f32)
        for k in range(3):
            total = total + recv[k].astype(f32)
        return total

    def add_sibling(ref, other):
        def add(i, carry):
            ref[d, i] = (ref[d, i].astype(f32) + other[i].astype(f32)).astype(bf16)
            return carry

        unrolled(16, add, 0)

    def weight_grad(w):
        @region
        def _():
            for at, ref in ((0, ga), (2 * FA, gb)):
                for lo in range(0, ref.shape[3], FA):
                    cut = pl.ds(at + lo, FA)
                    g = mm(astore[w], bstore[w, d, :, cut]) + mm(arecv[w], brecv[w, :, cut])
                    ref[w, :, :, lo : lo + FA] = g.astype(bf16).reshape(16, RB, FA)

        def z_own(at, half):
            return gb.at[w, pl.ds(half * 8, 8), :, cols(c_at[at], FB // 2)]

        a_ring = sum_b(lambda i: ga.at[w, i], im.at[w], rm.at[w])
        b_ring = RingSum(links, z_own, zi.at[w], zr.at[w], zdev(1), zdev(3), 2)
        a_ring.first()
        b_ring.first()
        return a_ring, b_ring

    region(lambda: unrolled(2, back_of(wb.at[0], 4), 0))
    wait_all(ex_down)
    wd_a, wd_b = weight_grad(1)
    region(lambda: unrolled(4, back_of(wa.at[0], 0), 0))

    def hidden_back(i, carry):
        total, crossed = carry
        row = rows(i, C)
        g = sg[row]
        n = nrm[row]
        gcol[row, 1:2] = jnp.sum(g * n, axis=1, keepdims=True)
        gcol[row, 2:3] = jnp.sum(g, axis=1, keepdims=True)
        s = g * vcol[row, 1:2]
        sg[row] = s
        return (
            total + jnp.sum(s, axis=0, keepdims=True),
            crossed + jnp.sum(s * n, axis=0, keepdims=True),
        )


    fo.wait_send()
    out_o_own.wait()
    wd_a.direct()

    @region
    def _():
        total1, crossed1 = unrolled(4, hidden_back, (zero, zero))

        def norm1_back(i, carry):
            row = rows(i, C)
            s = stat[0:1] * (sg[row] - total1 * (1.0 / D) - nrm[row] * (crossed1 * (1.0 / D)))
            sg[row] = s
            low = s.astype(bf16)
            delta[row] = low
            gcol[row, 0:1] = jnp.sum(low.astype(f32), axis=1, keepdims=True)
            return carry

        unrolled(4, norm1_back, 0)
        outt[...] = transposed(delta[...])
        for i in range(2):
            part = transposed(mm(outt[...], wo2[i].reshape(D, HW)).astype(bf16))
            dct[2 * i : 2 * i + 2] = part.reshape(2, C, TOK)
        dctx[:, tcols] = dct[c]


    dc = []
    for h in range(HEADS):
        hrow = pl.ds(h * HD, HD)
        dc.append(
            triple(
                dct.at[0],
                lambda k: dct.at[lax.rem(c + k, 4), hrow],
                lambda k: dctx.at[hrow, tcols],
                zdev,
            )
        )

    sv[0:8] = transposed(gcol[...])[0:8]
    sv[6:7] = jnp.broadcast_to(jnp.sum(stat[4:5], axis=1, keepdims=True), (1, D))
    sv[7:8] = jnp.broadcast_to(length.astype(f32), (1, D))
    v_sent = [links.send(sv, rs0, sib)]
    v_from = [(0, 0)]
    half8 = pl.ds(pl.multiple_of(8 * d, 8), 8)
    other8 = pl.ds(pl.multiple_of(8 * e, 8), 8)

    def sv_add():
        v_sent.pop().wait()
        lo, n = v_from[-1]
        if n == 0:
            sv[...] = sv[...] + rs0[...]
        else:
            total = sv[half8]
            for i in range(n):
                total = total + rsv[lo + i]
            sv[half8] = total

    def sv_send(dev):
        lo = sum(v_from[-1])
        v_from.append((lo, 3))
        v_sent.append(
            triple(
                rsv.at[pl.ds(lo, 3)],
                lambda k: sv.at[half8],
                lambda k: rsv.at[lo + k - 1],
                dev,
            )
        )

    wait_all(ex_up)
    wd_b.direct()
    wu_a, wu_b = weight_grad(0)
    sv_add()
    sv_send(bdev)

    @region
    def _():
        g = mt(delta[...], ctxa[...].reshape(D, TOK)).astype(bf16)
        for i in range(2):
            gao[i] = g[:, i * HW : (i + 1) * HW].reshape(16, RB, HW)

    go_x = links.send(gao.at[e], gor, sib)
    wd_a.middle()
    wd_b.middle()

    def bwd_head(h, meanwhile=None):
        hrow = pl.ds(h * HD, HD)
        krow = pl.ds(C + h * HD, HD)
        of = h * C

        dk = dv = jnp.zeros((HD, LEN), f32)
        for n in range(LEN // WT):
            at = cols(n, WT)
            inv = linv[h, 0:1, at]
            dc = dctx[hrow, at].astype(f32)
            inner = jnp.sum(dc * ctxt[hrow, at].astype(f32), axis=0, keepdims=True) * inv
            dcs = (dc * inv).astype(bf16)
            probs = pst[h, :, at]
            dv = dv + mt(dcs, probs)
            dp = mm(vtm[h, :, 0:HD], dcs) - inner
            ds = (probs.astype(f32) * dp).astype(bf16)
            dk = dk + mt(qkvt[hrow, at], ds)
            dqkvt[of : of + HD, at] = (mm(qkvt[krow, :], ds) * (HD**-0.5)).astype(bf16)
            if n == 0 and meanwhile is not None:
                meanwhile()
        dqkvt[of + HD : of + 2 * HD] = dk.astype(bf16)
        dqkvt[of + 2 * HD : of + 3 * HD] = dv.astype(bf16)

    spare = HL - QC
    row_iota = lax.broadcasted_iota(jnp.int32, (RB, spare), 0)

    def qkv_grad(h, ref, at):
        of = dqkvt[h * C : (h + 1) * C]
        g = mt(xf[...], of).astype(bf16)
        sums = mt(jnp.ones((8, LEN), bf16), of)[0:1]
        for half in range(2):
            lo = half * QC
            part_rows = jnp.zeros((RB, spare), f32)
            for j in range(3):
                part = sums[:, lo + j * spare : lo + (j + 1) * spare]
                part_rows = jnp.where(row_iota == j, jnp.broadcast_to(part, (RB, spare)), part_rows)
            ref[half, :, :, at : at + QC] = g[:, lo : lo + QC].reshape(16, RB, QC)
            ref[half, :, :, at + QC : at + HL] = jnp.broadcast_to(
                part_rows.astype(bf16)[None], (16, RB, spare)
            )

    dc[0].wait_recv()
    bwd_head(0)
    wu_a.direct()
    wu_b.direct()
    go_x.wait_recv()
    add_sibling(gao, gor)
    o_sum = direct_sum(lambda i: gao.at[d, i], ro)
    o_sum.start()
    dc[1].wait_recv()
    bwd_head(1, lambda: qkv_grad(0, gqa, 0))
    wd_sends = end_b(wd_a, s1.at[1], r2.at[1])
    def total_z(w, ring):
        for half in range(2):
            sb0[w, half * 8 : half * 8 + 8] = ring.total(half).astype(bf16)
        ring_b = direct_sum(lambda i: sb0.at[w, i], br.at[w])
        ring_b.start()
        return ring_b

    wu_a.middle()
    wu_b.middle()


    sv_add()
    sv_send(adev)
    dc[2].wait_recv()
    bwd_head(2, lambda: qkv_grad(1, gqa, HL))

    def dx_part(i, slot=None):
        @region
        def _():
            row = rows(i, C)
            gi_o[...] = mm(wqkv[row], dqkvt[...])
            gi_o[:, tcols] = gi_o[:, tcols] + sg[row]
            if slot is not None:
                dxp[slot] = gi_o[...].astype(bf16)

    SLOT = {"far": 0, "right": 1, "left": 2}

    def dx_own(at, half):
        return dxp.at[SLOT[at], pl.ds(half * (C // 2), C // 2)]

    dx_sum = RingSum(links, dx_own, rxi, rx, zdev(1), zdev(3), 2)
    dx_part(c_at["far"], 0)
    dx_sum.first()
    bd_sum = total_z(1, wd_b)
    xa = links.send(gqa.at[e], gra, sib)
    region(lambda: qkv_grad(2, gqb, 0))
    xb = links.send(gqb.at[e], grb, sib)

    dx_part(c_at["right"], 1)
    dx_sum.direct_right()
    dx_part(c_at["left"], 2)
    dx_sum.direct_left()
    xa.wait_recv()
    add_sibling(gqa, gra)
    qa_sum = direct_sum(lambda i: gqa.at[d, i], rqa)
    qa_sum.start()
    xb.wait_recv()
    add_sibling(gqb, grb)
    qb_sum = direct_sum(lambda i: gqb.at[d, i], rqb)
    qb_sum.start()
    dx_part(c)
    o_sends = end_b(o_sum, so1, ro2)

    def along_z(w, sends):
        s2[w] = end_a(sends, s1.at[w], r2.at[w]).astype(bf16)
        return triple(
            r3.at[w],
            lambda k: s2.at[w, :, cols(lax.rem(c + k, 4), FA // 2)],
            lambda k: r3.at[w, k - 1],
            zdev,
        )

    w3 = {1: along_z(1, wd_sends)}
    wu_sends = end_b(wu_a, s1.at[0], r2.at[0])
    dx_sum.middle()
    bu_sum = total_z(0, wu_b)
    sv_add()
    sv_send(zdev)
    qa_sends = end_b(qa_sum, sqa, ra2)
    w3[0] = along_z(0, wu_sends)
    qb_sends = end_b(qb_sum, sqb, rb3)
    bd_sends = end_b(bd_sum, sb1.at[1], rb2.at[1])
    so2[0] = end_a(o_sends, so1, ro2).astype(bf16)
    o_x = links.send(so2.at[0], so2.at[1], sib)
    bu_sends = end_b(bu_sum, sb1.at[0], rb2.at[0])
    o_x.wait_recv()
    mine, other = so2[0], so2[1]
    low, high = jnp.where(d == 0, mine, other), jnp.where(d == 0, other, mine)
    so4[0], so4[1] = low[:, 0:C], low[:, C:]
    so4[2], so4[3] = high[:, 0:C], high[:, C:]
    o3 = triple(
        ro3, lambda k: so4.at[lax.rem(c + k, 4)], lambda k: ro3.at[k - 1], zdev
    )
    xq1[0, :, 0 : 2 * HL] = end_a(qa_sends, sqa, ra2)
    xq1[0, :, 2 * HL :] = end_a(qb_sends, sqb, rb3)
    q3 = links.send(xq1.at[0], xq1.at[1], sib)
    wait_all((w3[1], w3[0]))
    sv_add()
    v_other = links.send(sv.at[half8], rsv.at[9], sib)
    x1[0] = s2[:, :, cols(c, FA // 2)].astype(f32)
    for w in range(2):
        for k in range(3):
            x1[0, w] = x1[0, w] + r3[w, k].astype(f32)
    w4 = links.send(x1.at[0], x1.at[1], sib)
    xb1[0, 1] = end_a(bd_sends, sb1.at[1], rb2.at[1])
    xb1[0, 0] = end_a(bu_sends, sb1.at[0], rb2.at[0])
    wb4 = links.send(xb1.at[0], xb1.at[1], sib)
    o3.wait_recv()
    ototal = so4[c].astype(f32)
    for k in range(3):
        ototal = ototal + ro3[k].astype(f32)
    dwo_o[...] = ototal
    sv_o[half8] = sv[half8]
    v_other.wait_recv()
    sv_o[other8] = rsv[9]
    w4.wait_recv()
    dwa_o[d] = x1[0]
    dwa_o[e] = x1[1]
    q3.wait_recv()
    dqkv_o[d] = xq1[0]
    dqkv_o[e] = xq1[1]
    wb4.wait_recv()
    dwb_o[d] = xb1[0]
    dwb_o[e] = xb1[1]
    dx_sum.wait()
    for half in range(2):
        row = pl.ds(half * (C // 2), C // 2)
        gi_o[row] = gi_o[row] + rx[0, half].astype(f32) + rx[1, half].astype(f32)
    for copy in links.all:
        copy.wait()


def finish(
    out_i, gi_i, dwa_i, dwb_i, dwo_i, dqkv_i, sv_i,
    out, loss, gi, gwq, gbq, gwk, gwv, gbv, gwo, gob, gg1, gb1, gup, gub, gdn, gdb, gg2, gb2,
):
    c = lax.axis_index("col")
    out[...] = out_i[...]
    count = sv_i[7:8, 0:1] * 0.25
    factor = SLOTS / count
    loss[0] = jnp.sum(sv_i[6:7, 0:1] / (2.0 * D * count))
    gi[...] = gi_i[...] * factor
    low, high = dqkv_i[0] * factor, dqkv_i[1] * factor
    at = [h * HL for h in range(HEADS)]
    gwq[...] = jnp.concatenate([low[:, i : i + HD] for i in at], axis=1)
    parts = []
    for i in at:
        parts += [low[:, i + HD : i + QC], high[:, i : i + QC - HD]]
    gwk[...] = jnp.concatenate(parts, axis=1)
    gwv[...] = jnp.concatenate([high[:, i + QC - HD : i + QC] for i in at], axis=1)
    gbq[...] = jnp.concatenate([low[j : j + 1, i + QC : i + HL] for i in at for j in (0, 1)], axis=1)
    gbv[...] = jnp.concatenate([high[j : j + 1, i + QC : i + HL] for i in at for j in (1, 2)], axis=1)
    gwo[...] = dwo_i[...] * factor
    for i, ref in enumerate((gup, gdn)):
        for half in range(2):
            ref[:, half * FA // 2 : (half + 1) * FA // 2] = dwa_i[half, i] * factor
            at = FA + half * FB // 2
            ref[:, at : at + FB // 2] = dwb_i[half, i] * factor
    sums = sv_i[...] * factor
    for j in range(4):

        @pl.when(c == j)
        def _(j=j):
            for i in range(4):
                gub[i : i + 1] = sums[8 + j : 9 + j, i * 128 : (i + 1) * 128]
            for i in range(2):
                at = (j % 2) * FB + i * 128
                gub[4 + i : 5 + i] = sums[12 + j // 2 : 13 + j // 2, at : at + 128]
            for i, ref in enumerate((gob, gg1, gb1, gdb, gg2, gb2)):
                ref[...] = sums[i : i + 1, j * C : (j + 1) * C]


def local_step(
    inputs, teacher, lengths, query_weight, query_bias, key_weight, value_weight, value_bias,
    output_weight, output_bias, first_gain, first_shift, up_weight, up_bias, down_weight,
    down_bias, second_gain, second_shift,
):
    anyspec = pl.BlockSpec(memory_space=pl.ANY)
    vm = pl.BlockSpec(memory_space=pltpu.VMEM)
    sds = jax.ShapeDtypeStruct
    V = pltpu.VMEM
    vectors = [
        v.reshape(1, -1)
        for v in (
            output_bias, first_gain, first_shift, down_bias, second_gain, second_shift,
            query_bias, value_bias,
        )
    ]
    vectors.append(up_bias.reshape(6, 128))
    got = pl.pallas_call(
        layer,
        name="layer",
        out_shape=(
            sds((C, LEN), bf16),
            sds((C, LEN), f32),
            sds((2, 2, RB, FA // 2), f32),
            sds((2, 2, RB, FB // 2), f32),
            sds((RB, C), f32),
            sds((2, RB, HW), f32),
            sds((16, D), f32),
        ),
        in_specs=[anyspec, anyspec, pl.BlockSpec(memory_space=pltpu.SMEM)] + [anyspec] * 15,
        out_specs=(anyspec, vm, vm, vm, vm, vm, vm),
        scratch_shapes=[
            V((D, LEN), bf16),
            V((4, C, TOK), bf16),
            V((2, 16, RB, 4 * FA), bf16),
            V((2, 16, RB, 4 * FB), bf16),
            V((2, 16, RB, HW), bf16),
            V((2, 16, RB, HW), bf16),
            V((4, RB, C), bf16),
            V((D, 3 * C), bf16),
            V((4, 16, C), f32),
            V((4, 8, D), f32),
            V((D, 128), f32),
            V((2 * C, LEN), bf16),
            V((HEADS, LEN, 2 * HD), bf16),
            V((HEADS, 2 * HD, LEN), bf16),
            V((HEADS, HD + 16, LEN), bf16),
            V((HEADS, LEN, 2 * HD), bf16),
            V((HEADS, LEN, LEN), bf16),
            V((HEADS, 8, LEN), f32),
            V((C, LEN), bf16),
            V((4, C, TOK), bf16),
            V((D, TOK), f32),
            V((D, TOK), f32),
            V((D, TOK), f32),
            V((2, 2, TOK, FF // 2), bf16),
            V((2, D, TOK), bf16),
            V((TOK, FF), bf16),
            V((2, TOK, FF // 2), bf16),
            V((2, D, TOK), bf16),
            V((2, 16, RB, 2 * FA), bf16),
            V((2, 16, RB, 2 * FB), bf16),
            V((2, 16, RB, 2 * HL), bf16),
            V((2, 16, RB, HL), bf16),
            V((16, RB, 2 * HL), bf16),
            V((16, RB, HL), bf16),
            V((2, 16, RB, HW), bf16),
            V((16, RB, HW), bf16),
            V((C, LEN), bf16),
            V((4, C, TOK), bf16),
            V((TOK, D), bf16),
            V((D, TOK), bf16),
            V((3 * C, LEN), bf16),
            V((3, C, LEN), bf16),
            V((2, C // 2, LEN), bf16),
            V((2, 2, C // 2, LEN), bf16),
            V((2, 4, RB, 2 * FA), bf16),
            V((2, 2, 4, RB, 2 * FA), bf16),
            V((2, 4, RB, 2 * FA), bf16),
            V((2, 3, RB, 2 * FA), bf16),
            V((2, RB, 2 * FA), bf16),
            V((2, 3, RB, FA // 2), bf16),
            V((2, 2, 8, RB, FB // 2), bf16),
            V((2, 2, 2, 8, RB, FB // 2), bf16),
            V((2, 16, RB, FB // 2), bf16),
            V((2, 3, 4, RB, FB // 2), bf16),
            V((2, 4, RB, FB // 2), bf16),
            V((2, 3, RB, FB // 2), bf16),
            V((3, 4, RB, 2 * HL), bf16),
            V((3, 4, RB, HL), bf16),
            V((4, RB, 2 * HL), bf16),
            V((4, RB, HL), bf16),
            V((3, RB, 2 * HL), bf16),
            V((3, RB, HL), bf16),
            V((3, 4, RB, HW), bf16),
            V((4, RB, HW), bf16),
            V((3, RB, HW), bf16),
            V((2, RB, HW), bf16),
            V((4, RB, C), bf16),
            V((3, RB, C), bf16),
            V((2, 2, RB, FA // 2), f32),
            V((2, 2, RB, FB // 2), f32),
            V((2, RB, HW), f32),
            V((8, TOK), f32),
            V((D, 128), f32),
            V((16, D), f32),
            V((16, D), f32),
            V((10, 8, D), f32),
            V((2, RB, D), bf16),
            V((3, RB, C), bf16),
            V((8, 1, C), f32),
            V((6, 128), f32),
            pltpu.SemaphoreType.DMA((18,)),
            pltpu.SemaphoreType.DMA((N_SEM,)),
            pltpu.SemaphoreType.DMA((N_SEM,)),
        ],
        compiler_params=pltpu.CompilerParams(
            collective_id=0, has_side_effects=True, vmem_limit_bytes=62 * 2**20
        ),
    )(
        inputs, teacher, lengths, query_weight, key_weight, value_weight, output_weight.T,
        up_weight, down_weight, *vectors,
    )
    vector = sds((1, C), f32)
    weight = sds((RB, C), f32)
    wide = sds((RB, D), f32)
    done = pl.pallas_call(
        finish,
        name="finish",
        out_shape=(
            sds((C, LEN), bf16), sds((1,), f32), sds((C, LEN), f32),
            weight, vector, weight, weight, vector, weight,
            vector, vector, vector, wide, sds((6, 128), f32), wide, vector, vector, vector,
        ),
        in_specs=[vm] * 7,
        out_specs=(vm, pl.BlockSpec(memory_space=pltpu.SMEM)) + (vm,) * 16,
    )(*got)
    shapes = [
        (C, LEN), (), (C, LEN), (RB, C), (C,), (RB, C), (RB, C), (C,), (RB, C), (C,), (C,), (C,),
        (RB, D), (D,), (RB, D), (C,), (C,), (C,),
    ]
    done = [o.reshape(shape) for o, shape in zip(done, shapes)]
    done[8] = done[8].T
    return tuple(done)


def solution(mesh):
    split = Mesh(
        mesh.devices.reshape(mesh.shape["dp"], 4, 4, mesh.shape["col"]), AXES
    )
    tokens = P("col", DP_ROW)
    weight = P(ROW, "col")
    vector = P("col")
    return jax.shard_map(
        local_step,
        mesh=split,
        in_specs=(
            tokens, tokens, P(DP_ROW), weight, vector, weight, weight, vector,
            P("col", ROW), vector, vector, vector, weight, vector, weight,
            vector, vector, vector,
        ),
        out_specs=(
            tokens, P(), tokens, weight, vector, weight, weight, vector,
            P("col", ROW), vector, vector, vector, weight, vector, weight,
            vector, vector, vector,
        ),
        check_vma=False,
    )
```
